32 devices in a mesh: dp: 8 (over z, x), tensor: 4 (over y, core).
Axes of the slice: x: 2, y: 2, z: 4, core: 2. Of those that a mesh axis runs over, the one named last changes fastest.
Arguments:
- decoder_in: bfloat16 [8, 128, 768], P('dp'), may hold values from -6 to 6
- encoder_out: bfloat16 [8, 6144, 768], P('dp', 'tensor'), may hold values from -6 to 6
- out_grad: bfloat16 [8, 128, 768], P('dp'), may hold values from -6 to 6
- group_ids: int32 [8], P('dp'), may hold values from 0 to 3
- target_mask: int32 [8, 128], P('dp'), may hold values 0 or 1
- bucket_ids: int32 [128, 128], replicated, may hold values from 0 to 31
- gain_self: float32 [768], replicated, may hold values from 0.5 to 1.5
- gain_cross: float32 [768], replicated, may hold values from 0.5 to 1.5
- gain_ffn: float32 [768], replicated, may hold values from 0.5 to 1.5
- query_self: bfloat16 [768, 768], P(None, 'tensor'), may hold values from -0.0546875 to 0.0546875
- key_self: bfloat16 [768, 768], P(None, 'tensor'), may hold values from -0.21875 to 0.21875
- value_self: bfloat16 [768, 768], P(None, 'tensor'), may hold values from -0.21875 to 0.21875
- output_self: bfloat16 [768, 768], P('tensor'), may hold values from -0.75 to 0.75
- query_cross: bfloat16 [768, 768], P(None, 'tensor'), may hold values from -0.0546875 to 0.0546875
- key_cross: bfloat16 [768, 768], P(None, 'tensor'), may hold values from -0.21875 to 0.21875
- value_cross: bfloat16 [768, 768], P(None, 'tensor'), may hold values from -0.21875 to 0.21875
- output_cross: bfloat16 [768, 768], P('tensor'), may hold values from -2 to 2
- gate_weight: bfloat16 [768, 2048], P(None, 'tensor'), may hold values from -0.21875 to 0.21875
- up_weight: bfloat16 [768, 2048], P(None, 'tensor'), may hold values from -0.21875 to 0.21875
- down_weight: bfloat16 [2048, 768], P('tensor'), may hold values from -0.1875 to 0.1875
- position_bias: float32 [4, 32, 12], P(None, None, 'tensor'), may hold values from -4 to 4
Outputs:
- block_out: bfloat16 [8, 128, 768], P('dp')
- decoder_grad: bfloat16 [8, 128, 768], P('dp')
- encoder_grad: bfloat16 [8, 6144, 768], P('dp', 'tensor')
- grad_gain_self: float32 [768], replicated
- grad_gain_cross: float32 [768], replicated
- grad_gain_ffn: float32 [768], replicated
- grad_query_self: float32 [768, 768], P(None, 'tensor')
- grad_key_self: float32 [768, 768], P(None, 'tensor')
- grad_value_self: float32 [768, 768], P(None, 'tensor')
- grad_output_self: float32 [768, 768], P('tensor')
- grad_query_cross: float32 [768, 768], P(None, 'tensor')
- grad_key_cross: float32 [768, 768], P(None, 'tensor')
- grad_value_cross: float32 [768, 768], P(None, 'tensor')
- grad_output_cross: float32 [768, 768], P('tensor')
- grad_gate: float32 [768, 2048], P(None, 'tensor')
- grad_up: float32 [768, 2048], P(None, 'tensor')
- grad_down: float32 [2048, 768], P('tensor')
- grad_position: float32 [4, 32, 12], P(None, None, 'tensor')
The draws below stay inside these ranges and needn't reach their ends.
All inputs are finite; a program needn't handle non-finite values. No bound on the sum of `target_mask` on one device may be relied on, other than what follows from the above.
Results may differ from the reference program's by a relative error of at most 0.039.
The reference program's roundings to bfloat16 on the way count: a program that leaves them out, or rounds other values in their place, can miss the bound.
Values may be sent and summed in bfloat16 or wider, within the bound.
A program may use at most 128 MiB of HBM per device.

```python
import jax
import jax.numpy as jnp
from jax import lax

D = 768
HEADS = 12
DH = 64
FF = 2048
BUCKETS = 32
GROUPS = 4
TGT = 128
ENC = 6144
QUERIES = 8


def place_ends(drawn, stream_key, least, top_value):
    extent = drawn.shape
    index_at = [jax.random.randint(jax.random.fold_in(stream_key, axis), (), 0, extent[axis]) for axis in range(len(extent))]
    drawn = drawn.at[tuple(index_at)].set(least)
    longest = extent.index(max(extent))
    index_at[longest] = (index_at[longest] + 1) % extent[longest]
    return drawn.at[tuple(index_at)].set(top_value)


def block_levels(own_key, dims, split, smallest, top_value):
    loudness, own = 1.0, jax.random.fold_in(own_key, 6)
    for position, shards_of in split:
        heights = jnp.exp(jax.random.uniform(jax.random.fold_in(own, position), (shards_of,), jnp.float32, smallest / len(split), top_value / len(split)))
        loudness = loudness * jnp.repeat(heights, dims[position] // shards_of).reshape([-1 if axis == position else 1 for axis in range(len(dims))])
    return loudness


def scatter_about(rng, extent, deviation, reach, cuts=(), kind=jnp.bfloat16):
    values = jax.random.normal(rng, extent, jnp.float32) * deviation
    if len(cuts) > 0:
        values = block_levels(rng, extent, cuts, -0.22, 0.18) * values
    return jnp.clip(values, min=-reach, max=reach).astype(kind)


def setup_inputs(seed: int = 0) -> dict:
    splits = jax.random.split(jax.random.key(seed), 22)
    return {
        "decoder_in": scatter_about(splits[0], (QUERIES, TGT, D), 1.0, 6.0, ((0, 8),)),
        "encoder_out": scatter_about(splits[1], (QUERIES, ENC, D), 1.0, 6.0, ((0, 8), (1, 4))),
        "out_grad": scatter_about(splits[2], (QUERIES, TGT, D), 1.0, 6.0, ((0, 8),)),
        "group_ids": place_ends(jax.random.randint(splits[3], (QUERIES,), 0, GROUPS), jax.random.fold_in(splits[3], 1), 0, GROUPS - 1).astype(jnp.int32),
        "target_mask": place_ends((jax.random.randint(splits[4], (QUERIES, TGT), 0, 4) < 3).astype(jnp.int32), jax.random.fold_in(splits[4], 1), 0, 1),
        "bucket_ids": place_ends(jax.random.randint(splits[5], (TGT, TGT), 0, BUCKETS), jax.random.fold_in(splits[5], 1), 0, BUCKETS - 1).astype(jnp.int32),
        "gain_self": jnp.clip(1.0 + 0.1 * jax.random.normal(splits[6], (D,), jnp.float32), 0.5, 1.5),
        "gain_cross": jnp.clip(1.0 + 0.1 * jax.random.normal(splits[7], (D,), jnp.float32), 0.5, 1.5),
        "gain_ffn": jnp.clip(1.0 + 0.1 * jax.random.normal(splits[8], (D,), jnp.float32), 0.5, 1.5),
        "query_self": scatter_about(splits[9], (D, HEADS * DH), (D * DH // 4) ** -0.5, 0.0546875, ((1, 4),)),
        "key_self": scatter_about(splits[10], (D, HEADS * DH), D ** -0.5, 0.21875, ((1, 4),)),
        "value_self": scatter_about(splits[11], (D, HEADS * DH), D ** -0.5, 0.21875, ((1, 4),)),
        "output_self": scatter_about(splits[12], (HEADS * DH, D), (max(D // 12, 4)) ** -0.5, 0.75, ((0, 4),)),
        "query_cross": scatter_about(splits[13], (D, HEADS * DH), (D * DH // 4) ** -0.5, 0.0546875, ((1, 4),)),
        "key_cross": scatter_about(splits[14], (D, HEADS * DH), D ** -0.5, 0.21875, ((1, 4),)),
        "value_cross": scatter_about(splits[15], (D, HEADS * DH), D ** -0.5, 0.21875, ((1, 4),)),
        "output_cross": scatter_about(splits[16], (HEADS * DH, D), (max(D // 96, 2)) ** -0.5, 2.0, ((0, 4),)),
        "gate_weight": scatter_about(splits[17], (D, FF), D ** -0.5, 0.21875, ((1, 4),)),
        "up_weight": scatter_about(splits[18], (D, FF), D ** -0.5, 0.21875, ((1, 4),)),
        "down_weight": scatter_about(splits[19], (FF, D), (FF // 2) ** -0.5, 0.1875, ((0, 4),)),
        "position_bias": scatter_about(splits[20], (GROUPS, BUCKETS, HEADS), 1.0, 4.0, ((2, 4),), jnp.float32),
    }


EPS = 1e-06
NEG = -1000000000.0
HIGH = lax.Precision.HIGHEST

@jax.custom_vjp
def low(v):
    return lax.optimization_barrier(v.astype(jnp.bfloat16)).astype(jnp.float32)

@jax.custom_vjp
def low_back(v):
    return v

def low_keep(v):
    return (low(v), None)

def low_pass(kept, grad):
    return (grad,)

def back_keep(v):
    return (v, None)

def back_low(kept, grad):
    return (low(grad),)
low.defvjp(low_keep, low_pass)
low_back.defvjp(back_keep, back_low)

def rms_norm(values, gain):
    return values * lax.rsqrt(lax.optimization_barrier(jnp.mean(values * values, axis=-1, keepdims=True)) + EPS) * gain

def project(left, right):
    return jnp.dot(left, right, precision=HIGH)

def split_heads(values):
    return values.reshape(values.shape[0], HEADS, DH)

def softmax_rows(scores):
    row_max = lax.optimization_barrier(jnp.max(scores, axis=-1, keepdims=True))
    exponent = jnp.exp(scores - row_max)
    return exponent / lax.optimization_barrier(jnp.sum(exponent, axis=-1, keepdims=True))

def attention(query_rows, key_rows, value_rows, bias):
    scores = jnp.einsum('ihd,jhd->hij', split_heads(query_rows), split_heads(key_rows), precision=HIGH) + bias
    scores = low_back(scores)
    probabilities = low(softmax_rows(scores))
    mixture = jnp.einsum('hij,jhd->ihd', probabilities, split_heads(value_rows), precision=HIGH)
    return low_back(low(mixture.reshape(mixture.shape[0], HEADS * DH)))

def block_forward(params, inputs, encoder_rows, group_hot, bucket_ids, allowed):
    gain_self, gain_cross, gain_ffn, query_self, key_self, value_self, output_self, query_cross, key_cross, value_cross, output_cross, gate_weight, up_weight, down_weight, position_bias = params
    bias_table = jnp.einsum('g,gbh->bh', group_hot, position_bias, precision=HIGH)
    spread = jnp.transpose(jnp.take(bias_table, bucket_ids, axis=0), (2, 0, 1))
    self_bias = jnp.where(allowed[None], spread, NEG)
    self_input = low(rms_norm(inputs, gain_self))
    query_rows = low_back(low(project(self_input, query_self)))
    key_rows = low_back(low(project(self_input, key_self)))
    value_rows = low_back(low(project(self_input, value_self)))
    after_self = inputs + low_back(project(attention(query_rows, key_rows, value_rows, self_bias), output_self))
    cross_input = low(rms_norm(after_self, gain_cross))
    cross_query = low_back(low(project(cross_input, query_cross)))
    cross_key = low_back(low(project(encoder_rows, key_cross)))
    cross_value = low_back(low(project(encoder_rows, value_cross)))
    after_cross = after_self + low_back(project(attention(cross_query, cross_key, cross_value, 0.0), output_cross))
    ffn_input = low(rms_norm(after_cross, gain_ffn))
    gate_value = low_back(project(ffn_input, gate_weight))
    up_value = low_back(project(ffn_input, up_weight))
    hidden = low_back(low(jax.nn.gelu(gate_value, approximate=True) * up_value))
    return after_cross + low_back(project(hidden, down_weight))

def reference(decoder_in, encoder_out, out_grad, group_ids, target_mask, bucket_ids, gain_self, gain_cross, gain_ffn, query_self, key_self, value_self, output_self, query_cross, key_cross, value_cross, output_cross, gate_weight, up_weight, down_weight, position_bias):
    weights = tuple((weight.astype(jnp.float32) for weight in (gain_self, gain_cross, gain_ffn, query_self, key_self, value_self, output_self, query_cross, key_cross, value_cross, output_cross, gate_weight, up_weight, down_weight, position_bias)))
    positions = jnp.arange(TGT)
    causal = positions[None, :] <= positions[:, None]
    diagonal = positions[None, :] == positions[:, None]

    def one_query(totals, query_item):
        tokens, encoded, cotangent, group_id, keep_mask = query_item
        allowed = causal & ((keep_mask[None, :] == 1) | diagonal)
        group_hot = (jnp.arange(GROUPS) == group_id).astype(jnp.float32)

        def forward(params, inputs, encoder_rows):
            return block_forward(params, inputs, encoder_rows, group_hot, bucket_ids, allowed)
        result, pullback = jax.vjp(forward, weights, tokens.astype(jnp.float32), encoded.astype(jnp.float32))
        weight_grads, token_grad, encoded_grad = pullback(cotangent.astype(jnp.float32))
        totals = jax.tree.map(jnp.add, totals, weight_grads)
        return (totals, (result.astype(jnp.bfloat16), token_grad.astype(jnp.bfloat16), encoded_grad.astype(jnp.bfloat16)))
    zero_grads = jax.tree.map(jnp.zeros_like, weights)
    totals, outputs = lax.scan(one_query, zero_grads, (decoder_in, encoder_out, out_grad, group_ids, target_mask))
    return (outputs[0], outputs[1], outputs[2], totals[0], totals[1], totals[2], totals[3], totals[4], totals[5], totals[6], totals[7], totals[8], totals[9], totals[10], totals[11], totals[12], totals[13], totals[14])
```

```python
import functools

import jax
import jax.numpy as jnp
from jax import lax
from jax.experimental import pallas as pl
from jax.experimental.pallas import tpu as pltpu
from jax.sharding import PartitionSpec as P

DH = 64
EPS = 1e-06
NEG = -1000000000.0
HIGH = lax.Precision.HIGHEST
MESH = pl.DeviceIdType.MESH
BF = jnp.bfloat16
F32 = jnp.float32
VMEM = pl.BlockSpec(memory_space=pltpu.VMEM)


def rms_norm(values, gain):
    return values * lax.rsqrt(jnp.mean(values * values, axis=-1, keepdims=True) + EPS) * gain


def gated(gate_value, up_value):
    return jax.nn.gelu(gate_value, approximate=True) * up_value


def mm(left, right, dims):
    return lax.dot_general(left, right, ((dims[0], dims[1]), ((), ())), preferred_element_type=F32)


def matmul(left, right):
    return mm(left, right, ((1,), (0,)))


def matmul_left_t(left, right):
    return mm(left, right, ((0,), (0,)))


def matmul_right_t(left, right):
    return mm(left, right, ((1,), (1,)))


def remote(src, dst, send, recv, device):
    return pltpu.make_async_remote_copy(
        src_ref=src, dst_ref=dst, send_sem=send, recv_sem=recv, device_id=device, device_id_type=MESH
    )


def greet(devices):
    barrier = pltpu.get_barrier_semaphore()
    for device in devices:
        pl.semaphore_signal(barrier, inc=1, device_id=device, device_id_type=MESH)
    pl.semaphore_wait(barrier, len(devices))


def tensor_place():
    dp, me = lax.axis_index("dp"), lax.axis_index("tensor")
    core = lax.rem(me, 2)
    return dp, me, core, me // 2


def rows_at(start, size, step):
    return pl.ds(pl.multiple_of(start, step), size)


def tensor_sum_kernel(count, *refs):
    xs, outs = refs[:count], refs[count : 2 * count]
    near, half, far, send, recv = refs[2 * count :]
    dp, me, core, side = tensor_place()
    mate, across = (dp, side * 2 + 1 - core), (dp, (1 - side) * 2 + core)
    greet([mate, across])
    size = xs[0].shape[0] // 2
    mine, other = rows_at(core * size, size, size), rows_at((1 - core) * size, size, size)
    first = [remote(xs[a].at[other], near.at[a], send.at[0, a], recv.at[0, a], mate) for a in range(count)]
    second = [remote(half.at[a], far.at[a], send.at[1, a], recv.at[1, a], across) for a in range(count)]
    third = [remote(outs[a].at[mine], outs[a].at[mine], send.at[2, a], recv.at[2, a], mate) for a in range(count)]
    for copy in first:
        copy.start()
    for a in range(count):
        first[a].wait()
        half[a] = (xs[a][mine].astype(F32) + near[a].astype(F32)).astype(BF)
        second[a].start()
    for a in range(count):
        second[a].wait()
        outs[a][mine] = (half[a].astype(F32) + far[a].astype(F32)).astype(BF)
        third[a].start()
    for copy in third:
        copy.wait()


def tensor_sum(values, collective_id):
    count = len(values)
    rows, width = values[0].shape
    return pl.pallas_call(
        functools.partial(tensor_sum_kernel, count),
        out_shape=[jax.ShapeDtypeStruct((rows, width), BF)] * count,
        in_specs=[VMEM] * count,
        out_specs=[VMEM] * count,
        scratch_shapes=[
            pltpu.VMEM((count, rows // 2, width), BF),
            pltpu.VMEM((count, rows // 2, width), BF),
            pltpu.VMEM((count, rows // 2, width), BF),
            pltpu.SemaphoreType.DMA((3, count)),
            pltpu.SemaphoreType.DMA((3, count)),
        ],
        compiler_params=pltpu.CompilerParams(collective_id=collective_id, has_side_effects=True),
    )(*values)


def tensor_gather_kernel(count, *refs):
    xs, outs = refs[:count], refs[count : 2 * count]
    send, recv, local = refs[2 * count :]
    dp, me, core, side = tensor_place()
    mate, across = (dp, side * 2 + 1 - core), (dp, (1 - side) * 2 + core)
    greet([mate, across])
    size = xs[0].shape[0]
    mine, theirs = rows_at(me * size, size, size), rows_at(((1 - side) * 2 + core) * size, size, size)
    keep = [pltpu.make_async_copy(xs[a], outs[a].at[mine], local.at[a]) for a in range(count)]
    to_across = [remote(xs[a], outs[a].at[mine], send.at[0, a], recv.at[0, a], across) for a in range(count)]
    to_mate = [remote(xs[a], outs[a].at[mine], send.at[1, a], recv.at[1, a], mate) for a in range(count)]
    onward = [remote(outs[a].at[theirs], outs[a].at[theirs], send.at[2, a], recv.at[2, a], mate) for a in range(count)]
    for a in range(count):
        to_across[a].start()
    for a in range(count):
        to_mate[a].start()
        keep[a].start()
    for a in range(count):
        to_across[a].wait()
        onward[a].start()
    for a in range(count):
        to_mate[a].wait()
        keep[a].wait()
        onward[a].wait()


def tensor_gather(values, collective_id):
    count = len(values)
    rows, width = values[0].shape
    return pl.pallas_call(
        functools.partial(tensor_gather_kernel, count),
        out_shape=[jax.ShapeDtypeStruct((4 * rows, width), BF)] * count,
        in_specs=[VMEM] * count,
        out_specs=[VMEM] * count,
        scratch_shapes=[
            pltpu.SemaphoreType.DMA((3, count)),
            pltpu.SemaphoreType.DMA((3, count)),
            pltpu.SemaphoreType.DMA((count,)),
        ],
        compiler_params=pltpu.CompilerParams(collective_id=collective_id, has_side_effects=True),
    )(*values)


def mixture_kernel(parts, mix_ref, stat_ref, out_ref, total_ref, mixes, stats, send, recv):
    dp, me, core, side = tensor_place()
    peers = [lax.rem(me + k, parts) for k in range(1, parts)]
    greet([(dp, peer) for peer in peers])
    size = mix_ref.shape[0] // parts
    heads = size // DH
    first, second = [], []
    for k, peer in enumerate(peers):
        block = rows_at(peer * size, size, size)
        first.append(remote(mix_ref.at[block], mixes.at[k], send.at[0, k], recv.at[0, k], (dp, peer)))
        first.append(remote(stat_ref.at[peer], stats.at[k], send.at[1, k], recv.at[1, k], (dp, peer)))
    mine = rows_at(me * size, size, size)
    for k, peer in enumerate(peers):
        second.append(remote(out_ref.at[mine], out_ref.at[mine], send.at[2, k], recv.at[2, k], (dp, peer)))
        second.append(remote(total_ref.at[me], total_ref.at[me], send.at[3, k], recv.at[3, k], (dp, peer)))
    for copy in first:
        copy.start()
    for copy in first:
        copy.wait()
    own = stat_ref[me]
    others = [stats[k] for k in range(parts - 1)]
    everyone = [own] + others
    top = everyone[0]
    for stat in everyone[1:]:
        top = jnp.maximum(top, stat)
    scales = [jnp.exp(stat - top) for stat in everyone]
    denominator = scales[0]
    for scale in scales[1:]:
        denominator = denominator + scale
    total_ref[me] = top + jnp.log(denominator)
    shares = [scale / denominator for scale in scales]
    own_mix = mix_ref[mine].astype(F32)
    for h in range(heads):
        rows = slice(h * DH, (h + 1) * DH)
        sum_up = own_mix[rows] * shares[0][h : h + 1]
        for k in range(parts - 1):
            sum_up = sum_up + mixes[k, rows].astype(F32) * shares[k + 1][h : h + 1]
        out_ref[rows_at(me * size + h * DH, DH, DH)] = sum_up.astype(BF)
    for copy in second:
        copy.start()
    for copy in second:
        copy.wait()


def combine_mixture(mix, stat, collective_id):
    parts = stat.shape[0]
    rows, width = mix.shape
    return pl.pallas_call(
        functools.partial(mixture_kernel, parts),
        out_shape=[jax.ShapeDtypeStruct(mix.shape, BF), jax.ShapeDtypeStruct(stat.shape, F32)],
        in_specs=[VMEM] * 2,
        out_specs=[VMEM] * 2,
        scratch_shapes=[
            pltpu.VMEM((parts - 1, rows // parts, width), BF),
            pltpu.VMEM((parts - 1,) + stat.shape[1:], F32),
            pltpu.SemaphoreType.DMA((4, parts - 1)),
            pltpu.SemaphoreType.DMA((4, parts - 1)),
        ],
        compiler_params=pltpu.CompilerParams(collective_id=collective_id, has_side_effects=True),
    )(mix, stat)


def scatter_kernel(count, parts, *refs):
    xs, outs = refs[:count], refs[count : 2 * count]
    bufs, send, recv = refs[2 * count :]
    dp, me, core, side = tensor_place()
    peers = [lax.rem(me + k, parts) for k in range(1, parts)]
    greet([(dp, peer) for peer in peers])
    size = xs[0].shape[0] // parts
    copies = []
    for a in range(count):
        for k, peer in enumerate(peers):
            block = rows_at(peer * size, size, size)
            copies.append(remote(xs[a].at[block], bufs.at[a, k], send.at[a, k], recv.at[a, k], (dp, peer)))
    for copy in copies:
        copy.start()
    for copy in copies:
        copy.wait()
    for a in range(count):
        sum_up = xs[a][rows_at(me * size, size, size)].astype(F32)
        for k in range(parts - 1):
            sum_up = sum_up + bufs[a, k].astype(F32)
        outs[a][...] = sum_up


def tensor_scatter(values, parts, collective_id):
    count = len(values)
    rows, width = values[0].shape
    return pl.pallas_call(
        functools.partial(scatter_kernel, count, parts),
        out_shape=[jax.ShapeDtypeStruct((rows // parts, width), F32)] * count,
        in_specs=[VMEM] * count,
        out_specs=[VMEM] * count,
        scratch_shapes=[
            pltpu.VMEM((count, parts - 1, rows // parts, width), BF),
            pltpu.SemaphoreType.DMA((count, parts - 1)),
            pltpu.SemaphoreType.DMA((count, parts - 1)),
        ],
        compiler_params=pltpu.CompilerParams(collective_id=collective_id, has_side_effects=True),
    )(*values)


def dp_sum_kernel(ranks, chunks, x_ref, out_ref, near, half, far, *sems):
    near_send, near_recv, far_send, far_recv, back_send, back_recv, end_send, end_recv = sems
    dp, tensor = lax.axis_index("dp"), lax.axis_index("tensor")
    x, z = lax.rem(dp, 2), dp // 2
    mate = (z * 2 + 1 - x, tensor)
    peers = [(lax.rem(z + k, ranks), k - 1) for k in range(1, ranks)]
    places = [(peer * 2 + x, tensor) for peer, k in peers]
    greet([mate] + places)
    rows = x_ref.shape[0]
    size = rows // 2 // chunks
    part = size // ranks
    def mine(c):
        return x * (rows // 2) + c * size
    def other(c):
        return (1 - x) * (rows // 2) + c * size
    first = [remote(x_ref.at[rows_at(other(c), size, size)], near.at[c], near_send.at[c], near_recv.at[c], mate) for c in range(chunks)]
    for copy in first:
        copy.start()
    second, third, fourth = [], [], []
    for c in range(chunks):
        second.append([remote(half.at[c, rows_at(peer * part, part, part)], far.at[c, k], far_send.at[c, k], far_recv.at[c, k], place) for (peer, k), place in zip(peers, places)])
        block = rows_at(mine(c) + z * part, part, part)
        third.append([remote(out_ref.at[block], out_ref.at[block], back_send.at[c, k], back_recv.at[c, k], place) for (peer, k), place in zip(peers, places)])
        block = rows_at(mine(c), size, size)
        fourth.append(remote(out_ref.at[block], out_ref.at[block], end_send.at[c], end_recv.at[c], mate))
    def one(c):
        first[c].wait()
        half[c] = (x_ref[rows_at(mine(c), size, size)].astype(F32) + near[c].astype(F32)).astype(BF)
        for copy in second[c]:
            copy.start()
    def two(c):
        for copy in second[c]:
            copy.wait()
        total = half[c, rows_at(z * part, part, part)].astype(F32)
        for k in range(ranks - 1):
            total = total + far[c, k].astype(F32)
        out_ref[rows_at(mine(c) + z * part, part, part)] = total.astype(BF)
        for copy in third[c]:
            copy.start()
    def three(c):
        for copy in third[c]:
            copy.wait()
        fourth[c].start()
    for c in range(chunks):
        one(c)
        if c >= 1:
            two(c - 1)
        if c >= 2:
            three(c - 2)
    two(chunks - 1)
    if chunks >= 2:
        three(chunks - 2)
    three(chunks - 1)
    for copy in fourth:
        copy.wait()


def dp_sum(packed, ranks, collective_id):
    rows, width = packed.shape
    z = ranks // 2
    chunks = 4 if z <= 4 else 1
    size = rows // 2 // chunks
    shapes = []
    for shape in ((chunks,), (chunks, z - 1), (chunks, z - 1), (chunks,)):
        shapes += [pltpu.SemaphoreType.DMA(shape)] * 2
    return pl.pallas_call(
        functools.partial(dp_sum_kernel, z, chunks),
        out_shape=jax.ShapeDtypeStruct(packed.shape, BF),
        in_specs=[VMEM],
        out_specs=VMEM,
        scratch_shapes=[
            pltpu.VMEM((chunks, size, width), BF),
            pltpu.VMEM((chunks, size, width), BF),
            pltpu.VMEM((chunks, z - 1, size // z, width), BF),
        ]
        + shapes,
        compiler_params=pltpu.CompilerParams(
            collective_id=collective_id, has_side_effects=True, vmem_limit_bytes=40 << 20
        ),
    )(packed)


def shards(
    tensor_size,
    dp_size,
    decoder_in,
    encoder_out,
    out_grad,
    group_ids,
    target_mask,
    bucket_ids,
    gain_self,
    gain_cross,
    gain_ffn,
    query_self,
    key_self,
    value_self,
    output_self,
    query_cross,
    key_cross,
    value_cross,
    output_cross,
    gate_weight,
    up_weight,
    down_weight,
    position_bias,
):
    query_count, target_len, width = decoder_in.shape
    assert query_count == 1
    heads = query_self.shape[1] // DH
    own = heads * DH
    all_heads = heads * tensor_size
    group_count, bucket_count, _ = position_bias.shape
    rows = encoder_out.shape[1]
    units = gate_weight.shape[1]

    key_t, value_t, query_t, output_all = tensor_gather(
        [key_cross.T, value_cross.T, query_cross.T, output_cross], 0
    )
    encoder = encoder_out[0]
    x = decoder_in[0].astype(F32)
    positions = jnp.arange(target_len)
    causal = positions[None, :] <= positions[:, None]
    diagonal = positions[None, :] == positions[:, None]
    allowed = causal & ((target_mask[0][None, :] == 1) | diagonal)
    group_hot = (group_ids[0] == jnp.arange(group_count)).astype(F32)
    bucket_hot = (jnp.arange(bucket_count)[:, None] == bucket_ids.reshape(-1)[None, :]).astype(F32)
    table = jnp.einsum("g,gkh->kh", group_hot, position_bias, precision=HIGH)
    spread = jnp.einsum("kp,kh->hp", bucket_hot, table, precision=HIGH)
    bias = jnp.where(allowed[None], spread.reshape(heads, target_len, target_len), NEG)
    self_in = rms_norm(x, gain_self).astype(BF)

    def to_heads(values, count):
        return values.reshape(values.shape[0], count, DH)

    q_self = to_heads(matmul(self_in, query_self).astype(BF), heads)
    k_self = to_heads(matmul(self_in, key_self).astype(BF), heads)
    v_self = to_heads(matmul(self_in, value_self).astype(BF), heads)
    scores = jnp.einsum("ihd,jhd->hij", q_self, k_self, preferred_element_type=F32) + bias
    p_self = jax.nn.softmax(scores, axis=-1)
    p_self_low = p_self.astype(BF)
    att_self = jnp.einsum("hij,jhd->ihd", p_self_low, v_self, preferred_element_type=F32).astype(BF)
    att_self = att_self.reshape(target_len, own)
    (self_out,) = tensor_sum([matmul(att_self, output_self).astype(BF)], 1)
    x2 = x + self_out.astype(F32)
    cross_in = rms_norm(x2, gain_cross).astype(BF)
    q_all = to_heads(matmul_right_t(cross_in, query_t).astype(BF), all_heads)
    k_all = to_heads(matmul_right_t(encoder, key_t).astype(BF), all_heads)
    v_all = to_heads(matmul_right_t(encoder, value_t).astype(BF), all_heads)
    cross_scores = jnp.einsum("ihd,jhd->hij", q_all, k_all, preferred_element_type=F32)
    top = jnp.max(cross_scores, axis=-1, keepdims=True)
    part_lse = top + jnp.log(jnp.sum(jnp.exp(cross_scores - top), axis=-1, keepdims=True))
    weights = jnp.exp(cross_scores - part_lse).astype(BF)
    part_mix = jnp.einsum("hij,jhd->hdi", weights, v_all, preferred_element_type=F32)
    stat = jnp.zeros((tensor_size, 8, target_len), F32)
    stat = stat.at[:, :heads].set(part_lse.reshape(tensor_size, heads, target_len))
    mix_t, total = combine_mixture(part_mix.astype(BF).reshape(all_heads * DH, target_len), stat, 2)
    lse = total[:, :heads].reshape(all_heads, target_len, 1)
    att_cross = mix_t.T
    x3 = x2 + matmul(att_cross, output_all)
    ffn_in = rms_norm(x3, gain_ffn).astype(BF)
    gate_value = matmul(ffn_in, gate_weight)
    up_value = matmul(ffn_in, up_weight)
    hidden = gated(gate_value, up_value).astype(BF)
    ffn_part = matmul(hidden, down_weight).astype(BF)
    out_low = out_grad[0]
    grad_down = matmul_left_t(hidden, out_low)
    d_hidden = matmul_right_t(out_low, down_weight).astype(BF)
    _, gated_pull = jax.vjp(gated, gate_value, up_value)
    d_gate, d_up = gated_pull(d_hidden.astype(F32))
    d_gate, d_up = d_gate.astype(BF), d_up.astype(BF)
    grad_gate = matmul_left_t(d_gate, ffn_in)
    grad_up = matmul_left_t(d_up, ffn_in)
    ffn_in_part = matmul_right_t(d_gate, gate_weight) + matmul_right_t(d_up, up_weight)
    ffn_in_grad, ffn_out = tensor_sum([ffn_in_part.astype(BF), ffn_part], 3)
    block_out = (x3 + ffn_out.astype(F32)).astype(BF)[None]
    _, ffn_pull = jax.vjp(rms_norm, x3, gain_ffn)
    ffn_norm_grad, grad_gain_ffn = ffn_pull(ffn_in_grad.astype(F32))
    g2 = out_low.astype(F32) + ffn_norm_grad
    g2_low = g2.astype(BF)
    me = lax.axis_index("tensor")
    att_own = lax.dynamic_slice(mix_t, (me * own, 0), (own, target_len))
    grad_output_cross = matmul(att_own, g2_low)
    d_att = to_heads(matmul_right_t(g2_low, output_all).astype(BF), all_heads)
    p_cross = jnp.exp(cross_scores - lse)
    dp_cross = jnp.einsum("ihd,jhd->hij", d_att, v_all, preferred_element_type=F32)
    delta = jnp.sum(d_att.astype(F32) * att_cross.reshape(target_len, all_heads, DH).astype(F32), axis=-1)
    ds_cross = (p_cross * (dp_cross - delta.T[:, :, None])).astype(BF)
    dk = jnp.einsum("hij,ihd->jhd", ds_cross, q_all, preferred_element_type=F32).astype(BF).reshape(rows, -1)
    dv = jnp.einsum("hij,ihd->jhd", p_cross.astype(BF), d_att, preferred_element_type=F32).astype(BF).reshape(rows, -1)
    dq_part = jnp.einsum("hij,jhd->ihd", ds_cross, k_all, preferred_element_type=F32).astype(BF)
    (dq,) = tensor_sum([dq_part.reshape(target_len, -1)], 4)
    encoder_grad = (matmul(dk, key_t) + matmul(dv, value_t)).astype(BF)[None]
    key_part = matmul_left_t(dk, encoder).astype(BF)
    value_part = matmul_left_t(dv, encoder).astype(BF)
    grad_key_cross, grad_value_cross = tensor_scatter([key_part, value_part], tensor_size, 5)
    dq_own = lax.dynamic_slice(dq, (0, me * own), (target_len, own))
    grad_query_cross = matmul_left_t(dq_own, cross_in)
    cross_in_grad = matmul(dq, query_t)
    _, cross_pull = jax.vjp(rms_norm, x2, gain_cross)
    cross_norm_grad, grad_gain_cross = cross_pull(cross_in_grad)
    g1 = g2 + cross_norm_grad
    g1_low = g1.astype(BF)
    grad_output_self = matmul_left_t(att_self, g1_low)
    d_att_self = to_heads(matmul_right_t(g1_low, output_self).astype(BF), heads)
    dp_self = jnp.einsum("ihd,jhd->hij", d_att_self, v_self, preferred_element_type=F32)
    inner = jnp.sum(p_self * dp_self, axis=-1, keepdims=True)
    ds_self = (p_self * (dp_self - inner)).astype(BF)
    sv = jnp.einsum("hij,ihd->jhd", p_self_low, d_att_self, preferred_element_type=F32).astype(BF).reshape(target_len, own)
    sk = jnp.einsum("hij,ihd->jhd", ds_self, q_self, preferred_element_type=F32).astype(BF).reshape(target_len, own)
    sq = jnp.einsum("hij,jhd->ihd", ds_self, k_self, preferred_element_type=F32).astype(BF).reshape(target_len, own)
    table_grad = jnp.einsum(
        "hp,kp->kh", ds_self.reshape(heads, -1), bucket_hot.astype(BF), preferred_element_type=F32
    )
    grad_position = group_hot[:, None, None] * table_grad[None]
    grad_query_self = matmul_left_t(sq, self_in)
    grad_key_self = matmul_left_t(sk, self_in)
    grad_value_self = matmul_left_t(sv, self_in)
    self_part = matmul_right_t(sq, query_self) + matmul_right_t(sk, key_self) + matmul_right_t(sv, value_self)
    (self_in_grad,) = tensor_sum([self_part.astype(BF)], 6)
    _, self_pull = jax.vjp(rms_norm, x, gain_self)
    self_norm_grad, grad_gain_self = self_pull(self_in_grad.astype(F32))
    decoder_grad = (g1 + self_norm_grad).astype(BF)[None]
    small = lax.psum((grad_gain_self, grad_gain_cross, grad_gain_ffn, grad_position), "dp")
    pieces = [
        grad_query_self, grad_key_self, grad_value_self, grad_output_self,
        grad_query_cross, grad_key_cross, grad_value_cross, grad_output_cross,
        grad_gate, grad_up, grad_down,
    ]
    packed = jnp.concatenate([piece.astype(BF) for piece in pieces], axis=0)
    packed = dp_sum(packed, dp_size, 7)
    outs, at = [], 0
    for k, piece in enumerate(pieces):
        value = packed[at : at + piece.shape[0]].astype(F32)
        at += piece.shape[0]
        outs.append(value if k in (3, 7, 10) else value.T)
    return (block_out, decoder_grad, encoder_grad) + tuple(small[:3]) + tuple(outs) + (small[3],)


def solution(mesh):
    rows = P("dp", None, None)
    encoder = P("dp", "tensor", None)
    columns, lines, whole = P(None, "tensor"), P("tensor", None), P()
    head_table = P(None, None, "tensor")
    weights = (columns, columns, columns, lines, columns, columns, columns, lines, columns, columns, lines, head_table)
    return jax.shard_map(
        functools.partial(shards, mesh.shape["tensor"], mesh.shape["dp"]),
        mesh=mesh,
        in_specs=(rows, encoder, rows, P("dp"), P("dp", None), whole, whole, whole, whole) + weights,
        out_specs=(rows, rows, encoder, whole, whole, whole) + weights,
        check_vma=False,
    )
```

```python
import functools
from types import SimpleNamespace

import jax
import jax.numpy as jnp
from jax import lax
from jax.experimental import pallas as pl
from jax.experimental.pallas import tpu as pltpu
from jax.sharding import PartitionSpec as P

DH = 64
EPS = 1e-06
NEG = -1000000000.0
TILE = 256
MESH = pl.DeviceIdType.MESH
BF = jnp.bfloat16
F32 = jnp.float32
VMEM = pl.BlockSpec(memory_space=pltpu.VMEM)
SMEM = pl.BlockSpec(memory_space=pltpu.SMEM)
ANY = pl.BlockSpec(memory_space=pl.ANY)
GELU_SCALE = 0.7978845608028654
GELU_CUBIC = 0.044715


IN_X = (True, True, True, False, False, True, False, True, False, True, True, True, True, False)
SCHEDULE = (
    ((0, 0),),
    ((3, 0),),
    (),
    ((1, 0),),
    ((0, 1),),
    ((2, 0),),
    ((1, 1), (3, 1),),
    ((5, 0),),
    (),
    ((0, 2), (2, 1),),
    ((3, 2),),
    ((1, 2), (5, 1),),
    ((4, 0), (0, 3),),
    ((2, 2), (3, 3),),
    ((1, 3),),
    ((0, 4), (2, 3),),
    ((4, 1), (1, 4), (6, 0),),
    ((3, 4), (7, 0), (0, 5),),
    ((5, 2),),
    (),
    ((4, 2), (1, 5), (9, 0), (8, 0),),
    ((2, 4),),
    ((7, 1), (6, 1), (5, 3),),
    ((3, 5),),
    ((4, 3), (10, 0),),
    ((6, 2), (8, 1), (5, 4),),
    ((2, 5),),
    ((7, 2), (4, 4), (13, 0),),
    ((9, 1),),
    ((9, 2), (11, 0), (8, 2), (6, 3),),
    ((5, 5), (7, 3), (12, 0), (4, 5),),
    ((10, 1), (13, 1), (9, 3),),
    ((8, 3), (10, 2), (6, 4), (7, 4), (13, 2), (9, 4), (7, 5), (8, 4), (6, 5), (11, 1), (11, 2), (9, 5), (10, 3), (12, 1), (12, 2), (8, 5), (11, 3), (10, 4), (12, 3), (13, 3), (11, 4), (10, 5), (12, 4), (13, 4), (11, 5), (12, 5), (13, 5),),
)


def nn(left, right):
    return lax.dot_general(left, right, (((1,), (0,)), ((), ())), preferred_element_type=F32)


def nt(left, right):
    return lax.dot_general(left, right, (((1,), (1,)), ((), ())), preferred_element_type=F32)


def tn(left, right):
    return lax.dot_general(left, right, (((0,), (0,)), ((), ())), preferred_element_type=F32)


def span(start, size, step=None):
    return pl.ds(pl.multiple_of(start, step or size), size)


class Sems:
    def __init__(self, ref):
        self.ref, self.used = ref, 0

    def take(self):
        self.used += 1
        assert self.used <= self.ref.shape[0]
        return self.ref.at[self.used - 1]


class Wire:
    def __init__(self, sems, src, dst, device):
        self.copy = pltpu.make_async_remote_copy(
            src_ref=src, dst_ref=dst, send_sem=sems.take(), recv_sem=sems.take(), device_id=device, device_id_type=MESH
        )

    def start(self):
        self.copy.start()

    def sent(self):
        self.copy.wait_send()

    def came(self):
        self.copy.wait_recv()

    def wait(self):
        self.copy.wait()


class TensorSum:
    def __init__(self, sems, place, src, near, half, far, out):
        self.src, self.near, self.half, self.far, self.out = src, near, half, far, out
        size = src.shape[0] // 2
        self.mine = span(place.core * size, size)
        other = span((1 - place.core) * size, size)
        self.first = Wire(sems, src.at[other], near, place.mate)
        self.second = Wire(sems, half, far, place.across)
        self.third = Wire(sems, out.at[self.mine], out.at[self.mine], place.mate)

    def one(self):
        self.first.start()

    def two(self):
        self.first.wait()
        self.half[...] = (self.src[self.mine].astype(F32) + self.near[...].astype(F32)).astype(BF)
        self.second.start()

    def three(self):
        self.second.wait()
        self.out[self.mine] = (self.half[...].astype(F32) + self.far[...].astype(F32)).astype(BF)
        self.third.start()

    def four(self):
        self.third.wait()


class TensorMix:
    def __init__(self, sems, place, mix, stat, bufs, out, total):
        self.place, self.mix, self.stat, self.out, self.total = place, mix, stat, out, total
        near, half, far, near_stat, half_stat, far_stat = bufs
        self.bufs = bufs
        size, core = mix.shape[0] // 2, place.core
        self.size = size
        self.mine, other = span(core * size, size), span((1 - core) * size, size)
        self.mine_stat, other_stat = span(core * 8, 8), span((1 - core) * 8, 8)
        self.first = [
            Wire(sems, mix.at[other], near, place.mate),
            Wire(sems, stat.at[other_stat], near_stat, place.mate),
        ]
        self.second = [Wire(sems, half, far, place.across), Wire(sems, half_stat, far_stat, place.across)]
        self.third = [
            Wire(sems, out.at[self.mine], out.at[self.mine], place.mate),
            Wire(sems, total.at[self.mine_stat], total.at[self.mine_stat], place.mate),
        ]

    def join(self, ours, theirs, ours_stat, theirs_stat, flip, store):
        low_stat = jnp.where(flip, theirs_stat, ours_stat)
        high_stat = jnp.where(flip, ours_stat, theirs_stat)
        top = jnp.maximum(low_stat, high_stat)
        total = top + jnp.log(jnp.exp(low_stat - top) + jnp.exp(high_stat - top))
        low_share, high_share = jnp.exp(low_stat - total), jnp.exp(high_stat - total)
        for h in range(self.size // DH):
            rows = slice(h * DH, (h + 1) * DH)
            a, b = ours(rows), theirs(rows)
            low, high = jnp.where(flip, b, a), jnp.where(flip, a, b)
            store(rows, (low * low_share[h : h + 1] + high * high_share[h : h + 1]).astype(BF))
        return total

    def one(self):
        for wire in self.first:
            wire.start()

    def two(self):
        near, half, far, near_stat, half_stat, far_stat = self.bufs
        core, size = self.place.core, self.size
        for wire in self.first:
            wire.wait()

        def ours(rows):
            return self.mix[span(core * size + rows.start, DH)].astype(F32)

        def store(rows, value):
            half[rows] = value

        half_stat[...] = self.join(
            ours, lambda rows: near[rows].astype(F32), self.stat[self.mine_stat], near_stat[...], core == 1, store
        )
        for wire in self.second:
            wire.start()

    def three(self):
        near, half, far, near_stat, half_stat, far_stat = self.bufs
        core, size = self.place.core, self.size
        for wire in self.second:
            wire.wait()

        def store(rows, value):
            self.out[span(core * size + rows.start, DH)] = value

        self.total[self.mine_stat] = self.join(
            lambda rows: half[rows].astype(F32),
            lambda rows: far[rows].astype(F32),
            half_stat[...],
            far_stat[...],
            self.place.side == 1,
            store,
        )
        for wire in self.third:
            wire.start()

    def four(self):
        for wire in self.third:
            wire.wait()


class WeightGather:
    def __init__(self, sems, place, own, whole, local):
        rows = own.shape[0]
        half = rows // 2
        me, core, side, x = place.me, place.core, place.side, place.x
        there = (1 - side) * 2 + core
        self.own, self.whole = own, whole
        mine = span(me * rows, rows)
        direct = span(there * rows + x * half, half)
        relayed = span(there * rows + (1 - x) * half, half)
        self.across = Wire(sems, own.at[span(x * half, half)], whole.at[span(me * rows + x * half, half)], place.across)
        self.mate = Wire(sems, own, whole.at[mine], place.mate)
        self.side = Wire(sems, whole.at[direct], whole.at[direct], place.beside)
        self.direct = Wire(sems, whole.at[direct], whole.at[direct], place.mate)
        self.relayed = Wire(sems, whole.at[relayed], whole.at[relayed], place.mate)
        self.keep = pltpu.make_async_copy(own, whole.at[mine], local)

    def start(self):
        self.across.start()
        self.mate.start()
        self.keep.start()

    def one(self):
        self.across.came()
        self.side.start()
        self.direct.start()

    def two(self):
        self.side.came()
        self.relayed.start()

    def three(self):
        self.mate.came()
        self.keep.wait()
        self.direct.came()
        self.relayed.came()

    def end(self):
        for wire in (self.across, self.mate, self.side, self.direct, self.relayed):
            wire.sent()


class ChunkX:
    def __init__(self, sems, place, g, out, bufs):
        self.place = place
        near, inn, mid, tot, fin = self.bufs = bufs
        half = g.shape[0] // 2
        x = place.x
        self.g, self.mine = g, span(x * half, half)
        other = span((1 - x) * half, half)
        self.rs = Wire(sems, g.at[other], near, place.beside)
        self.out = Wire(sems, g.at[self.mine], inn, place.pair)
        self.middle = Wire(sems, g.at[self.mine], mid, place.middle)
        self.back = Wire(sems, tot, tot, place.pair)
        self.ag = Wire(sems, tot, fin, place.beside)
        self.save = [
            pltpu.make_async_copy(tot, out.at[self.mine], sems.take()),
            pltpu.make_async_copy(fin, out.at[other], sems.take()),
        ]

    def s0(self):
        self.rs.start()

    def s1(self):
        self.rs.wait()
        self.g[self.mine] = self.g[self.mine] + self.bufs[0][...]

        @pl.when(self.place.end)
        def _():
            self.out.start()

    def s2(self):
        @pl.when(self.place.inner)
        def _():
            self.out.came()
            self.g[self.mine] = self.g[self.mine] + self.bufs[1][...]
            self.middle.start()

    def s3(self):
        @pl.when(self.place.inner)
        def _():
            self.middle.wait()
            self.bufs[3][...] = self.g[self.mine] + self.bufs[2][...]
            self.back.start()
            self.ag.start()
            self.save[0].start()

    def s4(self):
        @pl.when(self.place.end)
        def _():
            self.back.came()
            self.ag.start()
            self.save[0].start()

    def s5(self):
        self.ag.came()
        self.save[1].start()

    def finish(self):
        @pl.when(self.place.end)
        def _():
            self.out.sent()

        @pl.when(self.place.inner)
        def _():
            self.back.sent()

        self.ag.sent()
        for copy in self.save:
            copy.wait()


class ChunkZ:
    def __init__(self, sems, place, g, out, bufs):
        self.place = place
        inn, mid, r, xr, tot = self.bufs = bufs
        half = g.shape[0] // 2
        at = place.high
        self.g, self.mine = g, span(at * half, half)
        self.other = span((1 - at) * half, half)
        self.out = Wire(sems, g, inn, place.pair)
        self.rs = Wire(sems, g.at[self.other], mid, place.middle)
        self.x = Wire(sems, r, xr, place.beside)
        self.ag = Wire(sems, tot.at[self.mine], tot.at[self.mine], place.middle)
        self.back = [
            Wire(sems, tot.at[self.mine], tot.at[self.mine], place.pair),
            Wire(sems, tot.at[self.other], tot.at[self.other], place.pair),
        ]
        self.save = pltpu.make_async_copy(tot, out, sems.take())

    def s0(self):
        @pl.when(self.place.end)
        def _():
            self.out.start()

    def s1(self):
        @pl.when(self.place.inner)
        def _():
            self.out.came()
            self.g[...] = self.g[...] + self.bufs[0][...]
            self.rs.start()

    def s2(self):
        @pl.when(self.place.inner)
        def _():
            self.rs.wait()
            self.bufs[2][...] = self.g[self.mine] + self.bufs[1][...]
            self.x.start()

    def s3(self):
        @pl.when(self.place.inner)
        def _():
            self.x.wait()
            self.bufs[4][self.mine] = self.bufs[2][...] + self.bufs[3][...]
            self.ag.start()
            self.back[0].start()

    def s4(self):
        @pl.when(self.place.inner)
        def _():
            self.ag.came()
            self.back[1].start()
            self.save.start()

    def s5(self):
        @pl.when(self.place.end)
        def _():
            for wire in self.back:
                wire.came()
            self.save.start()

    def finish(self):
        @pl.when(self.place.end)
        def _():
            self.out.sent()

        @pl.when(self.place.inner)
        def _():
            self.ag.sent()
            for wire in self.back:
                wire.sent()

        self.save.wait()


class SmallSum:
    def __init__(self, sems, place, bufs):
        self.place = place
        own, near, sum1, inn, sum2, mid, tot = self.bufs = bufs
        self.x = Wire(sems, own, near, place.beside)
        self.out = Wire(sems, sum1, inn, place.pair)
        self.middle = Wire(sems, sum2, mid, place.middle)
        self.back = Wire(sems, tot, tot, place.pair)

    def s0(self):
        self.x.start()

    def s1(self):
        own, near, sum1, inn, sum2, mid, tot = self.bufs
        self.x.wait()
        sum1[...] = own[...] + near[...]

        @pl.when(self.place.end)
        def _():
            self.out.start()

    def s2(self):
        own, near, sum1, inn, sum2, mid, tot = self.bufs

        @pl.when(self.place.inner)
        def _():
            self.out.came()
            sum2[...] = sum1[...] + inn[...]
            self.middle.start()

    def s3(self):
        own, near, sum1, inn, sum2, mid, tot = self.bufs

        @pl.when(self.place.inner)
        def _():
            self.middle.wait()
            tot[...] = sum2[...] + mid[...]
            self.back.start()
            self.back.sent()

    def s4(self):
        @pl.when(self.place.end)
        def _():
            self.out.sent()
            self.back.came()


def rms_scale(values):
    return lax.rsqrt(jnp.mean(values * values, axis=-1, keepdims=True) + EPS)


def norm_back(values, gain, dy):
    scale = rms_scale(values)
    normal = values * scale
    gain_grad = jnp.sum(dy * normal, axis=0, keepdims=True)
    pulled = dy * gain
    mean = jnp.mean(pulled * normal, axis=-1, keepdims=True)
    return scale * (pulled - normal * mean), gain_grad


def fold(values, op):
    rows, width = values.shape
    return op(values.reshape(rows // 8, 8, width), axis=0)


def chunk_plan(own, width, units):
    plan = [(0, k * (units // 2), units // 2) for k in range(2)]
    plan += [(a, k * (width // 2), width // 2) for a in (1, 2) for k in range(2)]
    plan += [(3, k * own, own) for k in range(8)]
    return [(in_x, *block) for in_x, block in zip(IN_X, plan)]


def block_kernel(cfg, *refs):
    groups, at = [], 0
    for tree in cfg.trees:
        groups.append(SimpleNamespace(**jax.tree.unflatten(tree, refs[at : at + tree.num_leaves])))
        at += tree.num_leaves
    ins, outs, scr = groups
    gain_self, gain_cross, gain_ffn = (gain[...].reshape(1, cfg.width) for gain in ins.gains)
    heads, all_heads, width, tokens, rows = cfg.heads, cfg.all_heads, cfg.width, cfg.tokens, cfg.rows
    own, pairs, tiles = heads * DH, all_heads // 2, rows // TILE
    summing = cfg.summing
    sems = Sems(scr.sems)
    dp, me = lax.axis_index("dp"), lax.axis_index("tensor")
    core, side = lax.rem(me, 2), me // 2
    x, z = lax.rem(dp, 2), dp // 2
    place = SimpleNamespace(
        me=me,
        core=core,
        side=side,
        x=x,
        mate=(dp, side * 2 + 1 - core),
        across=(dp, (1 - side) * 2 + core),
        beside=(dp + 1 - 2 * x, me),
    )
    barrier = pltpu.get_barrier_semaphore()
    for friend in (place.mate, place.across, place.beside):
        pl.semaphore_signal(barrier, inc=1, device_id=friend, device_id_type=MESH)
    if summing:
        inner = jnp.logical_or(z == 1, z == 2)
        place.inner, place.end = inner, jnp.logical_not(inner)
        place.high = z // 2
        place.pair = ((z + 1 - 2 * lax.rem(z, 2)) * 2 + x, me)
        place.middle = ((3 - z) * 2 + x, me)
        pl.semaphore_signal(barrier, inc=1, device_id=place.pair, device_id_type=MESH)

        @pl.when(inner)
        def _():
            pl.semaphore_signal(barrier, inc=1, device_id=place.middle, device_id_type=MESH)

    def fetch(src, dst):
        copy = pltpu.make_async_copy(src, dst, sems.take())
        copy.start()
        return copy

    enc, down, gate_w, up_w = scr.enc, scr.down, scr.gate_w, scr.up_w
    load_enc = fetch(ins.encoder, enc)
    load_ffn = [fetch(ins.down_w, down), fetch(ins.gate_w, gate_w), fetch(ins.up_w, up_w)]

    xv = ins.x[...].astype(F32)
    self_in = scr.self_in
    self_in[...] = (xv * rms_scale(xv) * gain_self).astype(BF)
    qkv = scr.qkv
    self_weights = (ins.wq_self, ins.wk_self, ins.wv_self)
    for k, weight in enumerate(self_weights):
        qkv[k * own : (k + 1) * own] = nt(weight[...], self_in[...]).astype(BF)
    if summing:
        pl.semaphore_wait(barrier, 4 + inner.astype(jnp.int32))
    else:
        pl.semaphore_wait(barrier, 3)
    wk, wq, wv, wo = scr.wk, scr.wq, scr.wv, scr.wo
    get_k, get_q, get_v, get_o = gathers = [
        WeightGather(sems, place, part, whole, sems.take())
        for part, whole in ((ins.wk_cross, wk), (ins.wq_cross, wq), (ins.wv_cross, wv), (ins.wo_cross, wo))
    ]
    get_k.start()
    get_q.start()
    scr.bucket[...] = ins.bucket[...].T
    bucket = scr.bucket
    keep = jnp.broadcast_to(ins.mask[...].astype(F32), (tokens, tokens)).T
    j_at = lax.broadcasted_iota(jnp.int32, (tokens, tokens), 0)
    i_at = lax.broadcasted_iota(jnp.int32, (tokens, tokens), 1)
    allowed = jnp.logical_or(jnp.logical_and(j_at <= i_at, keep == 1.0), j_at == i_at)
    group = ins.group[0]
    buckets = cfg.buckets
    for h in range(heads):
        scr.p_self[h] = jnp.full((tokens, tokens), NEG, F32)

    def spread(b, _):
        hit = jnp.logical_and(bucket[...] == b, allowed)
        for h in range(heads):
            scr.p_self[h] = jnp.where(hit, ins.table[h, group, b], scr.p_self[h])
        return 0

    lax.fori_loop(0, buckets, spread, 0)
    get_v.start()
    att_self = scr.att_self

    def attend(h):
        q = qkv[h * DH : (h + 1) * DH]
        k = qkv[own + h * DH : own + (h + 1) * DH]
        v = qkv[2 * own + h * DH : 2 * own + (h + 1) * DH]
        s = tn(k, q) + scr.p_self[h]
        e = jnp.exp(s - jnp.max(s, axis=0, keepdims=True))
        p = e / jnp.sum(e, axis=0, keepdims=True)
        scr.p_self[h] = p
        att_self[h * DH : (h + 1) * DH] = nn(v, p.astype(BF)).astype(BF)

    attend(0)
    get_o.start()
    for h in range(1, heads):
        attend(h)
    get_k.one()

    def tensor_sum(bufs):
        return TensorSum(sems, place, *bufs)

    s1 = tensor_sum(scr.s1)
    s1.src[...] = tn(att_self[...], ins.wo_self[...]).astype(BF)
    s1.one()
    get_q.one()
    get_k.two()
    s1.two()
    get_v.one()
    get_q.two()
    get_o.one()
    get_v.two()
    load_enc.wait()
    get_k.three()
    kc, vc, kt, vt, e_ref = scr.kc, scr.vc, scr.kt, scr.vt, scr.e

    def project(dst, weight):
        def body(r, _):
            at = span(r * TILE, TILE)
            dst[at] = nt(enc[at], weight[...]).astype(BF)
            return 0

        lax.fori_loop(0, tiles, body, 0)

    def project_t(dst, weight):
        def body(r, _):
            at = span(r * TILE, TILE)
            dst[:, at] = nt(weight[...], enc[at]).astype(BF)
            return 0

        lax.fori_loop(0, tiles, body, 0)

    project(kc, wk)
    s1.three()
    get_o.two()
    get_v.three()
    project_t(vt, wv)
    s1.four()
    x2 = scr.x2
    x2[...] = xv + s1.out[...].astype(F32)
    cross_in = scr.cross_in
    cross_in[...] = (x2[...] * rms_scale(x2[...]) * gain_cross).astype(BF)
    get_q.three()
    bq, bw = scr.bq, scr.bw
    bq[...] = jnp.zeros(bq.shape, BF)
    bw[...] = jnp.zeros(bw.shape, BF)
    q_t = nt(wq[...], cross_in[...]).astype(BF)
    for h in range(all_heads):
        at = slice(h * DH, (h + 1) * DH)
        bq[at, (h % 2) * tokens : (h % 2 + 1) * tokens] = q_t[at]
    s_ref, mix, stat, top_ref = scr.s, scr.mix, scr.stat, scr.top
    stat[...] = jnp.zeros(stat.shape, F32)
    top_ref[...] = jnp.zeros(top_ref.shape, F32)
    per_half = pairs // 2

    def stat_row(p):
        return (p // per_half) * 8 + 2 * (p - (p // per_half) * per_half)

    def forward_pair(p, _):
        head_at = span(p * 2 * DH, 2 * DH)
        score_at = span(p * 2 * tokens, 2 * tokens)
        weights = bq[head_at]
        top = None
        for r in range(tiles):
            at = slice(r * TILE, (r + 1) * TILE)
            s = nn(kc[at, head_at], weights)
            s_ref[at] = s
            part = fold(s, jnp.max)
            top = part if top is None else jnp.maximum(top, part)
        top = jnp.max(top, axis=0, keepdims=True)
        total, acc = None, None
        for r in range(tiles):
            at = slice(r * TILE, (r + 1) * TILE)
            e = jnp.exp(s_ref[at] - top)
            part = fold(e, jnp.sum)
            total = part if total is None else total + part
            low = e.astype(BF)
            e_ref[at, score_at] = low
            part = nn(vt[head_at, at], low)
            acc = part if acc is None else acc + part
        total = jnp.sum(total, axis=0, keepdims=True)
        inverse = 1.0 / total
        lse = top + jnp.log(total)
        row = stat_row(p)
        for k in range(2):
            lanes = slice(k * tokens, (k + 1) * tokens)
            value = acc[k * DH : (k + 1) * DH, lanes] * inverse[:, lanes]
            mix[span(p * 2 * DH + k * DH, DH)] = value.astype(BF)
            stat[pl.ds(row + k, 1)] = lse[:, lanes]
            top_ref[pl.ds(row + k, 1)] = top[:, lanes]
        return 0

    lax.fori_loop(0, pairs, forward_pair, 0)
    att, lse = scr.att, scr.lse
    s2 = TensorMix(sems, place, mix, stat, scr.mix_bufs, att, lse)
    s2.one()
    for load in load_ffn:
        load.wait()
    og = ins.out_grad
    scr.d_hidden[...] = nt(og[...], down[...]).astype(BF).astype(F32)
    s2.two()
    project(vc, wv)
    s2.three()
    get_o.three()
    s2.four()
    x3 = scr.x3
    x3[...] = x2[...] + tn(att[...], wo[...])
    ffn_in = scr.ffn_in
    ffn_in[...] = (x3[...] * rms_scale(x3[...]) * gain_ffn).astype(BF)
    gate = nn(ffn_in[...], gate_w[...])
    up = nn(ffn_in[...], up_w[...])
    squared = gate * gate
    curve = jnp.tanh(GELU_SCALE * (gate + GELU_CUBIC * (squared * gate)))
    gelu = 0.5 * gate * (1.0 + curve)
    slope = 0.5 * (1.0 + curve) + 0.5 * gate * (1.0 - curve * curve) * (
        GELU_SCALE * (1.0 + 3.0 * GELU_CUBIC * squared)
    )
    d_hidden = scr.d_hidden[...]
    scr.hidden[...] = (gelu * up).astype(BF)
    scr.d_gate[...] = (d_hidden * up * slope).astype(BF)
    scr.d_up[...] = (d_hidden * gelu).astype(BF)

    chunks = []
    if summing:
        for (in_x, source, start, size), bufs in zip(cfg.chunks, scr.chunks):
            rows_at = pl.ds(start, size)
            maker = ChunkX if in_x else ChunkZ
            chunks.append(maker(sems, place, scr.grads[source].at[rows_at], outs.grads[source].at[rows_at], bufs))
    schedule = iter(cfg.schedule)

    def poll():
        if summing:
            for n, k in next(schedule):
                chunk = chunks[n]
                (chunk.s0, chunk.s1, chunk.s2, chunk.s3, chunk.s4, chunk.s5)[k]()

    g_down, g_gate, g_up, g_small = scr.grads
    g_down[...] = tn(scr.hidden[...], og[...]).astype(BF)
    poll()
    g_gate[...] = tn(ffn_in[...], scr.d_gate[...]).astype(BF)
    poll()
    g_up[...] = tn(ffn_in[...], scr.d_up[...]).astype(BF)
    poll()
    s3, so = tensor_sum(scr.s3), tensor_sum(scr.so)
    s3.src[...] = (nt(scr.d_gate[...], gate_w[...]) + nt(scr.d_up[...], up_w[...])).astype(BF)
    s3.one()
    so.src[...] = nn(scr.hidden[...], down[...]).astype(BF)
    s3.two()
    poll()
    project_t(kt, wk)
    poll()
    s3.three()
    so.one()
    s3.four()
    so.two()
    poll()
    g2, g2_low = scr.g2, scr.g2_low
    dv, gain_grad = norm_back(x3[...], gain_ffn, s3.out[...].astype(F32))
    g2[...] = og[...].astype(F32) + dv
    g2_low[...] = g2[...].astype(BF)
    small = scr.small[0]
    small[...] = jnp.zeros(small.shape, F32)
    small[2:3, :width] = gain_grad
    g_small[0:own] = nn(att[span(me * own, own)], g2_low[...]).astype(BF)
    poll()
    d_att = nt(wo[...], g2_low[...])
    delta_ref = scr.delta
    for h in range(all_heads):
        at = slice(h * DH, (h + 1) * DH)
        p, k = divmod(h, 2)
        row = (p // per_half) * 8 + 2 * (p % per_half) + k
        share = jnp.exp(top_ref[row : row + 1] - lse[row : row + 1])
        low = (d_att[at] * share).astype(BF)
        bw[at, k * tokens : (k + 1) * tokens] = low
        delta_ref[p : p + 1, k * tokens : (k + 1) * tokens] = jnp.sum(
            low.astype(F32) * att[at].astype(F32), axis=0, keepdims=True
        )
    so.three()
    s4 = tensor_sum(scr.s4)

    def backward_pair(p, _):
        head_at = span(p * 2 * DH, 2 * DH)
        score_at = span(p * 2 * tokens, 2 * tokens)
        wq_block, wa_block = bq[head_at], bw[head_at]
        delta = delta_ref[pl.ds(p, 1)]
        acc = None
        for r in range(tiles):
            at = slice(r * TILE, (r + 1) * TILE)
            e = e_ref[at, score_at]
            grad = nn(vc[at, head_at], wa_block)
            ds = (e.astype(F32) * (grad - delta)).astype(BF)
            part = nn(kt[head_at, at], ds)
            acc = part if acc is None else acc + part
            kc[at, head_at] = nt(ds, wq_block).astype(BF)
            vc[at, head_at] = nt(e, wa_block).astype(BF)
            kt[head_at, at] = nt(wq_block, ds).astype(BF)
            vt[head_at, at] = nt(wa_block, e).astype(BF)
        for k in range(2):
            value = acc[k * DH : (k + 1) * DH, k * tokens : (k + 1) * tokens]
            s4.src[span(p * 2 * DH + k * DH, DH)] = value.astype(BF)
        return 0

    for p in range(pairs):
        poll()
        lax.fori_loop(p, p + 1, backward_pair, 0)
    s4.one()
    so.four()
    outs.block_out[...] = (x3[...] + so.out[...].astype(F32)).astype(BF)
    poll()

    parts, kv_near, kv_half, kv_far = scr.parts, scr.kv_near, scr.kv_half, scr.kv_far
    to_mate, to_across = [], []
    for a in range(2):
        to_mate.append(
            Wire(sems, parts[a].at[span((1 - core) * 2 * own, 2 * own)], kv_near.at[a], place.mate)
        )
        to_across.append(Wire(sems, kv_half.at[a, span((1 - side) * own, own)], kv_far.at[a], place.across))

    def weight_part(a):
        source = (kt, vt)[a]

        def body(t, _):
            slot = lax.rem(t, 2) * 2 + t // 2
            parts[a][span(slot * own, own)] = nn(source[span(t * own, own)], enc[...]).astype(BF)
            return 0

        lax.fori_loop(0, 4, body, 0)
        to_mate[a].start()

    def pass_across(a):
        to_mate[a].wait()
        mine = span(core * 2 * own, 2 * own)
        kv_half[a] = (parts[a][mine].astype(F32) + kv_near[a].astype(F32)).astype(BF)
        to_across[a].start()

    s4.two()
    weight_part(0)
    poll()
    s4.three()
    pass_across(0)
    weight_part(1)
    s4.four()
    poll()
    d_cross = tn(s4.out[...], wq[...])
    pass_across(1)
    dv, gain_grad = norm_back(x2[...], gain_cross, d_cross)
    small[1:2, :width] = gain_grad
    g1, g1_low = scr.g1, scr.g1_low
    g1[...] = g2[...] + dv
    g1_low[...] = g1[...].astype(BF)
    g_small[own : 2 * own] = nn(s4.out[span(me * own, own)], cross_in[...]).astype(BF)
    g_small[2 * own : 3 * own] = nn(att_self[...], g1_low[...]).astype(BF)
    poll()
    d_att_self = nt(ins.wo_self[...], g1_low[...]).astype(BF)
    d_qkv = scr.d_qkv
    for h in range(heads):
        at = slice(h * DH, (h + 1) * DH)
        q = qkv[h * DH : (h + 1) * DH]
        k = qkv[own + h * DH : own + (h + 1) * DH]
        v = qkv[2 * own + h * DH : 2 * own + (h + 1) * DH]
        p = scr.p_self[h]
        grad = tn(v, d_att_self[at])
        ds = (p * (grad - jnp.sum(p * grad, axis=0, keepdims=True))).astype(BF)
        scr.ds_self[h] = ds.astype(F32)
        d_qkv[h * DH : (h + 1) * DH] = nn(k, ds).astype(BF)
        d_qkv[own + h * DH : own + (h + 1) * DH] = nt(q, ds).astype(BF)
        d_qkv[2 * own + h * DH : 2 * own + (h + 1) * DH] = nt(d_att_self[at], p.astype(BF)).astype(BF)
    poll()
    g_small[3 * own : 6 * own] = nn(d_qkv[...], self_in[...]).astype(BF)
    poll()
    s5 = tensor_sum(scr.s5)
    total = None
    for k, weight in enumerate(self_weights):
        part = tn(d_qkv[k * own : (k + 1) * own], weight[...])
        total = part if total is None else total + part
    s5.src[...] = total.astype(BF)
    s5.one()
    poll()
    rows_ref = scr.bucket_rows

    def count(b, _):
        hit = bucket[...] == b
        for h in range(heads):
            value = jnp.where(hit, scr.ds_self[h], 0.0)
            rows_ref[pl.ds(h * buckets + b, 1)] = jnp.sum(value, axis=0, keepdims=True)
        return 0

    s5.two()
    rows_ref[...] = jnp.zeros(rows_ref.shape, F32)
    lax.fori_loop(0, buckets, count, 0)
    position = jnp.sum(rows_ref[...].T, axis=0, keepdims=True)
    for g in range(cfg.groups):
        hot = jnp.where(group == g, 1.0, 0.0).astype(F32)
        small[8 + g : 9 + g, :tokens] = position * hot
    poll()

    saves = [None, None]

    def encoder_tile(r):
        at = slice(r * TILE, (r + 1) * TILE)
        slot = r % 2
        if saves[slot] is not None:
            saves[slot].wait()
        stage = scr.stage.at[slot]
        stage[...] = (nn(kc[at], wk[...]) + nn(vc[at], wv[...])).astype(BF)
        saves[slot] = fetch(stage, outs.encoder_grad.at[pl.ds(r * TILE, TILE)])

    for r in range(tiles // 2):
        encoder_tile(r)
        poll()
    for a in range(2):
        to_across[a].wait()
        g_small[(6 + a) * own : (7 + a) * own] = (
            kv_half[a, span(side * own, own)].astype(F32) + kv_far[a].astype(F32)
        ).astype(BF)
    poll()
    s5.three()
    for r in range(tiles // 2, tiles):
        encoder_tile(r)
        poll()
    s5.four()
    dv, gain_grad = norm_back(xv, gain_self, s5.out[...].astype(F32))
    outs.decoder_grad[...] = (g1[...] + dv).astype(BF)
    small[0:1, :width] = gain_grad
    for copy in saves:
        copy.wait()
    if summing:
        little = SmallSum(sems, place, scr.small)
        little.s0()
        poll()
        little.s1()
        poll()
        little.s2()
        poll()
        little.s3()
        poll()
        little.s4()
        outs.small_sum[...] = little.bufs[6][...]
        poll()
        for chunk in chunks:
            chunk.finish()
    else:
        for copy in [fetch(src, dst) for src, dst in zip(scr.grads, outs.grads)]:
            copy.wait()
        outs.small_sum[...] = small[...]
    for gather in gathers:
        gather.end()


def finish_kernel(own, buckets, heads, groups, ins, outs, scr):
    used = [0]

    def copy(src, dst):
        made = pltpu.make_async_copy(src, dst, scr.sems.at[used[0]])
        used[0] += 1
        made.start()
        return made

    loads = [copy(src, dst) for src, dst in zip(ins.grads, scr.low)]
    keeps = [copy(src, dst) for src, dst in zip(ins.kept, outs.kept)]
    for k in range(3):
        outs.gains[k][...] = ins.little[k : k + 1].reshape(outs.gains[k].shape)
    for h in range(heads):
        outs.position[h] = ins.little[8 : 8 + groups, h * buckets : (h + 1) * buckets]
    for k in range(3):
        loads[k].wait()
        scr.wide[k][...] = scr.low[k][...].astype(F32)
        keeps.append(copy(scr.wide[k], outs.wide[k]))
    loads[3].wait()
    for k, out in enumerate(outs.pieces):
        at = slice(k * own, (k + 1) * own)
        scr.wide[3][at] = scr.low[3][at].astype(F32)
        keeps.append(copy(scr.wide[3].at[at], out))
    for made in keeps:
        made.wait()


def shards(
    mesh_shape,
    decoder_in,
    encoder_out,
    out_grad,
    group_ids,
    target_mask,
    bucket_ids,
    gain_self,
    gain_cross,
    gain_ffn,
    query_self,
    key_self,
    value_self,
    output_self,
    query_cross,
    key_cross,
    value_cross,
    output_cross,
    gate_weight,
    up_weight,
    down_weight,
    position_bias,
):
    dp_size, tensor_size = mesh_shape
    query_count, tokens, width = decoder_in.shape
    assert query_count == 1 and tensor_size == 4 and dp_size % 2 == 0
    heads = query_self.shape[1] // DH
    own, all_heads = heads * DH, heads * tensor_size
    groups, buckets, _ = position_bias.shape
    rows, units = encoder_out.shape[1], gate_weight.shape[1]
    summing = dp_size == 8

    def vmem(*shape, kind=BF):
        return pltpu.VMEM(shape, kind)

    def shape_of(*shape, kind=BF):
        return jax.ShapeDtypeStruct(shape, kind)

    inputs = dict(
        x=(decoder_in[0], VMEM),
        out_grad=(out_grad[0], VMEM),
        encoder=(encoder_out[0], ANY),
        group=(group_ids, SMEM),
        mask=(target_mask, VMEM),
        bucket=(bucket_ids, VMEM),
        gains=[(gain_self, VMEM), (gain_cross, VMEM), (gain_ffn, VMEM)],
        wq_self=(query_self.T, VMEM),
        wk_self=(key_self.T, VMEM),
        wv_self=(value_self.T, VMEM),
        wo_self=(output_self, VMEM),
        wq_cross=(query_cross.T, VMEM),
        wk_cross=(key_cross.T, VMEM),
        wv_cross=(value_cross.T, VMEM),
        wo_cross=(output_cross, VMEM),
        gate_w=(gate_weight, ANY),
        up_w=(up_weight, ANY),
        down_w=(down_weight, ANY),
        table=(jnp.transpose(position_bias, (2, 0, 1)), SMEM),
    )
    grad_shapes = [(units, width), (width, units), (width, units), (8 * own, width)]
    outputs = dict(
        block_out=(shape_of(tokens, width), VMEM),
        decoder_grad=(shape_of(tokens, width), VMEM),
        encoder_grad=(shape_of(rows, width), ANY),
        grads=[(shape_of(*shape), ANY) for shape in grad_shapes],
        small_sum=(shape_of(16, width, kind=F32), VMEM),
    )
    plan = chunk_plan(own, width, units)
    all_own = all_heads * DH

    def sum_bufs(count, lanes):
        return [vmem(size, lanes) for size in (count, count // 2, count // 2, count // 2, count)]

    def chunk_bufs(in_x, source, size):
        lanes = grad_shapes[source][1]
        full = () if in_x else (0, 4)
        return [vmem(size if k in full else size // 2, lanes) for k in range(5)]

    token_low, token_wide = vmem(tokens, width), vmem(tokens, width, kind=F32)
    stats = vmem(16, tokens, kind=F32)
    halves = vmem(all_own // 2, tokens)
    scratch = dict(
        enc=vmem(rows, width), down=vmem(units, width), gate_w=vmem(width, units), up_w=vmem(width, units),
        self_in=token_low, cross_in=token_low, ffn_in=token_low, g1_low=token_low, g2_low=token_low,
        x2=token_wide, x3=token_wide, g1=token_wide, g2=token_wide,
        qkv=vmem(3 * own, tokens), d_qkv=vmem(3 * own, tokens), att_self=vmem(own, tokens),
        bucket=vmem(tokens, tokens, kind=jnp.int32), bucket_rows=vmem(128, tokens, kind=F32),
        p_self=vmem(heads, tokens, tokens, kind=F32), ds_self=vmem(heads, tokens, tokens, kind=F32),
        wk=vmem(all_own, width), wq=vmem(all_own, width), wv=vmem(all_own, width), wo=vmem(all_own, width),
        bq=vmem(all_own, 2 * tokens), bw=vmem(all_own, 2 * tokens),
        kc=vmem(rows, all_own), vc=vmem(rows, all_own), kt=vmem(all_own, rows), vt=vmem(all_own, rows),
        e=vmem(rows, all_heads * tokens), s=vmem(rows, 2 * tokens, kind=F32),
        mix=vmem(all_own, tokens), att=vmem(all_own, tokens), stat=stats, top=stats, lse=stats,
        mix_bufs=[halves] * 3 + [vmem(8, tokens, kind=F32)] * 3,
        delta=vmem(8, 2 * tokens, kind=F32),
        d_hidden=vmem(tokens, units, kind=F32), hidden=vmem(tokens, units),
        d_gate=vmem(tokens, units), d_up=vmem(tokens, units),
        s1=sum_bufs(tokens, width), s3=sum_bufs(tokens, width), so=sum_bufs(tokens, width),
        s4=sum_bufs(all_own, tokens), s5=sum_bufs(tokens, width),
        parts=[vmem(all_own, width)] * 2, kv_near=vmem(2, 2 * own, width),
        kv_half=vmem(2, 2 * own, width), kv_far=vmem(2, own, width),
        stage=vmem(2, TILE, width),
        grads=[vmem(*shape) for shape in grad_shapes],
        small=[vmem(16, width, kind=F32)] * (7 if summing else 1),
        chunks=[chunk_bufs(in_x, source, size) for in_x, source, _, size in plan] if summing else [],
        sems=pltpu.SemaphoreType.DMA((320,)),
    )
    pair = lambda entry: isinstance(entry, tuple)
    first = lambda tree: jax.tree.map(lambda entry: entry[0], tree, is_leaf=pair)
    second = lambda tree: jax.tree.map(lambda entry: entry[1], tree, is_leaf=pair)
    flat = jax.tree.leaves
    trees = [jax.tree.structure(first(inputs)), jax.tree.structure(first(outputs)), jax.tree.structure(scratch)]
    cfg = SimpleNamespace(
        trees=trees, heads=heads, all_heads=all_heads, width=width, tokens=tokens, rows=rows,
        buckets=buckets, groups=groups, summing=summing, chunks=plan, schedule=SCHEDULE,
    )
    result = pl.pallas_call(
        functools.partial(block_kernel, cfg),
        out_shape=flat(first(outputs)),
        in_specs=flat(second(inputs)),
        out_specs=flat(second(outputs)),
        scratch_shapes=flat(scratch),
        compiler_params=pltpu.CompilerParams(collective_id=0, has_side_effects=True, vmem_limit_bytes=63 << 20),
        name="block",
    )(*flat(first(inputs)))
    got = SimpleNamespace(**jax.tree.unflatten(trees[1], result))
    kept = [got.block_out, got.decoder_grad, got.encoder_grad]
    if summing:
        inputs = dict(grads=got.grads, kept=kept, little=got.small_sum)
        outputs = dict(
            kept=[shape_of(*value.shape) for value in kept],
            gains=[shape_of(width, kind=F32)] * 3,
            position=shape_of(heads, groups, buckets, kind=F32),
            wide=[shape_of(*shape, kind=F32) for shape in grad_shapes[:3]],
            pieces=[shape_of(own, width, kind=F32)] * 8,
        )
        scratch = dict(
            low=[vmem(*shape) for shape in grad_shapes],
            wide=[vmem(*shape, kind=F32) for shape in grad_shapes],
            sems=pltpu.SemaphoreType.DMA((32,)),
        )
        trees = [jax.tree.structure(inputs), jax.tree.structure(outputs), jax.tree.structure(scratch)]

        def finish(*refs):
            groups_of, at = [], 0
            for tree in trees:
                groups_of.append(SimpleNamespace(**jax.tree.unflatten(tree, refs[at : at + tree.num_leaves])))
                at += tree.num_leaves
            finish_kernel(own, buckets, heads, groups, *groups_of)

        specs_in = dict(grads=[ANY] * 4, kept=[ANY] * 3, little=VMEM)
        specs_out = dict(kept=[ANY] * 3, gains=[VMEM] * 3, position=VMEM, wide=[ANY] * 3, pieces=[ANY] * 8)
        result = pl.pallas_call(
            finish,
            out_shape=flat(outputs),
            in_specs=flat(specs_in),
            out_specs=flat(specs_out),
            scratch_shapes=flat(scratch),
            compiler_params=pltpu.CompilerParams(vmem_limit_bytes=63 << 20),
            name="finish",
        )(*flat(inputs))
        done = SimpleNamespace(**jax.tree.unflatten(trees[1], result))
        kept, gain_grads, position = done.kept, done.gains, jnp.transpose(done.position, (1, 2, 0))
        wide, pieces = done.wide, done.pieces
    else:
        sums, little = lax.psum(([value.astype(F32) for value in got.grads], got.small_sum), "dp")
        wide = sums[:3]
        pieces = [sums[3][k * own : (k + 1) * own] for k in range(8)]
        gain_grads = [little[k] for k in range(3)]
        position = little[8 : 8 + groups, : heads * buckets].reshape(groups, heads, buckets)
        position = jnp.transpose(position, (0, 2, 1))
    down, gate, up = wide
    oc, qc, os, qs, ks, vs, kc, vc = pieces
    return (
        *[value[None] for value in kept], *gain_grads,
        qs.T, ks.T, vs.T, os, qc.T, kc.T, vc.T, oc, gate, up, down, position,
    )


def solution(mesh):
    rows = P("dp", None, None)
    encoder = P("dp", "tensor", None)
    columns, lines, whole = P(None, "tensor"), P("tensor", None), P()
    head_table = P(None, None, "tensor")
    weights = (columns, columns, columns, lines, columns, columns, columns, lines, columns, columns, lines, head_table)
    return jax.shard_map(
        functools.partial(shards, (mesh.shape["dp"], mesh.shape["tensor"])),
        mesh=mesh,
        in_specs=(rows, encoder, rows, P("dp"), P("dp", None), whole, whole, whole, whole) + weights,
        out_specs=(rows, rows, encoder, whole, whole, whole) + weights,
        check_vma=False,
    )
```

```python
import functools
from types import SimpleNamespace

import jax
import jax.numpy as jnp
from jax import lax
from jax.experimental import pallas as pl
from jax.experimental.pallas import tpu as pltpu
from jax.sharding import PartitionSpec as P

DH = 64
EPS = 1e-06
NEG = -1000000000.0
TILE = 256
MESH = pl.DeviceIdType.MESH
BF = jnp.bfloat16
F32 = jnp.float32
VMEM = pl.BlockSpec(memory_space=pltpu.VMEM)
SMEM = pl.BlockSpec(memory_space=pltpu.SMEM)
ANY = pl.BlockSpec(memory_space=pl.ANY)
GELU_SCALE = 0.7978845608028654
GELU_CUBIC = 0.044715


IN_X = (True, True, True, True, True, False, True, False, True, True, True, True, True, False)
SCHEDULE = (
    (),
    ((3, 0),),
    ((2, 0), (5, 0),),
    ((4, 0),),
    (),
    ((3, 1),),
    (),
    ((2, 1), (6, 0), (5, 1),),
    ((1, 0),),
    ((0, 0), (3, 2), (4, 1),),
    (),
    (),
    ((5, 2), (3, 3), (4, 2), (2, 2), (1, 1), (6, 1),),
    (),
    (),
    ((4, 3), (1, 2),),
    ((2, 3), (5, 3), (3, 4),),
    ((6, 2), (0, 1), (12, 0),),
    (),
    ((8, 0), (5, 4),),
    (),
    ((0, 2), (9, 0), (7, 0),),
    (),
    ((1, 3), (7, 1), (2, 4), (0, 3), (12, 1),),
    ((4, 4), (12, 2),),
    (),
    ((8, 1), (8, 2), (13, 0), (7, 2), (10, 0), (11, 0), (6, 3), (9, 1), (12, 3), (2, 5), (13, 1), (0, 4), (6, 4), (1, 4), (7, 3), (13, 2), (8, 3), (5, 5), (9, 2),),
    ((7, 4), (3, 5), (10, 1), (10, 2), (11, 1), (9, 3), (8, 4), (12, 4), (11, 2), (10, 3),),
    (),
    ((9, 4),),
    (),
    ((11, 3), (6, 5), (10, 4), (12, 5), (11, 4),),
    ((4, 5),),
    (),
    ((13, 3), (13, 4), (0, 5), (9, 5), (13, 5), (7, 5), (1, 5), (8, 5), (11, 5), (10, 5),),
)


def nn(left, right):
    return lax.dot_general(left, right, (((1,), (0,)), ((), ())), preferred_element_type=F32)


def nt(left, right):
    return lax.dot_general(left, right, (((1,), (1,)), ((), ())), preferred_element_type=F32)


def tn(left, right):
    return lax.dot_general(left, right, (((0,), (0,)), ((), ())), preferred_element_type=F32)


def span(start, size, step=None):
    return pl.ds(pl.multiple_of(start, step or size), size)


class Sems:
    def __init__(self, ref):
        self.ref, self.used = ref, 0

    def take(self):
        self.used += 1
        assert self.used <= self.ref.shape[0]
        return self.ref.at[self.used - 1]


class Wire:
    def __init__(self, sems, src, dst, device):
        self.copy = pltpu.make_async_remote_copy(
            src_ref=src, dst_ref=dst, send_sem=sems.take(), recv_sem=sems.take(), device_id=device, device_id_type=MESH
        )

    def start(self):
        self.copy.start()

    def sent(self):
        self.copy.wait_send()

    def came(self):
        self.copy.wait_recv()

    def wait(self):
        self.copy.wait()


class TensorSum:
    def __init__(self, sems, place, src, near, half, far, out):
        self.src, self.near, self.half, self.far, self.out = src, near, half, far, out
        size = src.shape[0] // 2
        self.mine = span(place.core * size, size)
        other = span((1 - place.core) * size, size)
        self.first = Wire(sems, src.at[other], near, place.mate)
        self.second = Wire(sems, half, far, place.across)
        self.third = Wire(sems, out.at[self.mine], out.at[self.mine], place.mate)

    def one(self):
        self.first.start()

    def two(self):
        self.first.wait()
        self.half[...] = (self.src[self.mine].astype(F32) + self.near[...].astype(F32)).astype(BF)
        self.second.start()

    def three(self):
        self.second.wait()
        self.out[self.mine] = (self.half[...].astype(F32) + self.far[...].astype(F32)).astype(BF)
        self.third.start()

    def four(self):
        self.third.wait()


class TensorMix:
    def __init__(self, sems, place, mix, stat, bufs, out, total):
        self.place, self.mix, self.stat, self.out, self.total = place, mix, stat, out, total
        near, half, far, near_stat, half_stat, far_stat = bufs
        self.bufs = bufs
        size, core = mix.shape[0] // 2, place.core
        self.size = size
        self.mine, other = span(core * size, size), span((1 - core) * size, size)
        self.mine_stat, other_stat = span(core * 8, 8), span((1 - core) * 8, 8)
        self.first = [
            Wire(sems, mix.at[other], near, place.mate),
            Wire(sems, stat.at[other_stat], near_stat, place.mate),
        ]
        self.second = [Wire(sems, half, far, place.across), Wire(sems, half_stat, far_stat, place.across)]
        self.third = [
            Wire(sems, out.at[self.mine], out.at[self.mine], place.mate),
            Wire(sems, total.at[self.mine_stat], total.at[self.mine_stat], place.mate),
        ]

    def join(self, ours, theirs, ours_stat, theirs_stat, flip, store):
        low_stat = jnp.where(flip, theirs_stat, ours_stat)
        high_stat = jnp.where(flip, ours_stat, theirs_stat)
        top = jnp.maximum(low_stat, high_stat)
        total = top + jnp.log(jnp.exp(low_stat - top) + jnp.exp(high_stat - top))
        low_share, high_share = jnp.exp(low_stat - total), jnp.exp(high_stat - total)
        for h in range(self.size // DH):
            rows = slice(h * DH, (h + 1) * DH)
            a, b = ours(rows), theirs(rows)
            low, high = jnp.where(flip, b, a), jnp.where(flip, a, b)
            store(rows, (low * low_share[h : h + 1] + high * high_share[h : h + 1]).astype(BF))
        return total

    def one(self):
        for wire in self.first:
            wire.start()

    def two(self):
        near, half, far, near_stat, half_stat, far_stat = self.bufs
        core, size = self.place.core, self.size
        for wire in self.first:
            wire.wait()

        def ours(rows):
            return self.mix[span(core * size + rows.start, DH)].astype(F32)

        def store(rows, value):
            half[rows] = value

        half_stat[...] = self.join(
            ours, lambda rows: near[rows].astype(F32), self.stat[self.mine_stat], near_stat[...], core == 1, store
        )
        for wire in self.second:
            wire.start()

    def three(self):
        near, half, far, near_stat, half_stat, far_stat = self.bufs
        core, size = self.place.core, self.size
        for wire in self.second:
            wire.wait()

        def store(rows, value):
            self.out[span(core * size + rows.start, DH)] = value

        self.total[self.mine_stat] = self.join(
            lambda rows: half[rows].astype(F32),
            lambda rows: far[rows].astype(F32),
            half_stat[...],
            far_stat[...],
            self.place.side == 1,
            store,
        )
        for wire in self.third:
            wire.start()

    def four(self):
        for wire in self.third:
            wire.wait()


class WeightGather:
    def __init__(self, sems, place, own, whole, local):
        rows = own.shape[0]
        half = rows // 2
        me, core, side, x = place.me, place.core, place.side, place.x
        there = (1 - side) * 2 + core
        self.own, self.whole = own, whole
        mine = span(me * rows, rows)
        direct = span(there * rows + x * half, half)
        relayed = span(there * rows + (1 - x) * half, half)
        self.across = Wire(sems, own.at[span(x * half, half)], whole.at[span(me * rows + x * half, half)], place.across)
        self.mate = Wire(sems, own, whole.at[mine], place.mate)
        self.side = Wire(sems, whole.at[direct], whole.at[direct], place.beside)
        self.direct = Wire(sems, whole.at[direct], whole.at[direct], place.mate)
        self.relayed = Wire(sems, whole.at[relayed], whole.at[relayed], place.mate)
        self.keep = pltpu.make_async_copy(own, whole.at[mine], local)

    def start(self):
        self.across.start()
        self.mate.start()
        self.keep.start()

    def one(self):
        self.across.came()
        self.side.start()
        self.direct.start()

    def two(self):
        self.side.came()
        self.relayed.start()

    def three(self):
        self.mate.came()
        self.keep.wait()
        self.direct.came()
        self.relayed.came()

    def end(self):
        for wire in (self.across, self.mate, self.side, self.direct, self.relayed):
            wire.sent()


class QueryGather:
    def __init__(self, sems, place, own, whole):
        rows = own.shape[0]
        there = (1 - place.side) * 2 + place.core
        self.own, self.whole, self.mine = own, whole, span(place.me * rows, rows)
        self.across = Wire(sems, own, whole.at[self.mine], place.across)
        self.mate = Wire(sems, own, whole.at[self.mine], place.mate)
        theirs = whole.at[span(there * rows, rows)]
        self.onward = Wire(sems, theirs, theirs, place.mate)

    def one(self):
        self.across.start()
        self.mate.start()
        self.whole[self.mine] = self.own[...]

    def two(self):
        self.across.came()
        self.onward.start()

    def three(self):
        self.mate.came()
        self.onward.came()

    def end(self):
        for wire in (self.across, self.mate, self.onward):
            wire.sent()


class ChunkX:
    def __init__(self, sems, place, g, out, bufs):
        self.place = place
        near, inn, mid, tot, fin = self.bufs = bufs
        half = g.shape[0] // 2
        x = place.x
        self.g, self.mine = g, span(x * half, half)
        other = span((1 - x) * half, half)
        self.rs = Wire(sems, g.at[other], near, place.beside)
        self.out = Wire(sems, g.at[self.mine], inn, place.pair)
        self.middle = Wire(sems, g.at[self.mine], mid, place.middle)
        self.back = Wire(sems, tot, tot, place.pair)
        self.ag = Wire(sems, tot, fin, place.beside)
        self.save = [
            pltpu.make_async_copy(tot, out.at[self.mine], sems.take()),
            pltpu.make_async_copy(fin, out.at[other], sems.take()),
        ]

    def s0(self):
        self.rs.start()

    def s1(self):
        self.rs.wait()
        self.g[self.mine] = self.g[self.mine] + self.bufs[0][...]

        @pl.when(self.place.end)
        def _():
            self.out.start()

    def s2(self):
        @pl.when(self.place.inner)
        def _():
            self.out.came()
            self.g[self.mine] = self.g[self.mine] + self.bufs[1][...]
            self.middle.start()

    def s3(self):
        @pl.when(self.place.inner)
        def _():
            self.middle.wait()
            self.bufs[3][...] = self.g[self.mine] + self.bufs[2][...]
            self.back.start()
            self.ag.start()
            self.save[0].start()

    def s4(self):
        @pl.when(self.place.end)
        def _():
            self.back.came()
            self.ag.start()
            self.save[0].start()

    def s5(self):
        self.ag.came()
        self.save[1].start()

    def finish(self):
        @pl.when(self.place.end)
        def _():
            self.out.sent()

        @pl.when(self.place.inner)
        def _():
            self.back.sent()

        self.ag.sent()
        for copy in self.save:
            copy.wait()


class ChunkZ:
    def __init__(self, sems, place, g, out, bufs):
        self.place = place
        inn, mid, r, xr, tot = self.bufs = bufs
        half = g.shape[0] // 2
        at = place.high
        self.g, self.mine = g, span(at * half, half)
        self.other = span((1 - at) * half, half)
        self.out = Wire(sems, g, inn, place.pair)
        self.rs = Wire(sems, g.at[self.other], mid, place.middle)
        self.x = Wire(sems, r, xr, place.beside)
        self.ag = Wire(sems, tot.at[self.mine], tot.at[self.mine], place.middle)
        self.back = [
            Wire(sems, tot.at[self.mine], tot.at[self.mine], place.pair),
            Wire(sems, tot.at[self.other], tot.at[self.other], place.pair),
        ]
        self.save = pltpu.make_async_copy(tot, out, sems.take())

    def s0(self):
        @pl.when(self.place.end)
        def _():
            self.out.start()

    def s1(self):
        @pl.when(self.place.inner)
        def _():
            self.out.came()
            self.g[...] = self.g[...] + self.bufs[0][...]
            self.rs.start()

    def s2(self):
        @pl.when(self.place.inner)
        def _():
            self.rs.wait()
            self.bufs[2][...] = self.g[self.mine] + self.bufs[1][...]
            self.x.start()

    def s3(self):
        @pl.when(self.place.inner)
        def _():
            self.x.wait()
            self.bufs[4][self.mine] = self.bufs[2][...] + self.bufs[3][...]
            self.ag.start()
            self.back[0].start()

    def s4(self):
        @pl.when(self.place.inner)
        def _():
            self.ag.came()
            self.back[1].start()
            self.save.start()

    def s5(self):
        @pl.when(self.place.end)
        def _():
            for wire in self.back:
                wire.came()
            self.save.start()

    def finish(self):
        @pl.when(self.place.end)
        def _():
            self.out.sent()

        @pl.when(self.place.inner)
        def _():
            self.ag.sent()
            for wire in self.back:
                wire.sent()

        self.save.wait()


class SmallSum:
    def __init__(self, sems, place, bufs):
        self.place = place
        own, near, sum1, inn, sum2, mid, tot = self.bufs = bufs
        self.x = Wire(sems, own, near, place.beside)
        self.out = Wire(sems, sum1, inn, place.pair)
        self.middle = Wire(sems, sum2, mid, place.middle)
        self.back = Wire(sems, tot, tot, place.pair)

    def s0(self):
        self.x.start()

    def s1(self):
        own, near, sum1, inn, sum2, mid, tot = self.bufs
        self.x.wait()
        sum1[...] = own[...] + near[...]

        @pl.when(self.place.end)
        def _():
            self.out.start()

    def s2(self):
        own, near, sum1, inn, sum2, mid, tot = self.bufs

        @pl.when(self.place.inner)
        def _():
            self.out.came()
            sum2[...] = sum1[...] + inn[...]
            self.middle.start()

    def s3(self):
        own, near, sum1, inn, sum2, mid, tot = self.bufs

        @pl.when(self.place.inner)
        def _():
            self.middle.wait()
            tot[...] = sum2[...] + mid[...]
            self.back.start()
            self.back.sent()

    def s4(self):
        @pl.when(self.place.end)
        def _():
            self.out.sent()
            self.back.came()


def rms_scale(values):
    return lax.rsqrt(jnp.mean(values * values, axis=-1, keepdims=True) + EPS)


def norm_back(values, gain, dy):
    scale = rms_scale(values)
    normal = values * scale
    gain_grad = jnp.sum(dy * normal, axis=0, keepdims=True)
    pulled = dy * gain
    mean = jnp.mean(pulled * normal, axis=-1, keepdims=True)
    return scale * (pulled - normal * mean), gain_grad


def fold(values, op):
    rows, width = values.shape
    return op(values.reshape(rows // 8, 8, width), axis=0)


def chunk_plan(own, width, units):
    plan = [(0, k * (units // 2), units // 2) for k in range(2)]
    plan += [(a, k * (width // 2), width // 2) for a in (1, 2) for k in range(2)]
    plan += [(3, k * own, own) for k in range(8)]
    return [(in_x, *block) for in_x, block in zip(IN_X, plan)]


def block_kernel(cfg, *refs):
    groups, at = [], 0
    for tree in cfg.trees:
        groups.append(SimpleNamespace(**jax.tree.unflatten(tree, refs[at : at + tree.num_leaves])))
        at += tree.num_leaves
    ins, outs, scr = groups
    gain_self, gain_cross, gain_ffn = (gain[...].reshape(1, cfg.width) for gain in ins.gains)
    heads, all_heads, width, tokens, rows = cfg.heads, cfg.all_heads, cfg.width, cfg.tokens, cfg.rows
    own, pairs, tiles = heads * DH, all_heads // 2, rows // TILE
    summing = cfg.summing
    sems = Sems(scr.sems)
    dp, me = lax.axis_index("dp"), lax.axis_index("tensor")
    core, side = lax.rem(me, 2), me // 2
    x, z = lax.rem(dp, 2), dp // 2
    place = SimpleNamespace(
        me=me,
        core=core,
        side=side,
        x=x,
        mate=(dp, side * 2 + 1 - core),
        across=(dp, (1 - side) * 2 + core),
        beside=(dp + 1 - 2 * x, me),
    )
    barrier = pltpu.get_barrier_semaphore()
    for friend in (place.mate, place.across, place.beside):
        pl.semaphore_signal(barrier, inc=1, device_id=friend, device_id_type=MESH)
    if summing:
        inner = jnp.logical_or(z == 1, z == 2)
        place.inner, place.end = inner, jnp.logical_not(inner)
        place.high = z // 2
        place.pair = ((z + 1 - 2 * lax.rem(z, 2)) * 2 + x, me)
        place.middle = ((3 - z) * 2 + x, me)
        pl.semaphore_signal(barrier, inc=1, device_id=place.pair, device_id_type=MESH)

        @pl.when(inner)
        def _():
            pl.semaphore_signal(barrier, inc=1, device_id=place.middle, device_id_type=MESH)

    def fetch(src, dst):
        copy = pltpu.make_async_copy(src, dst, sems.take())
        copy.start()
        return copy

    enc, down, gate_w, up_w = scr.enc, scr.down, scr.gate_w, scr.up_w
    first_loads = [fetch(ins.x, scr.x)]
    self_weights = scr.wqkv
    for src, dst in zip((ins.wq_self, ins.wk_self, ins.wv_self), self_weights):
        first_loads.append(fetch(src, dst))
    load_bucket, load_out = fetch(ins.bucket, scr.bucket), fetch(ins.wo_self, scr.wo_self)
    load_query = fetch(ins.wq_cross, scr.wq_own)
    load_enc = fetch(ins.encoder, enc)
    load_ffn = [fetch(ins.out_grad, scr.og), fetch(ins.down_w, down), fetch(ins.gate_w, gate_w), fetch(ins.up_w, up_w)]

    for load in first_loads:
        load.wait()
    xv = scr.x[...].astype(F32)
    self_in = scr.self_in
    self_in[...] = (xv * rms_scale(xv) * gain_self).astype(BF)
    qkv = scr.qkv
    for k, weight in enumerate(self_weights):
        qkv[k * own : (k + 1) * own] = nt(weight[...], self_in[...]).astype(BF)
    if summing:
        pl.semaphore_wait(barrier, 4 + inner.astype(jnp.int32))
    else:
        pl.semaphore_wait(barrier, 3)
    wk, wq, wv, wo = scr.wk, scr.wq, scr.wv, scr.wo
    get_k, get_q, get_v, get_o = gathers = [
        WeightGather(sems, place, part, whole, sems.take())
        for part, whole in ((ins.wk_cross, wk), (ins.wq_cross, wq), (ins.wv_cross, wv), (ins.wo_cross, wo))
    ]
    get_k.start()
    load_bucket.wait()
    scr.bucket[...] = scr.bucket[...].T
    bucket = scr.bucket
    keep = jnp.broadcast_to(ins.mask[...].astype(F32), (tokens, tokens)).T
    j_at = lax.broadcasted_iota(jnp.int32, (tokens, tokens), 0)
    i_at = lax.broadcasted_iota(jnp.int32, (tokens, tokens), 1)
    allowed = jnp.logical_or(jnp.logical_and(j_at <= i_at, keep == 1.0), j_at == i_at)
    group = ins.group[0]
    buckets = cfg.buckets
    for h in range(heads):
        scr.p_self[h] = jnp.full((tokens, tokens), NEG, F32)

    def spread(b, _):
        hit = jnp.logical_and(bucket[...] == b, allowed)
        for h in range(heads):
            scr.p_self[h] = jnp.where(hit, ins.table[h, group, b], scr.p_self[h])
        return 0

    lax.fori_loop(0, buckets, spread, 0)
    att_self = scr.att_self

    def attend(h):
        q = qkv[h * DH : (h + 1) * DH]
        k = qkv[own + h * DH : own + (h + 1) * DH]
        v = qkv[2 * own + h * DH : 2 * own + (h + 1) * DH]
        s = tn(k, q) + scr.p_self[h]
        e = jnp.exp(s - jnp.max(s, axis=0, keepdims=True))
        p = e / jnp.sum(e, axis=0, keepdims=True)
        scr.p_self[h] = p
        att_self[h * DH : (h + 1) * DH] = nn(v, p.astype(BF)).astype(BF)

    for h in range(heads):
        attend(h)

    def tensor_sum(bufs):
        return TensorSum(sems, place, *bufs)

    s1 = tensor_sum(scr.s1)
    load_out.wait()
    s1.src[...] = tn(att_self[...], scr.wo_self[...]).astype(BF)
    s1.one()
    s1.two()
    get_v.start()
    get_k.one()
    load_enc.wait()
    kc, vc, e_ref = scr.kc, scr.vc, scr.e

    def project(dst, weight, first, count):
        lanes = span(first, count, 2 * DH)

        def body(r, _):
            at = span(r * TILE, TILE)
            dst[at, lanes] = nt(enc[at], weight[lanes]).astype(BF)
            return 0

        lax.fori_loop(0, tiles, body, 0)

    s1.three()
    s1.four()
    x2 = scr.x2
    x2[...] = scr.x[...].astype(F32) + s1.out[...].astype(F32)
    cross_in = scr.cross_in
    cross_in[...] = (x2[...] * rms_scale(x2[...]) * gain_cross).astype(BF)
    load_query.wait()
    scr.q_own[...] = nt(scr.wq_own[...], cross_in[...]).astype(BF)
    get_query = QueryGather(sems, place, scr.q_own, scr.q_t)
    get_query.one()
    get_o.start()
    get_q.start()
    get_k.two()
    get_v.one()
    get_k.three()
    project(kc, wk, 0, all_heads * DH)
    get_query.two()
    bq, bw = scr.bq, scr.bw
    bq[...] = jnp.zeros(bq.shape, BF)
    bw[...] = jnp.zeros(bw.shape, BF)
    get_query.three()
    for h in range(all_heads):
        at = slice(h * DH, (h + 1) * DH)
        bq[at, (h % 2) * tokens : (h % 2 + 1) * tokens] = scr.q_t[at]
    s_ref, mix, stat, top_ref = scr.s, scr.mix, scr.stat, scr.top
    stat[...] = jnp.zeros(stat.shape, F32)
    top_ref[...] = jnp.zeros(top_ref.shape, F32)
    per_half = pairs // 2

    def stat_row(p):
        return (p // per_half) * 8 + 2 * (p - (p // per_half) * per_half)

    def score_pair(p, _):
        head_at = span(p * 2 * DH, 2 * DH)
        score_at = span(p * 2 * tokens, 2 * tokens)
        weights = bq[head_at]
        top = None
        for r in range(tiles):
            at = slice(r * TILE, (r + 1) * TILE)
            s = nn(kc[at, head_at], weights)
            s_ref[at] = s
            part = fold(s, jnp.max)
            top = part if top is None else jnp.maximum(top, part)
        top = jnp.max(top, axis=0, keepdims=True)
        total = None
        for r in range(tiles):
            at = slice(r * TILE, (r + 1) * TILE)
            e = jnp.exp(s_ref[at] - top)
            part = fold(e, jnp.sum)
            total = part if total is None else total + part
            e_ref[at, score_at] = e.astype(BF)
        total = jnp.sum(total, axis=0, keepdims=True)
        scr.inverse[pl.ds(p, 1)] = 1.0 / total
        lse = top + jnp.log(total)
        row = stat_row(p)
        for k in range(2):
            lanes = slice(k * tokens, (k + 1) * tokens)
            stat[pl.ds(row + k, 1)] = lse[:, lanes]
            top_ref[pl.ds(row + k, 1)] = top[:, lanes]
        return 0

    def mix_pair(p, _):
        acc = tn(vc[:, span(p * 2 * DH, 2 * DH)], e_ref[:, span(p * 2 * tokens, 2 * tokens)])
        inverse = scr.inverse[pl.ds(p, 1)]
        for k in range(2):
            lanes = slice(k * tokens, (k + 1) * tokens)
            value = acc[k * DH : (k + 1) * DH, lanes] * inverse[:, lanes]
            mix[span(p * 2 * DH + k * DH, DH)] = value.astype(BF)
        return 0

    lax.fori_loop(0, pairs - 2, score_pair, 0)
    get_v.two()
    lax.fori_loop(pairs - 2, pairs, score_pair, 0)
    get_o.one()
    get_v.three()
    att, lse = scr.att, scr.lse
    s2 = TensorMix(sems, place, mix, stat, scr.mix_bufs, att, lse)
    for half in (1 - core, core):
        project(vc, wv, half * per_half * 2 * DH, per_half * 2 * DH)
        lax.fori_loop(half * per_half, (half + 1) * per_half, mix_pair, 0)
        if half is not core:
            s2.one()
            get_q.one()
    s2.two()
    for load in load_ffn:
        load.wait()
    og = scr.og
    scr.d_hidden[...] = nt(og[...], down[...]).astype(BF).astype(F32)
    get_o.two()
    s2.three()
    get_o.three()
    s2.four()
    x3 = scr.x3
    x3[...] = x2[...] + tn(att[...], wo[...])
    ffn_in = scr.ffn_in
    ffn_in[...] = (x3[...] * rms_scale(x3[...]) * gain_ffn).astype(BF)
    gate = nn(ffn_in[...], gate_w[...])
    up = nn(ffn_in[...], up_w[...])
    squared = gate * gate
    curve = jnp.tanh(GELU_SCALE * (gate + GELU_CUBIC * (squared * gate)))
    gelu = 0.5 * gate * (1.0 + curve)
    slope = 0.5 * (1.0 + curve) + 0.5 * gate * (1.0 - curve * curve) * (
        GELU_SCALE * (1.0 + 3.0 * GELU_CUBIC * squared)
    )
    d_hidden = scr.d_hidden[...]
    scr.hidden[...] = (gelu * up).astype(BF)
    scr.d_gate[...] = (d_hidden * up * slope).astype(BF)
    scr.d_up[...] = (d_hidden * gelu).astype(BF)

    chunks = []
    if summing:
        for (in_x, source, start, size), bufs in zip(cfg.chunks, scr.chunks):
            rows_at = pl.ds(start, size)
            maker = ChunkX if in_x else ChunkZ
            chunks.append(maker(sems, place, scr.grads[source].at[rows_at], outs.grads[source].at[rows_at], bufs))
    schedule = iter(cfg.schedule)

    def poll():
        if summing:
            for n, k in next(schedule):
                chunk = chunks[n]
                (chunk.s0, chunk.s1, chunk.s2, chunk.s3, chunk.s4, chunk.s5)[k]()

    g_down, g_gate, g_up, g_small = scr.grads
    g_down[...] = tn(scr.hidden[...], og[...]).astype(BF)
    poll()
    g_gate[...] = tn(ffn_in[...], scr.d_gate[...]).astype(BF)
    poll()
    g_up[...] = tn(ffn_in[...], scr.d_up[...]).astype(BF)
    poll()
    s3, so = tensor_sum(scr.s3), tensor_sum(scr.so)
    s3.src[...] = (nt(scr.d_gate[...], gate_w[...]) + nt(scr.d_up[...], up_w[...])).astype(BF)
    s3.one()
    so.src[...] = nn(scr.hidden[...], down[...]).astype(BF)
    s3.two()
    poll()
    get_q.two()
    poll()
    s3.three()
    so.one()
    s3.four()
    so.two()
    poll()
    g2, g2_low = scr.g2, scr.g2_low
    dv, gain_grad = norm_back(x3[...], gain_ffn, s3.out[...].astype(F32))
    g2[...] = og[...].astype(F32) + dv
    g2_low[...] = g2[...].astype(BF)
    small = scr.small[0]
    small[...] = jnp.zeros(small.shape, F32)
    small[2:3, :width] = gain_grad
    g_small[0:own] = nn(att[span(me * own, own)], g2_low[...]).astype(BF)
    poll()
    d_att = nt(wo[...], g2_low[...])
    delta_ref = scr.delta
    for h in range(all_heads):
        at = slice(h * DH, (h + 1) * DH)
        p, k = divmod(h, 2)
        row = (p // per_half) * 8 + 2 * (p % per_half) + k
        share = jnp.exp(top_ref[row : row + 1] - lse[row : row + 1])
        low = (d_att[at] * share).astype(BF)
        bw[at, k * tokens : (k + 1) * tokens] = low
        delta_ref[p : p + 1, k * tokens : (k + 1) * tokens] = jnp.sum(
            low.astype(F32) * att[at].astype(F32), axis=0, keepdims=True
        )
    so.three()
    s4 = tensor_sum(scr.s4)

    def backward_pair(p, _):
        head_at = span(p * 2 * DH, 2 * DH)
        score_at = span(p * 2 * tokens, 2 * tokens)
        wq_block, wa_block = bq[head_at], bw[head_at]
        delta = delta_ref[pl.ds(p, 1)]
        acc = None
        for r in range(tiles):
            at = slice(r * TILE, (r + 1) * TILE)
            e = e_ref[at, score_at]
            grad = nn(vc[at, head_at], wa_block)
            ds = (e.astype(F32) * (grad - delta)).astype(BF)
            part = tn(kc[at, head_at], ds)
            acc = part if acc is None else acc + part
            kc[at, head_at] = nt(ds, wq_block).astype(BF)
            vc[at, head_at] = nt(e, wa_block).astype(BF)
        for k in range(2):
            value = acc[k * DH : (k + 1) * DH, k * tokens : (k + 1) * tokens]
            s4.src[span(p * 2 * DH + k * DH, DH)] = value.astype(BF)
        return 0

    far_at, near_at = (1 - side) * per_half, side * per_half
    far_parts, near_parts = scr.far_parts, scr.near_parts
    kv_near, kv_home, kv_half, kv_far = scr.kv_near, scr.kv_home, scr.kv_half, scr.kv_far
    to_mate, to_across, to_home = [], [], []
    mine, other = span(core * own, own), span((1 - core) * own, own)
    for a in range(2):
        to_mate.append(Wire(sems, far_parts[a].at[other], kv_near.at[a], place.mate))
        to_across.append(Wire(sems, kv_half.at[a], kv_far.at[a], place.across))
        to_home.append(Wire(sems, near_parts[a].at[other], kv_home.at[a], place.mate))

    def weight_part(dst, source, first):
        rows_of = source[:, span(first * 2 * DH, 2 * own, 2 * DH)]

        def body(t, _):
            lanes = span(t * TILE, TILE)
            dst[:, lanes] = tn(rows_of, enc[:, lanes]).astype(BF)
            return 0

        lax.fori_loop(0, width // TILE, body, 0)

    def pass_across(a):
        to_mate[a].wait()
        kv_half[a] = (far_parts[a][mine].astype(F32) + kv_near[a].astype(F32)).astype(BF)
        to_across[a].start()

    for p in range(per_half):
        poll()
        lax.fori_loop(far_at + p, far_at + p + 1, backward_pair, 0)
    poll()
    so.four()
    scr.out_stage[...] = (x3[...] + so.out[...].astype(F32)).astype(BF)
    token_saves = [fetch(scr.out_stage, outs.block_out)]
    weight_part(far_parts[0], kc, far_at)
    to_mate[0].start()
    weight_part(far_parts[1], vc, far_at)
    to_mate[1].start()
    pass_across(0)
    for p in range(per_half):
        poll()
        lax.fori_loop(near_at + p, near_at + p + 1, backward_pair, 0)
    s4.one()
    poll()
    weight_part(near_parts[0], kc, near_at)
    to_home[0].start()
    s4.two()
    pass_across(1)
    poll()
    weight_part(near_parts[1], vc, near_at)
    to_home[1].start()
    s4.three()
    poll()

    def kv_done(a):
        to_home[a].wait()
        to_across[a].wait()
        total = near_parts[a][mine].astype(F32) + kv_home[a].astype(F32) + kv_far[a].astype(F32)
        g_small[(6 + a) * own : (7 + a) * own] = total.astype(BF)

    kv_done(0)
    s4.four()
    poll()
    get_q.three()
    d_cross = tn(s4.out[...], wq[...])
    dv, gain_grad = norm_back(x2[...], gain_cross, d_cross)
    small[1:2, :width] = gain_grad
    g1, g1_low = scr.g1, scr.g1_low
    g1[...] = g2[...] + dv
    g1_low[...] = g1[...].astype(BF)
    g_small[own : 2 * own] = nn(s4.out[span(me * own, own)], cross_in[...]).astype(BF)
    g_small[2 * own : 3 * own] = nn(att_self[...], g1_low[...]).astype(BF)
    poll()
    d_att_self = nt(scr.wo_self[...], g1_low[...]).astype(BF)
    d_qkv = scr.d_qkv
    for h in range(heads):
        at = slice(h * DH, (h + 1) * DH)
        q = qkv[h * DH : (h + 1) * DH]
        k = qkv[own + h * DH : own + (h + 1) * DH]
        v = qkv[2 * own + h * DH : 2 * own + (h + 1) * DH]
        p = scr.p_self[h]
        grad = tn(v, d_att_self[at])
        ds = (p * (grad - jnp.sum(p * grad, axis=0, keepdims=True))).astype(BF)
        scr.ds_self[h] = ds.astype(F32)
        d_qkv[h * DH : (h + 1) * DH] = nn(k, ds).astype(BF)
        d_qkv[own + h * DH : own + (h + 1) * DH] = nt(q, ds).astype(BF)
        d_qkv[2 * own + h * DH : 2 * own + (h + 1) * DH] = nt(d_att_self[at], p.astype(BF)).astype(BF)
    poll()
    g_small[3 * own : 6 * own] = nn(d_qkv[...], self_in[...]).astype(BF)
    poll()
    s5 = tensor_sum(scr.s5)
    total = None
    for k, weight in enumerate(self_weights):
        part = tn(d_qkv[k * own : (k + 1) * own], weight[...])
        total = part if total is None else total + part
    s5.src[...] = total.astype(BF)
    s5.one()
    poll()
    rows_ref = scr.bucket_rows

    def count(b, _):
        hit = bucket[...] == b
        for h in range(heads):
            value = jnp.where(hit, scr.ds_self[h], 0.0)
            rows_ref[pl.ds(h * buckets + b, 1)] = jnp.sum(value, axis=0, keepdims=True)
        return 0

    s5.two()
    rows_ref[...] = jnp.zeros(rows_ref.shape, F32)
    lax.fori_loop(0, buckets, count, 0)
    position = jnp.sum(rows_ref[...].T, axis=0, keepdims=True)
    for g in range(cfg.groups):
        hot = jnp.where(group == g, 1.0, 0.0).astype(F32)
        small[8 + g : 9 + g, :tokens] = position * hot
    poll()

    saves = [None, None]

    def encoder_tile(r):
        at = slice(r * TILE, (r + 1) * TILE)
        slot = r % 2
        if saves[slot] is not None:
            saves[slot].wait()
        stage = scr.stage.at[slot]
        stage[...] = (nn(kc[at], wk[...]) + nn(vc[at], wv[...])).astype(BF)
        saves[slot] = fetch(stage, outs.encoder_grad.at[pl.ds(r * TILE, TILE)])

    for r in range(tiles // 2):
        encoder_tile(r)
        poll()
    kv_done(1)
    poll()
    s5.three()
    for r in range(tiles // 2, tiles):
        encoder_tile(r)
        poll()
    s5.four()
    dv, gain_grad = norm_back(scr.x[...].astype(F32), gain_self, s5.out[...].astype(F32))
    scr.og[...] = (g1[...] + dv).astype(BF)
    token_saves.append(fetch(scr.og, outs.decoder_grad))
    small[0:1, :width] = gain_grad
    for copy in saves + token_saves:
        copy.wait()
    if summing:
        little = SmallSum(sems, place, scr.small)
        little.s0()
        poll()
        little.s1()
        poll()
        little.s2()
        poll()
        little.s3()
        poll()
        little.s4()
        outs.small_sum[...] = little.bufs[6][...]
        poll()
        for chunk in chunks:
            chunk.finish()
    else:
        for copy in [fetch(src, dst) for src, dst in zip(scr.grads, outs.grads)]:
            copy.wait()
        outs.small_sum[...] = small[...]
    for gather in gathers + [get_query]:
        gather.end()


def finish_kernel(own, buckets, heads, groups, ins, outs, scr):
    used = [0]

    def copy(src, dst):
        made = pltpu.make_async_copy(src, dst, scr.sems.at[used[0]])
        used[0] += 1
        made.start()
        return made

    loads = [copy(src, dst) for src, dst in zip(ins.grads, scr.low)]
    moves = [copy(src, dst) for src, dst in zip(ins.kept, scr.kept)]
    keeps = []
    for k in range(3):
        outs.gains[k][...] = ins.little[k : k + 1].reshape(outs.gains[k].shape)
    for h in range(heads):
        outs.position[h] = ins.little[8 : 8 + groups, h * buckets : (h + 1) * buckets]
    for k in range(3):
        loads[k].wait()
        scr.wide[k][...] = scr.low[k][...].astype(F32)
        keeps.append(copy(scr.wide[k], outs.wide[k]))
    loads[3].wait()
    for k, out in enumerate(outs.pieces):
        at = slice(k * own, (k + 1) * own)
        scr.wide[3][at] = scr.low[3][at].astype(F32)
        keeps.append(copy(scr.wide[3].at[at], out))
    for k, move in enumerate(moves):
        move.wait()
        keeps.append(copy(scr.kept[k], outs.kept[k]))
    for made in keeps:
        made.wait()


def shards(
    mesh_shape,
    decoder_in,
    encoder_out,
    out_grad,
    group_ids,
    target_mask,
    bucket_ids,
    gain_self,
    gain_cross,
    gain_ffn,
    query_self,
    key_self,
    value_self,
    output_self,
    query_cross,
    key_cross,
    value_cross,
    output_cross,
    gate_weight,
    up_weight,
    down_weight,
    position_bias,
):
    dp_size, tensor_size = mesh_shape
    query_count, tokens, width = decoder_in.shape
    assert query_count == 1 and tensor_size == 4 and dp_size % 2 == 0
    heads = query_self.shape[1] // DH
    own, all_heads = heads * DH, heads * tensor_size
    groups, buckets, _ = position_bias.shape
    rows, units = encoder_out.shape[1], gate_weight.shape[1]
    summing = dp_size == 8

    def vmem(*shape, kind=BF):
        return pltpu.VMEM(shape, kind)

    def shape_of(*shape, kind=BF):
        return jax.ShapeDtypeStruct(shape, kind)

    inputs = dict(
        x=(decoder_in[0], ANY),
        out_grad=(out_grad[0], ANY),
        encoder=(encoder_out[0], ANY),
        group=(group_ids, SMEM),
        mask=(target_mask, VMEM),
        bucket=(bucket_ids, ANY),
        gains=[(gain_self, VMEM), (gain_cross, VMEM), (gain_ffn, VMEM)],
        wq_self=(query_self.T, ANY),
        wk_self=(key_self.T, ANY),
        wv_self=(value_self.T, ANY),
        wo_self=(output_self, ANY),
        wq_cross=(query_cross.T, ANY),
        wk_cross=(key_cross.T, ANY),
        wv_cross=(value_cross.T, ANY),
        wo_cross=(output_cross, ANY),
        gate_w=(gate_weight, ANY),
        up_w=(up_weight, ANY),
        down_w=(down_weight, ANY),
        table=(jnp.transpose(position_bias, (2, 0, 1)), SMEM),
    )
    grad_shapes = [(units, width), (width, units), (width, units), (8 * own, width)]
    outputs = dict(
        block_out=(shape_of(tokens, width), ANY),
        decoder_grad=(shape_of(tokens, width), ANY),
        encoder_grad=(shape_of(rows, width), ANY),
        grads=[(shape_of(*shape), ANY) for shape in grad_shapes],
        small_sum=(shape_of(16, width, kind=F32), VMEM),
    )
    plan = chunk_plan(own, width, units)
    all_own = all_heads * DH

    def sum_bufs(count, lanes):
        return [vmem(size, lanes) for size in (count, count // 2, count // 2, count // 2, count)]

    def chunk_bufs(in_x, source, size):
        lanes = grad_shapes[source][1]
        full = () if in_x else (0, 4)
        return [vmem(size if k in full else size // 2, lanes) for k in range(5)]

    token_low, token_wide = vmem(tokens, width), vmem(tokens, width, kind=F32)
    stats, kv_block = vmem(16, tokens, kind=F32), vmem(2, own, width)
    halves = vmem(all_own // 2, tokens)
    scratch = dict(
        x=token_low, og=token_low, out_stage=token_low, wqkv=[vmem(own, width)] * 3, wo_self=vmem(own, width), wq_own=vmem(own, width),
        q_own=vmem(own, tokens), q_t=vmem(all_own, tokens),
        enc=vmem(rows, width), down=vmem(units, width), gate_w=vmem(width, units), up_w=vmem(width, units),
        self_in=token_low, cross_in=token_low, ffn_in=token_low, g1_low=token_low, g2_low=token_low,
        x2=token_wide, x3=token_wide, g1=token_wide, g2=token_wide,
        qkv=vmem(3 * own, tokens), d_qkv=vmem(3 * own, tokens), att_self=vmem(own, tokens),
        bucket=vmem(tokens, tokens, kind=jnp.int32), bucket_rows=vmem(128, tokens, kind=F32),
        p_self=vmem(heads, tokens, tokens, kind=F32), ds_self=vmem(heads, tokens, tokens, kind=F32),
        wk=vmem(all_own, width), wq=vmem(all_own, width), wv=vmem(all_own, width), wo=vmem(all_own, width),
        bq=vmem(all_own, 2 * tokens), bw=vmem(all_own, 2 * tokens),
        kc=vmem(rows, all_own), vc=vmem(rows, all_own),
        e=vmem(rows, all_heads * tokens), s=vmem(rows, 2 * tokens, kind=F32),
        mix=vmem(all_own, tokens), att=vmem(all_own, tokens), stat=stats, top=stats, lse=stats,
        mix_bufs=[halves] * 3 + [vmem(8, tokens, kind=F32)] * 3,
        delta=vmem(8, 2 * tokens, kind=F32), inverse=vmem(8, 2 * tokens, kind=F32),
        d_hidden=vmem(tokens, units, kind=F32), hidden=vmem(tokens, units),
        d_gate=vmem(tokens, units), d_up=vmem(tokens, units),
        s1=sum_bufs(tokens, width), s3=sum_bufs(tokens, width), so=sum_bufs(tokens, width),
        s4=sum_bufs(all_own, tokens), s5=sum_bufs(tokens, width),
        far_parts=[vmem(2 * own, width)] * 2, near_parts=[vmem(2 * own, width)] * 2,
        kv_near=kv_block, kv_home=kv_block, kv_half=kv_block, kv_far=kv_block,
        stage=vmem(2, TILE, width),
        grads=[vmem(*shape) for shape in grad_shapes],
        small=[vmem(16, width, kind=F32)] * (7 if summing else 1),
        chunks=[chunk_bufs(in_x, source, size) for in_x, source, _, size in plan] if summing else [],
        sems=pltpu.SemaphoreType.DMA((320,)),
    )
    pair = lambda entry: isinstance(entry, tuple)
    first = lambda tree: jax.tree.map(lambda entry: entry[0], tree, is_leaf=pair)
    second = lambda tree: jax.tree.map(lambda entry: entry[1], tree, is_leaf=pair)
    flat = jax.tree.leaves
    trees = [jax.tree.structure(first(inputs)), jax.tree.structure(first(outputs)), jax.tree.structure(scratch)]
    cfg = SimpleNamespace(
        trees=trees, heads=heads, all_heads=all_heads, width=width, tokens=tokens, rows=rows,
        buckets=buckets, groups=groups, summing=summing, chunks=plan, schedule=SCHEDULE,
    )
    result = pl.pallas_call(
        functools.partial(block_kernel, cfg),
        out_shape=flat(first(outputs)),
        in_specs=flat(second(inputs)),
        out_specs=flat(second(outputs)),
        scratch_shapes=flat(scratch),
        compiler_params=pltpu.CompilerParams(collective_id=0, has_side_effects=True, vmem_limit_bytes=63 << 20),
        name="block",
    )(*flat(first(inputs)))
    got = SimpleNamespace(**jax.tree.unflatten(trees[1], result))
    kept = [got.block_out, got.decoder_grad, got.encoder_grad]
    if summing:
        inputs = dict(grads=got.grads, kept=kept, little=got.small_sum)
        outputs = dict(
            kept=[shape_of(*value.shape) for value in kept],
            gains=[shape_of(width, kind=F32)] * 3,
            position=shape_of(heads, groups, buckets, kind=F32),
            wide=[shape_of(*shape, kind=F32) for shape in grad_shapes[:3]],
            pieces=[shape_of(own, width, kind=F32)] * 8,
        )
        scratch = dict(
            low=[vmem(*shape) for shape in grad_shapes],
            kept=[vmem(*value.shape) for value in kept],
            wide=[vmem(*shape, kind=F32) for shape in grad_shapes],
            sems=pltpu.SemaphoreType.DMA((32,)),
        )
        trees = [jax.tree.structure(inputs), jax.tree.structure(outputs), jax.tree.structure(scratch)]

        def finish(*refs):
            groups_of, at = [], 0
            for tree in trees:
                groups_of.append(SimpleNamespace(**jax.tree.unflatten(tree, refs[at : at + tree.num_leaves])))
                at += tree.num_leaves
            finish_kernel(own, buckets, heads, groups, *groups_of)

        specs_in = dict(grads=[ANY] * 4, kept=[ANY] * 3, little=VMEM)
        specs_out = dict(kept=[ANY] * 3, gains=[VMEM] * 3, position=VMEM, wide=[ANY] * 3, pieces=[ANY] * 8)
        result = pl.pallas_call(
            finish,
            out_shape=flat(outputs),
            in_specs=flat(specs_in),
            out_specs=flat(specs_out),
            scratch_shapes=flat(scratch),
            compiler_params=pltpu.CompilerParams(vmem_limit_bytes=63 << 20),
            name="finish",
        )(*flat(inputs))
        done = SimpleNamespace(**jax.tree.unflatten(trees[1], result))
        kept, gain_grads, position = done.kept, done.gains, jnp.transpose(done.position, (1, 2, 0))
        wide, pieces = done.wide, done.pieces
    else:
        sums, little = lax.psum(([value.astype(F32) for value in got.grads], got.small_sum), "dp")
        wide = sums[:3]
        pieces = [sums[3][k * own : (k + 1) * own] for k in range(8)]
        gain_grads = [little[k] for k in range(3)]
        position = little[8 : 8 + groups, : heads * buckets].reshape(groups, heads, buckets)
        position = jnp.transpose(position, (0, 2, 1))
    down, gate, up = wide
    oc, qc, os, qs, ks, vs, kc, vc = pieces
    return (
        *[value[None] for value in kept], *gain_grads,
        qs.T, ks.T, vs.T, os, qc.T, kc.T, vc.T, oc, gate, up, down, position,
    )


def solution(mesh):
    rows = P("dp", None, None)
    encoder = P("dp", "tensor", None)
    columns, lines, whole = P(None, "tensor"), P("tensor", None), P()
    head_table = P(None, None, "tensor")
    weights = (columns, columns, columns, lines, columns, columns, columns, lines, columns, columns, lines, head_table)
    return jax.shard_map(
        functools.partial(shards, (mesh.shape["dp"], mesh.shape["tensor"])),
        mesh=mesh,
        in_specs=(rows, encoder, rows, P("dp"), P("dp", None), whole, whole, whole, whole) + weights,
        out_specs=(rows, rows, encoder, whole, whole, whole) + weights,
        check_vma=False,
    )
```

```python
import functools
from types import SimpleNamespace

import jax
import jax.numpy as jnp
from jax import lax
from jax.experimental import pallas as pl
from jax.experimental.pallas import tpu as pltpu
from jax.sharding import PartitionSpec as P

DH = 64
EPS = 1e-06
NEG = -1000000000.0
TILE = 256
MESH = pl.DeviceIdType.MESH
BF = jnp.bfloat16
F32 = jnp.float32
VMEM = pl.BlockSpec(memory_space=pltpu.VMEM)
SMEM = pl.BlockSpec(memory_space=pltpu.SMEM)
ANY = pl.BlockSpec(memory_space=pl.ANY)
GELU_SCALE = 0.7978845608028654
GELU_CUBIC = 0.044715


IN_X = (True, True, True, False, True, True, False, True, True)
SCHEDULE = (
    ((9, 0),),
    (),
    (),
    ((2, 0), (3, 0), (1, 0),),
    (),
    ((9, 1),),
    (),
    (),
    ((3, 1), (4, 0),),
    (),
    ((2, 1), (9, 2),),
    ((0, 0), (1, 1),),
    ((3, 2), (2, 2),),
    (),
    ((9, 3), (4, 1),),
    ((1, 2), (2, 3),),
    ((0, 1), (3, 3),),
    ((7, 0),),
    ((9, 4), (5, 0), (1, 3), (4, 2), (6, 0),),
    (),
    ((0, 2), (10, 0),),
    (),
    (),
    ((6, 1), (2, 4), (3, 4), (5, 1),),
    ((10, 1), (4, 3),),
    (),
    ((7, 1), (8, 0), (0, 3), (6, 2), (1, 4), (4, 4),),
    ((10, 2), (5, 2), (7, 2), (8, 1), (0, 4),),
    (),
    (),
    ((5, 3),),
    ((10, 3), (5, 4), (8, 2), (7, 3), (7, 4), (9, 5), (8, 3), (6, 3), (10, 4), (10, 5),),
    ((8, 4), (1, 5), (6, 4),),
    (),
    ((3, 5), (0, 5), (7, 5), (8, 5), (5, 5), (6, 5), (4, 5), (2, 5),),
)


def nn(left, right):
    return lax.dot_general(left, right, (((1,), (0,)), ((), ())), preferred_element_type=F32)


def nt(left, right):
    return lax.dot_general(left, right, (((1,), (1,)), ((), ())), preferred_element_type=F32)


def tn(left, right):
    return lax.dot_general(left, right, (((0,), (0,)), ((), ())), preferred_element_type=F32)


def span(start, size, step=None):
    return pl.ds(pl.multiple_of(start, step or size), size)


class Sems:
    def __init__(self, ref):
        self.ref, self.used = ref, 0

    def take(self):
        self.used += 1
        assert self.used <= self.ref.shape[0]
        return self.ref.at[self.used - 1]


class Wire:
    def __init__(self, sems, src, dst, device):
        self.copy = pltpu.make_async_remote_copy(
            src_ref=src, dst_ref=dst, send_sem=sems.take(), recv_sem=sems.take(), device_id=device, device_id_type=MESH
        )

    def start(self):
        self.copy.start()

    def sent(self):
        self.copy.wait_send()

    def came(self):
        self.copy.wait_recv()

    def wait(self):
        self.copy.wait()


class TensorSum:
    def __init__(self, sems, place, src, near, half, far, out):
        self.src, self.near, self.half, self.far, self.out = src, near, half, far, out
        size = src.shape[0] // 2
        self.mine = span(place.core * size, size)
        other = span((1 - place.core) * size, size)
        self.first = Wire(sems, src.at[other], near, place.mate)
        self.second = Wire(sems, half, far, place.across)
        self.third = Wire(sems, out.at[self.mine], out.at[self.mine], place.mate)

    def one(self):
        self.first.start()

    def two(self):
        self.first.wait()
        self.half[...] = (self.src[self.mine].astype(F32) + self.near[...].astype(F32)).astype(BF)
        self.second.start()

    def three(self):
        self.second.wait()
        self.out[self.mine] = (self.half[...].astype(F32) + self.far[...].astype(F32)).astype(BF)
        self.third.start()

    def four(self):
        self.third.wait()


class TensorMix:
    def __init__(self, sems, place, mix, stat, bufs, out, total):
        self.place, self.mix, self.stat, self.out, self.total = place, mix, stat, out, total
        near, half, far, near_stat, half_stat, far_stat = bufs
        self.bufs = bufs
        size, core = mix.shape[0] // 2, place.core
        self.size = size
        self.mine, other = span(core * size, size), span((1 - core) * size, size)
        self.mine_stat, other_stat = span(core * 8, 8), span((1 - core) * 8, 8)
        self.first = [
            Wire(sems, mix.at[other], near, place.mate),
            Wire(sems, stat.at[other_stat], near_stat, place.mate),
        ]
        self.second = [Wire(sems, half, far, place.across), Wire(sems, half_stat, far_stat, place.across)]
        self.third = [
            Wire(sems, out.at[self.mine], out.at[self.mine], place.mate),
            Wire(sems, total.at[self.mine_stat], total.at[self.mine_stat], place.mate),
        ]

    def join(self, ours, theirs, ours_stat, theirs_stat, flip, store):
        low_stat = jnp.where(flip, theirs_stat, ours_stat)
        high_stat = jnp.where(flip, ours_stat, theirs_stat)
        top = jnp.maximum(low_stat, high_stat)
        total = top + jnp.log(jnp.exp(low_stat - top) + jnp.exp(high_stat - top))
        low_share, high_share = jnp.exp(low_stat - total), jnp.exp(high_stat - total)
        for h in range(self.size // DH):
            rows = slice(h * DH, (h + 1) * DH)
            a, b = ours(rows), theirs(rows)
            low, high = jnp.where(flip, b, a), jnp.where(flip, a, b)
            store(rows, (low * low_share[h : h + 1] + high * high_share[h : h + 1]).astype(BF))
        return total

    def one(self):
        for wire in self.first:
            wire.start()

    def two(self):
        near, half, far, near_stat, half_stat, far_stat = self.bufs
        core, size = self.place.core, self.size
        for wire in self.first:
            wire.wait()

        def ours(rows):
            return self.mix[span(core * size + rows.start, DH)].astype(F32)

        def store(rows, value):
            half[rows] = value

        half_stat[...] = self.join(
            ours, lambda rows: near[rows].astype(F32), self.stat[self.mine_stat], near_stat[...], core == 1, store
        )
        for wire in self.second:
            wire.start()

    def three(self):
        near, half, far, near_stat, half_stat, far_stat = self.bufs
        core, size = self.place.core, self.size
        for wire in self.second:
            wire.wait()

        def store(rows, value):
            self.out[span(core * size + rows.start, DH)] = value

        self.total[self.mine_stat] = self.join(
            lambda rows: half[rows].astype(F32),
            lambda rows: far[rows].astype(F32),
            half_stat[...],
            far_stat[...],
            self.place.side == 1,
            store,
        )
        for wire in self.third:
            wire.start()

    def four(self):
        for wire in self.third:
            wire.wait()


class WeightGather:
    def __init__(self, sems, place, own, whole, local):
        rows = own.shape[0]
        half = rows // 2
        me, core, side, x = place.me, place.core, place.side, place.x
        there = (1 - side) * 2 + core
        self.own, self.whole = own, whole
        mine = span(me * rows, rows)
        direct = span(there * rows + x * half, half)
        relayed = span(there * rows + (1 - x) * half, half)
        self.across = Wire(sems, own.at[span(x * half, half)], whole.at[span(me * rows + x * half, half)], place.across)
        self.mate = Wire(sems, own, whole.at[mine], place.mate)
        self.side = Wire(sems, whole.at[direct], whole.at[direct], place.beside)
        self.direct = Wire(sems, whole.at[direct], whole.at[direct], place.mate)
        self.relayed = Wire(sems, whole.at[relayed], whole.at[relayed], place.mate)
        self.keep = pltpu.make_async_copy(own, whole.at[mine], local)

    def start(self):
        self.across.start()
        self.mate.start()
        self.keep.start()

    def one(self):
        self.across.came()
        self.side.start()
        self.direct.start()

    def two(self):
        self.side.came()
        self.relayed.start()

    def three(self):
        self.mate.came()
        self.keep.wait()
        self.direct.came()
        self.relayed.came()

    def end(self):
        for wire in (self.across, self.mate, self.side, self.direct, self.relayed):
            wire.sent()


class QueryGather:
    def __init__(self, sems, place, own, whole):
        rows = own.shape[0]
        there = (1 - place.side) * 2 + place.core
        self.own, self.whole, self.mine = own, whole, span(place.me * rows, rows)
        self.across = Wire(sems, own, whole.at[self.mine], place.across)
        self.mate = Wire(sems, own, whole.at[self.mine], place.mate)
        theirs = whole.at[span(there * rows, rows)]
        self.onward = Wire(sems, theirs, theirs, place.mate)

    def one(self):
        self.across.start()
        self.mate.start()
        self.whole[self.mine] = self.own[...]

    def two(self):
        self.across.came()
        self.onward.start()

    def three(self):
        self.mate.came()
        self.onward.came()

    def end(self):
        for wire in (self.across, self.mate, self.onward):
            wire.sent()


class ChunkX:
    def __init__(self, sems, place, g, out, bufs):
        self.place = place
        near, inn, mid, tot, fin = self.bufs = bufs
        half = g.shape[0] // 2
        x = place.x
        self.g, self.mine = g, span(x * half, half)
        other = span((1 - x) * half, half)
        self.rs = Wire(sems, g.at[other], near, place.beside)
        self.out = Wire(sems, g.at[self.mine], inn, place.pair)
        self.middle = Wire(sems, g.at[self.mine], mid, place.middle)
        self.back = Wire(sems, tot, tot, place.pair)
        self.ag = Wire(sems, tot, fin, place.beside)
        self.save = [
            pltpu.make_async_copy(tot, out.at[self.mine], sems.take()),
            pltpu.make_async_copy(fin, out.at[other], sems.take()),
        ]

    def s0(self):
        self.rs.start()

    def s1(self):
        self.rs.wait()
        self.g[self.mine] = self.g[self.mine] + self.bufs[0][...]

        @pl.when(self.place.end)
        def _():
            self.out.start()

    def s2(self):
        @pl.when(self.place.inner)
        def _():
            self.out.came()
            self.g[self.mine] = self.g[self.mine] + self.bufs[1][...]
            self.middle.start()

    def s3(self):
        @pl.when(self.place.inner)
        def _():
            self.middle.wait()
            self.bufs[3][...] = self.g[self.mine] + self.bufs[2][...]
            self.back.start()
            self.ag.start()
            self.save[0].start()

    def s4(self):
        @pl.when(self.place.end)
        def _():
            self.back.came()
            self.ag.start()
            self.save[0].start()

    def s5(self):
        self.ag.came()
        self.save[1].start()

    def finish(self):
        @pl.when(self.place.end)
        def _():
            self.out.sent()

        @pl.when(self.place.inner)
        def _():
            self.back.sent()

        self.ag.sent()
        for copy in self.save:
            copy.wait()


class ChunkZ:
    def __init__(self, sems, place, g, out, bufs):
        self.place = place
        inn, mid, r, xr, tot = self.bufs = bufs
        half = g.shape[0] // 2
        at = place.high
        self.g, self.mine = g, span(at * half, half)
        self.other = span((1 - at) * half, half)
        self.out = Wire(sems, g, inn, place.pair)
        self.rs = Wire(sems, g.at[self.other], mid, place.middle)
        self.x = Wire(sems, r, xr, place.beside)
        self.ag = Wire(sems, tot.at[self.mine], tot.at[self.mine], place.middle)
        self.back = [
            Wire(sems, tot.at[self.mine], tot.at[self.mine], place.pair),
            Wire(sems, tot.at[self.other], tot.at[self.other], place.pair),
        ]
        self.save = pltpu.make_async_copy(tot, out, sems.take())

    def s0(self):
        @pl.when(self.place.end)
        def _():
            self.out.start()

    def s1(self):
        @pl.when(self.place.inner)
        def _():
            self.out.came()
            self.g[...] = self.g[...] + self.bufs[0][...]
            self.rs.start()

    def s2(self):
        @pl.when(self.place.inner)
        def _():
            self.rs.wait()
            self.bufs[2][...] = self.g[self.mine] + self.bufs[1][...]
            self.x.start()

    def s3(self):
        @pl.when(self.place.inner)
        def _():
            self.x.wait()
            self.bufs[4][self.mine] = self.bufs[2][...] + self.bufs[3][...]
            self.ag.start()
            self.back[0].start()

    def s4(self):
        @pl.when(self.place.inner)
        def _():
            self.ag.came()
            self.back[1].start()
            self.save.start()

    def s5(self):
        @pl.when(self.place.end)
        def _():
            for wire in self.back:
                wire.came()
            self.save.start()

    def finish(self):
        @pl.when(self.place.end)
        def _():
            self.out.sent()

        @pl.when(self.place.inner)
        def _():
            self.ag.sent()
            for wire in self.back:
                wire.sent()

        self.save.wait()


class ChunkG:
    def __init__(self, sems, place, blocks, use=None):
        def wires(query, device):
            return [Wire(sems, block(query), block(query), device) for block in blocks]

        self.place, self.use = place, use
        first, second = place.far
        self.pair = wires(place.query, place.pair)
        self.x0 = wires(place.query, place.beside)
        self.x1 = wires(place.pair[0], place.beside)
        self.middle = wires(place.query, place.middle) + wires(place.pair[0], place.middle)
        self.back = wires(first, place.pair) + wires(second, place.pair)
        self.x2 = wires(first, place.beside) + wires(second, place.beside)

    def s0(self):
        for wire in self.pair + self.x0:
            wire.start()

    def s1(self):
        for wire in self.pair:
            wire.came()

        @pl.when(self.place.inner)
        def _():
            for wire in self.middle:
                wire.start()

        for wire in self.x1:
            wire.start()

    def s2(self):
        @pl.when(self.place.inner)
        def _():
            for wire in self.middle:
                wire.came()
            for wire in self.back + self.x2:
                wire.start()

    def s3(self):
        @pl.when(self.place.end)
        def _():
            for wire in self.back:
                wire.came()
            for wire in self.x2:
                wire.start()

    def s4(self):
        for wire in self.x0 + self.x1 + self.x2:
            wire.came()

    def s5(self):
        self.saves = self.use()

    def finish(self):
        for wire in self.pair + self.x0 + self.x1 + self.x2:
            wire.sent()

        @pl.when(self.place.inner)
        def _():
            for wire in self.middle + self.back:
                wire.sent()

        for copy in self.saves:
            copy.wait()


class SmallSum:
    def __init__(self, sems, place, bufs):
        self.place = place
        own, near, sum1, inn, sum2, mid, tot = self.bufs = bufs
        self.x = Wire(sems, own, near, place.beside)
        self.out = Wire(sems, sum1, inn, place.pair)
        self.middle = Wire(sems, sum2, mid, place.middle)
        self.back = Wire(sems, tot, tot, place.pair)

    def s0(self):
        self.x.start()

    def s1(self):
        own, near, sum1, inn, sum2, mid, tot = self.bufs
        self.x.wait()
        sum1[...] = own[...] + near[...]

        @pl.when(self.place.end)
        def _():
            self.out.start()

    def s2(self):
        own, near, sum1, inn, sum2, mid, tot = self.bufs

        @pl.when(self.place.inner)
        def _():
            self.out.came()
            sum2[...] = sum1[...] + inn[...]
            self.middle.start()

    def s3(self):
        own, near, sum1, inn, sum2, mid, tot = self.bufs

        @pl.when(self.place.inner)
        def _():
            self.middle.wait()
            tot[...] = sum2[...] + mid[...]
            self.back.start()
            self.back.sent()

    def s4(self):
        @pl.when(self.place.end)
        def _():
            self.out.sent()
            self.back.came()


def rms_scale(values):
    return lax.rsqrt(jnp.mean(values * values, axis=-1, keepdims=True) + EPS)


def norm_back(values, gain, dy):
    scale = rms_scale(values)
    normal = values * scale
    gain_grad = jnp.sum(dy * normal, axis=0, keepdims=True)
    pulled = dy * gain
    mean = jnp.mean(pulled * normal, axis=-1, keepdims=True)
    return scale * (pulled - normal * mean), gain_grad


def fold(values, op):
    rows, width = values.shape
    return op(values.reshape(rows // 8, 8, width), axis=0)


def chunk_plan(own, width, units):
    plan = [(a, k * (width // 2), width // 2) for a in (1, 2) for k in range(2)]
    plan += [(3, k * own, own) for k in (0, 1, 2, 6, 7)]
    return [(in_x, *block) for in_x, block in zip(IN_X, plan)]


def block_kernel(cfg, *refs):
    groups, at = [], 0
    for tree in cfg.trees:
        groups.append(SimpleNamespace(**jax.tree.unflatten(tree, refs[at : at + tree.num_leaves])))
        at += tree.num_leaves
    ins, outs, scr = groups
    heads, all_heads, width, tokens, rows = cfg.heads, cfg.all_heads, cfg.width, cfg.tokens, cfg.rows
    own, pairs, tiles = heads * DH, all_heads // 2, rows // TILE
    summing = cfg.summing
    sems = Sems(scr.sems)
    dp, me = lax.axis_index("dp"), lax.axis_index("tensor")
    core, side = lax.rem(me, 2), me // 2
    x, z = lax.rem(dp, 2), dp // 2
    place = SimpleNamespace(
        me=me,
        core=core,
        side=side,
        x=x,
        mate=(dp, side * 2 + 1 - core),
        across=(dp, (1 - side) * 2 + core),
        beside=(dp + 1 - 2 * x, me),
    )
    barrier = pltpu.get_barrier_semaphore()
    for friend in (place.mate, place.across, place.beside):
        pl.semaphore_signal(barrier, inc=1, device_id=friend, device_id_type=MESH)
    if summing:
        inner = jnp.logical_or(z == 1, z == 2)
        place.inner, place.end = inner, jnp.logical_not(inner)
        place.high = z // 2
        place.pair = ((z + 1 - 2 * lax.rem(z, 2)) * 2 + x, me)
        place.middle = ((3 - z) * 2 + x, me)
        place.query = dp
        place.far = ((2 - z // 2) * 2 + x, 3 * (1 - z // 2) * 2 + x)
        pl.semaphore_signal(barrier, inc=1, device_id=place.pair, device_id_type=MESH)

        @pl.when(inner)
        def _():
            pl.semaphore_signal(barrier, inc=1, device_id=place.middle, device_id_type=MESH)

    def fetch(src, dst):
        copy = pltpu.make_async_copy(src, dst, sems.take())
        copy.start()
        return copy

    enc, down, gate_w, up_w = scr.enc, scr.down, scr.gate_w, scr.up_w
    first_loads = [fetch(ins.x, scr.x)] + [fetch(src, dst) for src, dst in zip(ins.gains, scr.gains)]
    self_weights = scr.wqkv
    for src, dst in zip((ins.wq_self, ins.wk_self, ins.wv_self), self_weights):
        first_loads.append(fetch(src, dst))
    load_bucket, load_out = fetch(ins.bucket, scr.bucket), fetch(ins.wo_self, scr.wo_self)
    load_small = [fetch(ins.mask, scr.mask), fetch(ins.group, scr.group), fetch(ins.table, scr.table)]
    load_query = fetch(ins.wq_cross, scr.wq_own)
    load_enc = fetch(ins.encoder, enc)
    load_ffn = [fetch(ins.out_grad, scr.og), fetch(ins.down_w, down), fetch(ins.gate_w, gate_w), fetch(ins.up_w, up_w)]

    for load in first_loads:
        load.wait()
    gain_self, gain_cross, gain_ffn = (gain[...].reshape(1, width) for gain in scr.gains)
    xv = scr.x[...].astype(F32)
    self_in = scr.self_in
    self_in[...] = (xv * rms_scale(xv) * gain_self).astype(BF)
    qkv = scr.qkv
    for k, weight in enumerate(self_weights):
        qkv[k * own : (k + 1) * own] = nt(weight[...], self_in[...]).astype(BF)
    if summing:
        pl.semaphore_wait(barrier, 4 + inner.astype(jnp.int32))
    else:
        pl.semaphore_wait(barrier, 3)
    wk, wq, wv, wo = scr.wk, scr.wq, scr.wv, scr.wo
    get_k, get_q, get_v, get_o = gathers = [
        WeightGather(sems, place, part, whole, sems.take())
        for part, whole in ((ins.wk_cross, wk), (ins.wq_cross, wq), (ins.wv_cross, wv), (ins.wo_cross, wo))
    ]
    get_k.start()
    if summing:
        lanes_half = span(core * (width // 2), width // 2, 2 * DH)
        og_all, self_all, hidden_all, d_qkv_all = scr.gathered

        def rows_of(query):
            return span(query * tokens, tokens)

        load_ffn[0].wait()
        og_all[rows_of(dp), lanes_half] = scr.og[:, lanes_half]
        self_all[rows_of(dp), lanes_half] = self_in[:, lanes_half]
        early = ChunkG(
            sems,
            place,
            [lambda query: og_all.at[rows_of(query), lanes_half], lambda query: self_all.at[rows_of(query), lanes_half]],
            lambda: [],
        )
        shares = [Wire(sems, ref.at[:, lanes_half], ref.at[:, lanes_half], place.mate) for ref in (og_all, self_all)]
        early.s0()
    load_bucket.wait()
    for load in load_small:
        load.wait()
    scr.bucket[...] = scr.bucket[...].T
    bucket = scr.bucket
    keep = jnp.broadcast_to(scr.mask[...].astype(F32), (tokens, tokens)).T
    j_at = lax.broadcasted_iota(jnp.int32, (tokens, tokens), 0)
    i_at = lax.broadcasted_iota(jnp.int32, (tokens, tokens), 1)
    allowed = jnp.logical_or(jnp.logical_and(j_at <= i_at, keep == 1.0), j_at == i_at)
    group = scr.group[0]
    buckets = cfg.buckets
    for h in range(heads):
        scr.p_self[h] = jnp.full((tokens, tokens), NEG, F32)

    def spread(b, _):
        hit = jnp.logical_and(bucket[...] == b, allowed)
        for h in range(heads):
            scr.p_self[h] = jnp.where(hit, scr.table[h, group, b], scr.p_self[h])
        return 0

    lax.fori_loop(0, buckets, spread, 0)
    att_self = scr.att_self

    def attend(h):
        q = qkv[h * DH : (h + 1) * DH]
        k = qkv[own + h * DH : own + (h + 1) * DH]
        v = qkv[2 * own + h * DH : 2 * own + (h + 1) * DH]
        s = tn(k, q) + scr.p_self[h]
        e = jnp.exp(s - jnp.max(s, axis=0, keepdims=True))
        p = e / jnp.sum(e, axis=0, keepdims=True)
        scr.p_self[h] = p
        att_self[h * DH : (h + 1) * DH] = nn(v, p.astype(BF)).astype(BF)

    for h in range(heads):
        attend(h)

    def tensor_sum(bufs):
        return TensorSum(sems, place, *bufs)

    s1 = tensor_sum(scr.s1)
    load_out.wait()
    s1.src[...] = tn(att_self[...], scr.wo_self[...]).astype(BF)
    s1.one()
    s1.two()
    get_v.start()
    bq, bw = scr.bq, scr.bw
    for ref in (bq, bw, scr.stat, scr.top, scr.small[0], scr.bucket_rows):
        ref[...] = jnp.zeros(ref.shape, ref.dtype)
    get_k.one()
    load_enc.wait()
    if summing:
        early.s1()
    kc, vc, e_ref = scr.kc, scr.vc, scr.e

    def project(dst, weight):
        def body(r, _):
            at = span(r * TILE, TILE)
            dst[at] = nt(enc[at], weight[...]).astype(BF)
            return 0

        lax.fori_loop(0, tiles, body, 0)

    s1.three()
    s1.four()
    x2 = scr.x2
    x2[...] = scr.x[...].astype(F32) + s1.out[...].astype(F32)
    cross_in = scr.cross_in
    cross_in[...] = (x2[...] * rms_scale(x2[...]) * gain_cross).astype(BF)
    load_query.wait()
    scr.q_own[...] = nt(scr.wq_own[...], cross_in[...]).astype(BF)
    get_query = QueryGather(sems, place, scr.q_own, scr.q_t)
    get_query.one()
    get_o.start()
    get_q.start()
    get_k.two()
    get_v.one()
    get_k.three()
    project(kc, wk)
    get_query.two()
    get_query.three()
    for h in range(all_heads):
        at = slice(h * DH, (h + 1) * DH)
        bq[at, (h % 2) * tokens : (h % 2 + 1) * tokens] = scr.q_t[at]
    s_ref, mix, stat, top_ref = scr.s, scr.mix, scr.stat, scr.top
    per_half = pairs // 2

    def stat_row(p):
        return (p // per_half) * 8 + 2 * (p - (p // per_half) * per_half)

    def score_pair(p, _):
        head_at = span(p * 2 * DH, 2 * DH)
        score_at = span(p * 2 * tokens, 2 * tokens)
        weights = bq[head_at]
        top = None
        for r in range(tiles):
            at = slice(r * TILE, (r + 1) * TILE)
            s = nn(kc[at, head_at], weights)
            s_ref[at] = s
            part = fold(s, jnp.max)
            top = part if top is None else jnp.maximum(top, part)
        top = jnp.max(top, axis=0, keepdims=True)
        total = None
        for r in range(tiles):
            at = slice(r * TILE, (r + 1) * TILE)
            e = jnp.exp(s_ref[at] - top)
            part = fold(e, jnp.sum)
            total = part if total is None else total + part
            e_ref[at, score_at] = e.astype(BF)
        total = jnp.sum(total, axis=0, keepdims=True)
        scr.inverse[pl.ds(p, 1)] = 1.0 / total
        lse = top + jnp.log(total)
        row = stat_row(p)
        for k in range(2):
            lanes = slice(k * tokens, (k + 1) * tokens)
            stat[pl.ds(row + k, 1)] = lse[:, lanes]
            top_ref[pl.ds(row + k, 1)] = top[:, lanes]
        return 0

    def mix_pair(p, _):
        acc = tn(vc[:, span(p * 2 * DH, 2 * DH)], e_ref[:, span(p * 2 * tokens, 2 * tokens)])
        inverse = scr.inverse[pl.ds(p, 1)]
        for k in range(2):
            lanes = slice(k * tokens, (k + 1) * tokens)
            value = acc[k * DH : (k + 1) * DH, lanes] * inverse[:, lanes]
            mix[span(p * 2 * DH + k * DH, DH)] = value.astype(BF)
        return 0

    lax.fori_loop(0, pairs - 2, score_pair, 0)
    get_v.two()
    get_o.one()
    if summing:
        early.s2()
    lax.fori_loop(pairs - 2, pairs, score_pair, 0)
    get_v.three()
    att, lse = scr.att, scr.lse
    s2 = TensorMix(sems, place, mix, stat, scr.mix_bufs, att, lse)
    project(vc, wv)
    for half in (1 - core, core):
        lax.fori_loop(half * per_half, (half + 1) * per_half, mix_pair, 0)
        if half is not core:
            s2.one()
            get_q.one()
    s2.two()
    for load in load_ffn[1 if summing else 0 :]:
        load.wait()
    og = scr.og
    scr.d_hidden[...] = nt(og[...], down[...]).astype(BF).astype(F32)
    get_o.two()
    s2.three()
    get_o.three()
    s2.four()
    if summing:
        early.s3()
    x3 = scr.x3
    x3[...] = x2[...] + tn(att[...], wo[...])
    ffn_in = scr.ffn_in
    ffn_in[...] = (x3[...] * rms_scale(x3[...]) * gain_ffn).astype(BF)
    gate = nn(ffn_in[...], gate_w[...])
    up = nn(ffn_in[...], up_w[...])
    squared = gate * gate
    curve = jnp.tanh(GELU_SCALE * (gate + GELU_CUBIC * (squared * gate)))
    gelu = 0.5 * gate * (1.0 + curve)
    slope = 0.5 * (1.0 + curve) + 0.5 * gate * (1.0 - curve * curve) * (
        GELU_SCALE * (1.0 + 3.0 * GELU_CUBIC * squared)
    )
    d_hidden = scr.d_hidden[...]
    scr.hidden[...] = (gelu * up).astype(BF)
    scr.d_gate[...] = (d_hidden * up * slope).astype(BF)
    scr.d_up[...] = (d_hidden * gelu).astype(BF)

    g_down, g_gate, g_up, g_small = scr.grads
    chunks = []
    if summing:
        def use_hidden():
            g_down[...] = tn(hidden_all[...], og_all[...]).astype(BF)
            return [fetch(g_down, outs.grads[0])]

        def use_d_qkv():
            whole = jnp.concatenate([d_qkv_all[k] for k in range(cfg.queries)], axis=1)
            g_small[3 * own : 6 * own] = nn(whole, self_all[...]).astype(BF)
            at = pl.ds(3 * own, 3 * own)
            return [fetch(g_small.at[at], outs.grads[3].at[at])]

        for (in_x, source, start, size), bufs in zip(cfg.chunks, scr.chunks):
            rows_at = pl.ds(start, size)
            maker = ChunkX if in_x else ChunkZ
            chunks.append(maker(sems, place, scr.grads[source].at[rows_at], outs.grads[source].at[rows_at], bufs))
        chunks.append(ChunkG(sems, place, [lambda query: hidden_all.at[rows_of(query)]], use_hidden))
        chunks.append(ChunkG(sems, place, [lambda query: d_qkv_all.at[query]], use_d_qkv))
    schedule = iter(cfg.schedule)

    def poll():
        if summing:
            for n, k in next(schedule):
                chunk = chunks[n]
                (chunk.s0, chunk.s1, chunk.s2, chunk.s3, chunk.s4, chunk.s5)[k]()

    if summing:
        hidden_all[rows_of(dp)] = scr.hidden[...]
    else:
        g_down[...] = tn(scr.hidden[...], og[...]).astype(BF)
    poll()
    g_gate[...] = tn(ffn_in[...], scr.d_gate[...]).astype(BF)
    poll()
    g_up[...] = tn(ffn_in[...], scr.d_up[...]).astype(BF)
    poll()
    s3, so = tensor_sum(scr.s3), tensor_sum(scr.so)
    s3.src[...] = (nt(scr.d_gate[...], gate_w[...]) + nt(scr.d_up[...], up_w[...])).astype(BF)
    s3.one()
    so.src[...] = nn(scr.hidden[...], down[...]).astype(BF)
    s3.two()
    poll()
    get_q.two()
    poll()
    s3.three()
    so.one()
    s3.four()
    so.two()
    poll()
    g2, g2_low = scr.g2, scr.g2_low
    dv, gain_grad = norm_back(x3[...], gain_ffn, s3.out[...].astype(F32))
    g2[...] = og[...].astype(F32) + dv
    g2_low[...] = g2[...].astype(BF)
    small = scr.small[0]
    small[2:3, :width] = gain_grad
    g_small[0:own] = nn(att[span(me * own, own)], g2_low[...]).astype(BF)
    poll()
    d_att = nt(wo[...], g2_low[...])
    delta_ref = scr.delta
    for h in range(all_heads):
        at = slice(h * DH, (h + 1) * DH)
        p, k = divmod(h, 2)
        row = (p // per_half) * 8 + 2 * (p % per_half) + k
        share = jnp.exp(top_ref[row : row + 1] - lse[row : row + 1])
        low = (d_att[at] * share).astype(BF)
        bw[at, k * tokens : (k + 1) * tokens] = low
        delta_ref[p : p + 1, k * tokens : (k + 1) * tokens] = jnp.sum(
            low.astype(F32) * att[at].astype(F32), axis=0, keepdims=True
        )
    so.three()
    s4 = tensor_sum(scr.s4)

    def backward_pair(p, _):
        head_at = span(p * 2 * DH, 2 * DH)
        score_at = span(p * 2 * tokens, 2 * tokens)
        wq_block, wa_block = bq[head_at], bw[head_at]
        delta = delta_ref[pl.ds(p, 1)]
        acc = None
        for r in range(tiles):
            at = slice(r * TILE, (r + 1) * TILE)
            e = e_ref[at, score_at]
            grad = nn(vc[at, head_at], wa_block)
            ds = (e.astype(F32) * (grad - delta)).astype(BF)
            part = tn(kc[at, head_at], ds)
            acc = part if acc is None else acc + part
            kc[at, head_at] = nt(ds, wq_block).astype(BF)
            vc[at, head_at] = nt(e, wa_block).astype(BF)
        for k in range(2):
            value = acc[k * DH : (k + 1) * DH, k * tokens : (k + 1) * tokens]
            s4.src[span(p * 2 * DH + k * DH, DH)] = value.astype(BF)
        return 0

    far_at, near_at = (1 - side) * per_half, side * per_half
    far_parts, near_parts = scr.far_parts, scr.near_parts
    kv_near, kv_home, kv_half, kv_far = scr.kv_near, scr.kv_home, scr.kv_half, scr.kv_far
    to_mate, to_across, to_home = [], [], []
    mine, other = span(core * own, own), span((1 - core) * own, own)
    for a in range(2):
        to_mate.append(Wire(sems, far_parts[a].at[other], kv_near.at[a], place.mate))
        to_across.append(Wire(sems, kv_half.at[a], kv_far.at[a], place.across))
        to_home.append(Wire(sems, near_parts[a].at[other], kv_home.at[a], place.mate))

    def weight_part(dst, source, first):
        rows_of = source[:, span(first * 2 * DH, 2 * own, 2 * DH)]

        def body(t, _):
            lanes = span(t * TILE, TILE)
            dst[:, lanes] = tn(rows_of, enc[:, lanes]).astype(BF)
            return 0

        lax.fori_loop(0, width // TILE, body, 0)

    def pass_across(a):
        to_mate[a].wait()
        kv_half[a] = (far_parts[a][mine].astype(F32) + kv_near[a].astype(F32)).astype(BF)
        to_across[a].start()

    if summing:
        early.s4()
        early.s5()
        for wire in shares:
            wire.start()
    for p in range(per_half):
        poll()
        lax.fori_loop(far_at + p, far_at + p + 1, backward_pair, 0)
    poll()
    so.four()
    scr.out_stage[...] = (x3[...] + so.out[...].astype(F32)).astype(BF)
    token_saves = [fetch(scr.out_stage, outs.block_out)]
    if summing:
        for wire in shares:
            wire.came()
    weight_part(far_parts[0], kc, far_at)
    to_mate[0].start()
    weight_part(far_parts[1], vc, far_at)
    to_mate[1].start()
    pass_across(0)
    for p in range(per_half):
        poll()
        lax.fori_loop(near_at + p, near_at + p + 1, backward_pair, 0)
    s4.one()
    poll()
    weight_part(near_parts[0], kc, near_at)
    to_home[0].start()
    s4.two()
    pass_across(1)
    poll()
    weight_part(near_parts[1], vc, near_at)
    to_home[1].start()
    s4.three()
    poll()

    def kv_done(a):
        to_home[a].wait()
        to_across[a].wait()
        total = near_parts[a][mine].astype(F32) + kv_home[a].astype(F32) + kv_far[a].astype(F32)
        g_small[(6 + a) * own : (7 + a) * own] = total.astype(BF)

    kv_done(0)
    s4.four()
    poll()
    get_q.three()
    d_cross = tn(s4.out[...], wq[...])
    dv, gain_grad = norm_back(x2[...], gain_cross, d_cross)
    small[1:2, :width] = gain_grad
    g1, g1_low = scr.g1, scr.g1_low
    g1[...] = g2[...] + dv
    g1_low[...] = g1[...].astype(BF)
    g_small[own : 2 * own] = nn(s4.out[span(me * own, own)], cross_in[...]).astype(BF)
    g_small[2 * own : 3 * own] = nn(att_self[...], g1_low[...]).astype(BF)
    poll()
    d_att_self = nt(scr.wo_self[...], g1_low[...]).astype(BF)
    d_qkv = scr.d_qkv
    for h in range(heads):
        at = slice(h * DH, (h + 1) * DH)
        q = qkv[h * DH : (h + 1) * DH]
        k = qkv[own + h * DH : own + (h + 1) * DH]
        v = qkv[2 * own + h * DH : 2 * own + (h + 1) * DH]
        p = scr.p_self[h]
        grad = tn(v, d_att_self[at])
        ds = (p * (grad - jnp.sum(p * grad, axis=0, keepdims=True))).astype(BF)
        scr.ds_self[h] = ds.astype(F32)
        d_qkv[h * DH : (h + 1) * DH] = nn(k, ds).astype(BF)
        d_qkv[own + h * DH : own + (h + 1) * DH] = nt(q, ds).astype(BF)
        d_qkv[2 * own + h * DH : 2 * own + (h + 1) * DH] = nt(d_att_self[at], p.astype(BF)).astype(BF)
    poll()
    if summing:
        d_qkv_all[dp] = d_qkv[...]
    else:
        g_small[3 * own : 6 * own] = nn(d_qkv[...], self_in[...]).astype(BF)
    poll()
    s5 = tensor_sum(scr.s5)
    total = None
    for k, weight in enumerate(self_weights):
        part = tn(d_qkv[k * own : (k + 1) * own], weight[...])
        total = part if total is None else total + part
    s5.src[...] = total.astype(BF)
    s5.one()
    poll()
    rows_ref = scr.bucket_rows

    def count(b, _):
        hit = bucket[...] == b
        for h in range(heads):
            value = jnp.where(hit, scr.ds_self[h], 0.0)
            rows_ref[pl.ds(h * buckets + b, 1)] = jnp.sum(value, axis=0, keepdims=True)
        return 0

    s5.two()
    lax.fori_loop(0, buckets, count, 0)
    position = jnp.sum(rows_ref[...].T, axis=0, keepdims=True)
    for g in range(cfg.groups):
        hot = jnp.where(group == g, 1.0, 0.0).astype(F32)
        small[8 + g : 9 + g, :tokens] = position * hot
    poll()

    saves = [None, None]

    def encoder_tile(r):
        at = slice(r * TILE, (r + 1) * TILE)
        slot = r % 2
        if saves[slot] is not None:
            saves[slot].wait()
        stage = scr.stage.at[slot]
        stage[...] = (nn(kc[at], wk[...]) + nn(vc[at], wv[...])).astype(BF)
        saves[slot] = fetch(stage, outs.encoder_grad.at[pl.ds(r * TILE, TILE)])

    for r in range(tiles // 2):
        encoder_tile(r)
        poll()
    kv_done(1)
    poll()
    s5.three()
    for r in range(tiles // 2, tiles):
        encoder_tile(r)
        poll()
    s5.four()
    dv, gain_grad = norm_back(scr.x[...].astype(F32), gain_self, s5.out[...].astype(F32))
    scr.og[...] = (g1[...] + dv).astype(BF)
    token_saves.append(fetch(scr.og, outs.decoder_grad))
    small[0:1, :width] = gain_grad
    for copy in saves + token_saves:
        copy.wait()
    if summing:
        little = SmallSum(sems, place, scr.small)
        little.s0()
        poll()
        little.s1()
        poll()
        little.s2()
        poll()
        little.s3()
        poll()
        little.s4()
        last = fetch(little.bufs[6], outs.small_sum)
        poll()
        for chunk in chunks + [early]:
            chunk.finish()
        for wire in shares:
            wire.sent()
    else:
        for copy in [fetch(src, dst) for src, dst in zip(scr.grads, outs.grads)]:
            copy.wait()
        last = fetch(small, outs.small_sum)
    last.wait()
    for gather in gathers + [get_query]:
        gather.end()


def finish_kernel(own, buckets, heads, groups, ins, outs, scr):
    used = [0]

    def copy(src, dst):
        made = pltpu.make_async_copy(src, dst, scr.sems.at[used[0]])
        used[0] += 1
        made.start()
        return made

    loads = [copy(src, dst) for src, dst in zip(ins.grads, scr.low)]
    moves = [copy(src, dst) for src, dst in zip(ins.kept, scr.kept)]
    keeps = []
    for k in range(3):
        outs.gains[k][...] = ins.little[k : k + 1].reshape(outs.gains[k].shape)
    for h in range(heads):
        outs.position[h] = ins.little[8 : 8 + groups, h * buckets : (h + 1) * buckets]
    for k in range(3):
        loads[k].wait()
        scr.wide[k][...] = scr.low[k][...].astype(F32)
        keeps.append(copy(scr.wide[k], outs.wide[k]))
    loads[3].wait()
    for k, out in enumerate(outs.pieces):
        at = slice(k * own, (k + 1) * own)
        scr.wide[3][at] = scr.low[3][at].astype(F32)
        keeps.append(copy(scr.wide[3].at[at], out))
    for k, move in enumerate(moves):
        move.wait()
        keeps.append(copy(scr.kept[k], outs.kept[k]))
    for made in keeps:
        made.wait()


def shards(
    mesh_shape,
    decoder_in,
    encoder_out,
    out_grad,
    group_ids,
    target_mask,
    bucket_ids,
    gain_self,
    gain_cross,
    gain_ffn,
    query_self,
    key_self,
    value_self,
    output_self,
    query_cross,
    key_cross,
    value_cross,
    output_cross,
    gate_weight,
    up_weight,
    down_weight,
    position_bias,
):
    dp_size, tensor_size = mesh_shape
    query_count, tokens, width = decoder_in.shape
    assert query_count == 1 and tensor_size == 4 and dp_size % 2 == 0
    heads = query_self.shape[1] // DH
    own, all_heads = heads * DH, heads * tensor_size
    groups, buckets, _ = position_bias.shape
    rows, units = encoder_out.shape[1], gate_weight.shape[1]
    summing = dp_size == 8

    def vmem(*shape, kind=BF):
        return pltpu.VMEM(shape, kind)

    def shape_of(*shape, kind=BF):
        return jax.ShapeDtypeStruct(shape, kind)

    inputs = dict(
        x=(decoder_in[0], ANY),
        out_grad=(out_grad[0], ANY),
        encoder=(encoder_out[0], ANY),
        group=(group_ids, ANY),
        mask=(target_mask, ANY),
        bucket=(bucket_ids, ANY),
        gains=[(gain_self, ANY), (gain_cross, ANY), (gain_ffn, ANY)],
        wq_self=(query_self.T, ANY),
        wk_self=(key_self.T, ANY),
        wv_self=(value_self.T, ANY),
        wo_self=(output_self, ANY),
        wq_cross=(query_cross.T, ANY),
        wk_cross=(key_cross.T, ANY),
        wv_cross=(value_cross.T, ANY),
        wo_cross=(output_cross, ANY),
        gate_w=(gate_weight, ANY),
        up_w=(up_weight, ANY),
        down_w=(down_weight, ANY),
        table=(jnp.transpose(position_bias, (2, 0, 1)), ANY),
    )
    grad_shapes = [(units, width), (width, units), (width, units), (8 * own, width)]
    outputs = dict(
        block_out=(shape_of(tokens, width), ANY),
        decoder_grad=(shape_of(tokens, width), ANY),
        encoder_grad=(shape_of(rows, width), ANY),
        grads=[(shape_of(*shape), ANY) for shape in grad_shapes],
        small_sum=(shape_of(16, width, kind=F32), ANY),
    )
    plan = chunk_plan(own, width, units)
    all_own = all_heads * DH

    def sum_bufs(count, lanes):
        return [vmem(size, lanes) for size in (count, count // 2, count // 2, count // 2, count)]

    def chunk_bufs(in_x, source, size):
        lanes = grad_shapes[source][1]
        full = () if in_x else (0, 4)
        return [vmem(size if k in full else size // 2, lanes) for k in range(5)]

    token_low, token_wide = vmem(tokens, width), vmem(tokens, width, kind=F32)
    stats, kv_block = vmem(16, tokens, kind=F32), vmem(2, own, width)
    halves = vmem(all_own // 2, tokens)
    scratch = dict(
        gains=[vmem(width, kind=F32)] * 3, mask=vmem(1, tokens, kind=jnp.int32),
        group=pltpu.SMEM((1,), jnp.int32), table=pltpu.SMEM((heads, groups, buckets), F32),
        x=token_low, og=token_low, out_stage=token_low, wqkv=[vmem(own, width)] * 3, wo_self=vmem(own, width), wq_own=vmem(own, width),
        q_own=vmem(own, tokens), q_t=vmem(all_own, tokens),
        enc=vmem(rows, width), down=vmem(units, width), gate_w=vmem(width, units), up_w=vmem(width, units),
        self_in=token_low, cross_in=token_low, ffn_in=token_low, g1_low=token_low, g2_low=token_low,
        x2=token_wide, x3=token_wide, g1=token_wide, g2=token_wide,
        qkv=vmem(3 * own, tokens), d_qkv=vmem(3 * own, tokens), att_self=vmem(own, tokens),
        bucket=vmem(tokens, tokens, kind=jnp.int32), bucket_rows=vmem(128, tokens, kind=F32),
        p_self=vmem(heads, tokens, tokens, kind=F32), ds_self=vmem(heads, tokens, tokens, kind=F32),
        wk=vmem(all_own, width), wq=vmem(all_own, width), wv=vmem(all_own, width), wo=vmem(all_own, width),
        bq=vmem(all_own, 2 * tokens), bw=vmem(all_own, 2 * tokens),
        kc=vmem(rows, all_own), vc=vmem(rows, all_own),
        e=vmem(rows, all_heads * tokens), s=vmem(rows, 2 * tokens, kind=F32),
        mix=vmem(all_own, tokens), att=vmem(all_own, tokens), stat=stats, top=stats, lse=stats,
        mix_bufs=[halves] * 3 + [vmem(8, tokens, kind=F32)] * 3,
        delta=vmem(8, 2 * tokens, kind=F32), inverse=vmem(8, 2 * tokens, kind=F32),
        d_hidden=vmem(tokens, units, kind=F32), hidden=vmem(tokens, units),
        d_gate=vmem(tokens, units), d_up=vmem(tokens, units),
        s1=sum_bufs(tokens, width), s3=sum_bufs(tokens, width), so=sum_bufs(tokens, width),
        s4=sum_bufs(all_own, tokens), s5=sum_bufs(tokens, width),
        far_parts=[vmem(2 * own, width)] * 2, near_parts=[vmem(2 * own, width)] * 2,
        kv_near=kv_block, kv_home=kv_block, kv_half=kv_block, kv_far=kv_block,
        stage=vmem(2, TILE, width),
        grads=[vmem(*shape) for shape in grad_shapes],
        small=[vmem(16, width, kind=F32)] * (7 if summing else 1),
        gathered=[vmem(dp_size * tokens, width)] * 2
        + [vmem(dp_size * tokens, units), vmem(dp_size, 3 * own, tokens)] if summing else [],
        chunks=[chunk_bufs(in_x, source, size) for in_x, source, _, size in plan] if summing else [],
        sems=pltpu.SemaphoreType.DMA((400,)),
    )
    pair = lambda entry: isinstance(entry, tuple)
    first = lambda tree: jax.tree.map(lambda entry: entry[0], tree, is_leaf=pair)
    second = lambda tree: jax.tree.map(lambda entry: entry[1], tree, is_leaf=pair)
    flat = jax.tree.leaves
    trees = [jax.tree.structure(first(inputs)), jax.tree.structure(first(outputs)), jax.tree.structure(scratch)]
    cfg = SimpleNamespace(
        trees=trees, heads=heads, all_heads=all_heads, width=width, tokens=tokens, rows=rows,
        buckets=buckets, groups=groups, queries=dp_size, summing=summing, chunks=plan, schedule=SCHEDULE,
    )
    result = pl.pallas_call(
        functools.partial(block_kernel, cfg),
        out_shape=flat(first(outputs)),
        in_specs=flat(second(inputs)),
        out_specs=flat(second(outputs)),
        scratch_shapes=flat(scratch),
        compiler_params=pltpu.CompilerParams(collective_id=0, has_side_effects=True, vmem_limit_bytes=63 << 20),
        name="block",
    )(*flat(first(inputs)))
    got = SimpleNamespace(**jax.tree.unflatten(trees[1], result))
    kept = [got.block_out, got.decoder_grad, got.encoder_grad]
    if summing:
        inputs = dict(grads=got.grads, kept=kept, little=got.small_sum)
        outputs = dict(
            kept=[shape_of(*value.shape) for value in kept],
            gains=[shape_of(width, kind=F32)] * 3,
            position=shape_of(heads, groups, buckets, kind=F32),
            wide=[shape_of(*shape, kind=F32) for shape in grad_shapes[:3]],
            pieces=[shape_of(own, width, kind=F32)] * 8,
        )
        scratch = dict(
            low=[vmem(*shape) for shape in grad_shapes],
            kept=[vmem(*value.shape) for value in kept],
            wide=[vmem(*shape, kind=F32) for shape in grad_shapes],
            sems=pltpu.SemaphoreType.DMA((32,)),
        )
        trees = [jax.tree.structure(inputs), jax.tree.structure(outputs), jax.tree.structure(scratch)]

        def finish(*refs):
            groups_of, at = [], 0
            for tree in trees:
                groups_of.append(SimpleNamespace(**jax.tree.unflatten(tree, refs[at : at + tree.num_leaves])))
                at += tree.num_leaves
            finish_kernel(own, buckets, heads, groups, *groups_of)

        specs_in = dict(grads=[ANY] * 4, kept=[ANY] * 3, little=VMEM)
        specs_out = dict(kept=[ANY] * 3, gains=[VMEM] * 3, position=VMEM, wide=[ANY] * 3, pieces=[ANY] * 8)
        result = pl.pallas_call(
            finish,
            out_shape=flat(outputs),
            in_specs=flat(specs_in),
            out_specs=flat(specs_out),
            scratch_shapes=flat(scratch),
            compiler_params=pltpu.CompilerParams(vmem_limit_bytes=63 << 20),
            name="finish",
        )(*flat(inputs))
        done = SimpleNamespace(**jax.tree.unflatten(trees[1], result))
        kept, gain_grads, position = done.kept, done.gains, jnp.transpose(done.position, (1, 2, 0))
        wide, pieces = done.wide, done.pieces
    else:
        sums, little = lax.psum(([value.astype(F32) for value in got.grads], got.small_sum), "dp")
        wide = sums[:3]
        pieces = [sums[3][k * own : (k + 1) * own] for k in range(8)]
        gain_grads = [little[k] for k in range(3)]
        position = little[8 : 8 + groups, : heads * buckets].reshape(groups, heads, buckets)
        position = jnp.transpose(position, (0, 2, 1))
    down, gate, up = wide
    oc, qc, os, qs, ks, vs, kc, vc = pieces
    return (
        *[value[None] for value in kept], *gain_grads,
        qs.T, ks.T, vs.T, os, qc.T, kc.T, vc.T, oc, gate, up, down, position,
    )


def solution(mesh):
    rows = P("dp", None, None)
    encoder = P("dp", "tensor", None)
    columns, lines, whole = P(None, "tensor"), P("tensor", None), P()
    head_table = P(None, None, "tensor")
    weights = (columns, columns, columns, lines, columns, columns, columns, lines, columns, columns, lines, head_table)
    return jax.shard_map(
        functools.partial(shards, (mesh.shape["dp"], mesh.shape["tensor"])),
        mesh=mesh,
        in_specs=(rows, encoder, rows, P("dp"), P("dp", None), whole, whole, whole, whole) + weights,
        out_specs=(rows, rows, encoder, whole, whole, whole) + weights,
        check_vma=False,
    )
```

```python
import functools
from types import SimpleNamespace

import jax
import jax.numpy as jnp
from jax import lax
from jax.experimental import pallas as pl
from jax.experimental.pallas import tpu as pltpu
from jax.sharding import PartitionSpec as P

DH = 64
EPS = 1e-06
NEG = -1000000000.0
TILE = 256
MESH = pl.DeviceIdType.MESH
BF = jnp.bfloat16
F32 = jnp.float32
VMEM = pl.BlockSpec(memory_space=pltpu.VMEM)
SMEM = pl.BlockSpec(memory_space=pltpu.SMEM)
ANY = pl.BlockSpec(memory_space=pl.ANY)
GELU_SCALE = 0.7978845608028654
GELU_CUBIC = 0.044715


IN_X = (True, True, True, True, False, False, True, True, True)
SCHEDULE = (
    (),
    (),
    ((1, 0),),
    ((9, 0), (2, 0), (3, 0),),
    ((0, 0),),
    (),
    (),
    (),
    ((4, 0),),
    ((9, 1),),
    (),
    (),
    ((1, 1),),
    ((4, 1), (9, 2),),
    ((3, 1),),
    ((9, 3), (1, 2), (4, 2),),
    (),
    ((7, 0), (3, 2), (0, 1), (1, 3),),
    (),
    (),
    ((10, 0), (4, 3),),
    ((0, 2), (5, 0), (7, 1), (6, 0), (3, 3),),
    (),
    ((10, 1),),
    (),
    ((0, 3), (1, 4),),
    ((8, 0), (6, 1), (2, 1), (3, 4),),
    ((5, 1), (10, 2),),
    ((0, 4), (4, 4), (6, 2),),
    ((7, 2),),
    ((2, 2), (3, 5), (8, 1), (6, 3), (5, 2), (7, 3), (10, 3), (8, 2),),
    ((9, 4), (2, 3), (6, 4), (10, 4), (7, 4), (8, 3), (5, 3), (2, 4), (8, 4), (1, 5), (10, 5),),
    ((5, 4), (9, 5), (7, 5), (0, 5), (6, 5),),
    (),
    ((2, 5), (4, 5), (5, 5), (8, 5),),
)


def nn(left, right):
    return lax.dot_general(left, right, (((1,), (0,)), ((), ())), preferred_element_type=F32)


def nt(left, right):
    return lax.dot_general(left, right, (((1,), (1,)), ((), ())), preferred_element_type=F32)


def tn(left, right):
    return lax.dot_general(left, right, (((0,), (0,)), ((), ())), preferred_element_type=F32)


def span(start, size, step=None):
    return pl.ds(pl.multiple_of(start, step or size), size)


class Sems:
    def __init__(self, ref):
        self.ref, self.used = ref, 0

    def take(self):
        self.used += 1
        assert self.used <= self.ref.shape[0]
        return self.ref.at[self.used - 1]


class Wire:
    def __init__(self, sems, src, dst, device):
        self.copy = pltpu.make_async_remote_copy(
            src_ref=src, dst_ref=dst, send_sem=sems.take(), recv_sem=sems.take(), device_id=device, device_id_type=MESH
        )

    def start(self):
        self.copy.start()

    def sent(self):
        self.copy.wait_send()

    def came(self):
        self.copy.wait_recv()

    def wait(self):
        self.copy.wait()


class TensorSum:
    def __init__(self, sems, place, src, near, half, far, out):
        self.src, self.near, self.half, self.far, self.out = src, near, half, far, out
        size = src.shape[0] // 2
        self.mine = span(place.core * size, size)
        other = span((1 - place.core) * size, size)
        self.first = Wire(sems, src.at[other], near, place.mate)
        self.second = Wire(sems, half, far, place.across)
        self.third = Wire(sems, out.at[self.mine], out.at[self.mine], place.mate)

    def one(self):
        self.first.start()

    def two(self):
        self.first.wait()
        self.half[...] = (self.src[self.mine].astype(F32) + self.near[...].astype(F32)).astype(BF)
        self.second.start()

    def three(self):
        self.second.wait()
        self.out[self.mine] = (self.half[...].astype(F32) + self.far[...].astype(F32)).astype(BF)
        self.third.start()

    def four(self):
        self.third.wait()


class TensorMix:
    def __init__(self, sems, place, mix, stat, bufs, out, total):
        self.place, self.mix, self.stat, self.out, self.total = place, mix, stat, out, total
        near, half, far, near_stat, half_stat, far_stat = bufs
        self.bufs = bufs
        size, core = mix.shape[0] // 2, place.core
        self.size = size
        self.mine, other = span(core * size, size), span((1 - core) * size, size)
        self.mine_stat, other_stat = span(core * 8, 8), span((1 - core) * 8, 8)
        self.first = [
            Wire(sems, mix.at[other], near, place.mate),
            Wire(sems, stat.at[other_stat], near_stat, place.mate),
        ]
        self.second = [Wire(sems, half, far, place.across), Wire(sems, half_stat, far_stat, place.across)]
        self.third = [
            Wire(sems, out.at[self.mine], out.at[self.mine], place.mate),
            Wire(sems, total.at[self.mine_stat], total.at[self.mine_stat], place.mate),
        ]

    def join(self, ours, theirs, ours_stat, theirs_stat, flip, store):
        low_stat = jnp.where(flip, theirs_stat, ours_stat)
        high_stat = jnp.where(flip, ours_stat, theirs_stat)
        top = jnp.maximum(low_stat, high_stat)
        total = top + jnp.log(jnp.exp(low_stat - top) + jnp.exp(high_stat - top))
        low_share, high_share = jnp.exp(low_stat - total), jnp.exp(high_stat - total)
        for h in range(self.size // DH):
            rows = slice(h * DH, (h + 1) * DH)
            a, b = ours(rows), theirs(rows)
            low, high = jnp.where(flip, b, a), jnp.where(flip, a, b)
            store(rows, (low * low_share[h : h + 1] + high * high_share[h : h + 1]).astype(BF))
        return total

    def one(self):
        for wire in self.first:
            wire.start()

    def two(self):
        near, half, far, near_stat, half_stat, far_stat = self.bufs
        core, size = self.place.core, self.size
        for wire in self.first:
            wire.wait()

        def ours(rows):
            return self.mix[span(core * size + rows.start, DH)].astype(F32)

        def store(rows, value):
            half[rows] = value

        half_stat[...] = self.join(
            ours, lambda rows: near[rows].astype(F32), self.stat[self.mine_stat], near_stat[...], core == 1, store
        )
        for wire in self.second:
            wire.start()

    def three(self):
        near, half, far, near_stat, half_stat, far_stat = self.bufs
        core, size = self.place.core, self.size
        for wire in self.second:
            wire.wait()

        def store(rows, value):
            self.out[span(core * size + rows.start, DH)] = value

        self.total[self.mine_stat] = self.join(
            lambda rows: half[rows].astype(F32),
            lambda rows: far[rows].astype(F32),
            half_stat[...],
            far_stat[...],
            self.place.side == 1,
            store,
        )
        for wire in self.third:
            wire.start()

    def four(self):
        for wire in self.third:
            wire.wait()


class WeightGather:
    def __init__(self, sems, place, own, whole, local):
        rows = own.shape[0]
        half = rows // 2
        me, core, side, x = place.me, place.core, place.side, place.x
        there = (1 - side) * 2 + core
        self.own, self.whole = own, whole
        mine = span(me * rows, rows)
        direct = span(there * rows + x * half, half)
        relayed = span(there * rows + (1 - x) * half, half)
        self.across = Wire(sems, own.at[span(x * half, half)], whole.at[span(me * rows + x * half, half)], place.across)
        self.mate = Wire(sems, own, whole.at[mine], place.mate)
        self.side = Wire(sems, whole.at[direct], whole.at[direct], place.beside)
        self.direct = Wire(sems, whole.at[direct], whole.at[direct], place.mate)
        self.relayed = Wire(sems, whole.at[relayed], whole.at[relayed], place.mate)
        self.keep = pltpu.make_async_copy(own, whole.at[mine], local)

    def start(self):
        self.across.start()
        self.mate.start()
        self.keep.start()

    def one(self):
        self.across.came()
        self.side.start()
        self.direct.start()

    def two(self):
        self.side.came()
        self.relayed.start()

    def three(self):
        self.mate.came()
        self.keep.wait()
        self.direct.came()
        self.relayed.came()

    def end(self):
        for wire in (self.across, self.mate, self.side, self.direct, self.relayed):
            wire.sent()


class QueryGather:
    def __init__(self, sems, place, own, whole):
        rows = own.shape[0]
        there = (1 - place.side) * 2 + place.core
        self.own, self.whole, self.mine = own, whole, span(place.me * rows, rows)
        self.across = Wire(sems, own, whole.at[self.mine], place.across)
        self.mate = Wire(sems, own, whole.at[self.mine], place.mate)
        theirs = whole.at[span(there * rows, rows)]
        self.onward = Wire(sems, theirs, theirs, place.mate)

    def one(self):
        self.across.start()
        self.mate.start()
        self.whole[self.mine] = self.own[...]

    def two(self):
        self.across.came()
        self.onward.start()

    def three(self):
        self.mate.came()
        self.onward.came()

    def end(self):
        for wire in (self.across, self.mate, self.onward):
            wire.sent()


class ChunkX:
    def __init__(self, sems, place, g, out, bufs):
        self.place = place
        near, inn, mid, tot, fin = self.bufs = bufs
        half = g.shape[0] // 2
        x = place.x
        self.g, self.mine = g, span(x * half, half)
        other = span((1 - x) * half, half)
        self.rs = Wire(sems, g.at[other], near, place.beside)
        self.out = Wire(sems, g.at[self.mine], inn, place.pair)
        self.middle = Wire(sems, g.at[self.mine], mid, place.middle)
        self.back = Wire(sems, tot, tot, place.pair)
        self.ag = Wire(sems, tot, fin, place.beside)
        self.save = [
            pltpu.make_async_copy(tot, out.at[self.mine], sems.take()),
            pltpu.make_async_copy(fin, out.at[other], sems.take()),
        ]

    def s0(self):
        self.rs.start()

    def s1(self):
        self.rs.wait()
        self.g[self.mine] = self.g[self.mine] + self.bufs[0][...]

        @pl.when(self.place.end)
        def _():
            self.out.start()

    def s2(self):
        @pl.when(self.place.inner)
        def _():
            self.out.came()
            self.g[self.mine] = self.g[self.mine] + self.bufs[1][...]
            self.middle.start()

    def s3(self):
        @pl.when(self.place.inner)
        def _():
            self.middle.wait()
            self.bufs[3][...] = self.g[self.mine] + self.bufs[2][...]
            self.back.start()
            self.ag.start()
            self.save[0].start()

    def s4(self):
        @pl.when(self.place.end)
        def _():
            self.back.came()
            self.ag.start()
            self.save[0].start()

    def s5(self):
        self.ag.came()
        self.save[1].start()

    def finish(self):
        @pl.when(self.place.end)
        def _():
            self.out.sent()

        @pl.when(self.place.inner)
        def _():
            self.back.sent()

        self.ag.sent()
        for copy in self.save:
            copy.wait()


class ChunkZ:
    def __init__(self, sems, place, g, out, bufs):
        self.place = place
        inn, mid, r, xr, tot = self.bufs = bufs
        half = g.shape[0] // 2
        at = place.high
        self.g, self.mine = g, span(at * half, half)
        self.other = span((1 - at) * half, half)
        self.out = Wire(sems, g, inn, place.pair)
        self.rs = Wire(sems, g.at[self.other], mid, place.middle)
        self.x = Wire(sems, r, xr, place.beside)
        self.ag = Wire(sems, tot.at[self.mine], tot.at[self.mine], place.middle)
        self.back = [
            Wire(sems, tot.at[self.mine], tot.at[self.mine], place.pair),
            Wire(sems, tot.at[self.other], tot.at[self.other], place.pair),
        ]
        self.save = pltpu.make_async_copy(tot, out, sems.take())

    def s0(self):
        @pl.when(self.place.end)
        def _():
            self.out.start()

    def s1(self):
        @pl.when(self.place.inner)
        def _():
            self.out.came()
            self.g[...] = self.g[...] + self.bufs[0][...]
            self.rs.start()

    def s2(self):
        @pl.when(self.place.inner)
        def _():
            self.rs.wait()
            self.bufs[2][...] = self.g[self.mine] + self.bufs[1][...]
            self.x.start()

    def s3(self):
        @pl.when(self.place.inner)
        def _():
            self.x.wait()
            self.bufs[4][self.mine] = self.bufs[2][...] + self.bufs[3][...]
            self.ag.start()
            self.back[0].start()

    def s4(self):
        @pl.when(self.place.inner)
        def _():
            self.ag.came()
            self.back[1].start()
            self.save.start()

    def s5(self):
        @pl.when(self.place.end)
        def _():
            for wire in self.back:
                wire.came()
            self.save.start()

    def finish(self):
        @pl.when(self.place.end)
        def _():
            self.out.sent()

        @pl.when(self.place.inner)
        def _():
            self.ag.sent()
            for wire in self.back:
                wire.sent()

        self.save.wait()


class ChunkG:
    def __init__(self, sems, place, blocks, use=None):
        def wires(query, device):
            return [Wire(sems, block(query), block(query), device) for block in blocks]

        self.place, self.use = place, use
        first, second = place.far
        self.pair = wires(place.query, place.pair)
        self.x0 = wires(place.query, place.beside)
        self.x1 = wires(place.pair[0], place.beside)
        self.middle = wires(place.query, place.middle) + wires(place.pair[0], place.middle)
        self.back = wires(first, place.pair) + wires(second, place.pair)
        self.x2 = wires(first, place.beside) + wires(second, place.beside)

    def s0(self):
        for wire in self.pair + self.x0:
            wire.start()

    def s1(self):
        for wire in self.pair:
            wire.came()

        @pl.when(self.place.inner)
        def _():
            for wire in self.middle:
                wire.start()

        for wire in self.x1:
            wire.start()

    def s2(self):
        @pl.when(self.place.inner)
        def _():
            for wire in self.middle:
                wire.came()
            for wire in self.back + self.x2:
                wire.start()

    def s3(self):
        @pl.when(self.place.end)
        def _():
            for wire in self.back:
                wire.came()
            for wire in self.x2:
                wire.start()

    def s4(self):
        for wire in self.x0 + self.x1 + self.x2:
            wire.came()

    def s5(self):
        self.saves = self.use()

    def finish(self):
        for wire in self.pair + self.x0 + self.x1 + self.x2:
            wire.sent()

        @pl.when(self.place.inner)
        def _():
            for wire in self.middle + self.back:
                wire.sent()

        for copy in self.saves:
            copy.wait()


class SmallSum:
    def __init__(self, sems, place, bufs):
        self.place = place
        own, near, sum1, inn, sum2, mid, tot = self.bufs = bufs
        self.x = Wire(sems, own, near, place.beside)
        self.out = Wire(sems, sum1, inn, place.pair)
        self.middle = Wire(sems, sum2, mid, place.middle)
        self.back = Wire(sems, tot, tot, place.pair)

    def s0(self):
        self.x.start()

    def s1(self):
        own, near, sum1, inn, sum2, mid, tot = self.bufs
        self.x.wait()
        sum1[...] = own[...] + near[...]

        @pl.when(self.place.end)
        def _():
            self.out.start()

    def s2(self):
        own, near, sum1, inn, sum2, mid, tot = self.bufs

        @pl.when(self.place.inner)
        def _():
            self.out.came()
            sum2[...] = sum1[...] + inn[...]
            self.middle.start()

    def s3(self):
        own, near, sum1, inn, sum2, mid, tot = self.bufs

        @pl.when(self.place.inner)
        def _():
            self.middle.wait()
            tot[...] = sum2[...] + mid[...]
            self.back.start()
            self.back.sent()

    def s4(self):
        @pl.when(self.place.end)
        def _():
            self.out.sent()
            self.back.came()


def rms_scale(values):
    return lax.rsqrt(jnp.mean(values * values, axis=-1, keepdims=True) + EPS)


def norm_back(values, gain, dy):
    scale = rms_scale(values)
    normal = values * scale
    gain_grad = jnp.sum(dy * normal, axis=0, keepdims=True)
    pulled = dy * gain
    mean = jnp.mean(pulled * normal, axis=-1, keepdims=True)
    return scale * (pulled - normal * mean), gain_grad


def fold(values, op):
    rows, width = values.shape
    return op(values.reshape(rows // 8, 8, width), axis=0)


def chunk_plan(own, width, units):
    plan = [(a, k * (width // 2), width // 2) for a in (1, 2) for k in range(2)]
    plan += [(3, k * own, own) for k in (0, 1, 2, 6, 7)]
    return [(in_x, *block) for in_x, block in zip(IN_X, plan)]


def block_kernel(cfg, *refs):
    groups, at = [], 0
    for tree in cfg.trees:
        groups.append(SimpleNamespace(**jax.tree.unflatten(tree, refs[at : at + tree.num_leaves])))
        at += tree.num_leaves
    ins, outs, scr = groups
    heads, all_heads, width, tokens, rows = cfg.heads, cfg.all_heads, cfg.width, cfg.tokens, cfg.rows
    own, pairs, tiles = heads * DH, all_heads // 2, rows // TILE
    summing = cfg.summing
    sems = Sems(scr.sems)
    dp, me = lax.axis_index("dp"), lax.axis_index("tensor")
    core, side = lax.rem(me, 2), me // 2
    x, z = lax.rem(dp, 2), dp // 2
    place = SimpleNamespace(
        me=me,
        core=core,
        side=side,
        x=x,
        mate=(dp, side * 2 + 1 - core),
        across=(dp, (1 - side) * 2 + core),
        beside=(dp + 1 - 2 * x, me),
    )
    barrier = pltpu.get_barrier_semaphore()
    for friend in (place.mate, place.across, place.beside):
        pl.semaphore_signal(barrier, inc=1, device_id=friend, device_id_type=MESH)
    if summing:
        inner = jnp.logical_or(z == 1, z == 2)
        place.inner, place.end = inner, jnp.logical_not(inner)
        place.high = z // 2
        place.pair = ((z + 1 - 2 * lax.rem(z, 2)) * 2 + x, me)
        place.middle = ((3 - z) * 2 + x, me)
        place.query = dp
        place.far = ((2 - z // 2) * 2 + x, 3 * (1 - z // 2) * 2 + x)
        pl.semaphore_signal(barrier, inc=1, device_id=place.pair, device_id_type=MESH)

        @pl.when(inner)
        def _():
            pl.semaphore_signal(barrier, inc=1, device_id=place.middle, device_id_type=MESH)

    def fetch(src, dst):
        copy = pltpu.make_async_copy(src, dst, sems.take())
        copy.start()
        return copy

    enc, down, gate_w, up_w = scr.enc, scr.down, scr.gate_w, scr.up_w
    first_loads = [fetch(ins.x, scr.x)] + [fetch(src, dst) for src, dst in zip(ins.gains, scr.gains)]
    self_weights = scr.wqkv
    for src, dst in zip((ins.wq_self, ins.wk_self, ins.wv_self), self_weights):
        first_loads.append(fetch(src, dst))
    load_bucket, load_out = fetch(ins.bucket, scr.bucket), fetch(ins.wo_self, scr.wo_self)
    load_small = [fetch(ins.mask, scr.mask), fetch(ins.group, scr.group), fetch(ins.table, scr.table)]
    load_query = fetch(ins.wq_cross, scr.wq_own)
    load_enc = fetch(ins.encoder, enc)
    load_ffn = [fetch(ins.out_grad, scr.og), fetch(ins.down_w, down), fetch(ins.gate_w, gate_w), fetch(ins.up_w, up_w)]

    for load in first_loads:
        load.wait()
    gain_self, gain_cross, gain_ffn = (gain[...].reshape(1, width) for gain in scr.gains)
    xv = scr.x[...].astype(F32)
    self_in = scr.self_in
    self_in[...] = (xv * rms_scale(xv) * gain_self).astype(BF)
    qkv = scr.qkv
    for k, weight in enumerate(self_weights):
        qkv[k * own : (k + 1) * own] = nt(weight[...], self_in[...]).astype(BF)
    if summing:
        pl.semaphore_wait(barrier, 4 + inner.astype(jnp.int32))
    else:
        pl.semaphore_wait(barrier, 3)
    wk, wq, wv, wo = scr.wk, scr.wq, scr.wv, scr.wo
    get_k, get_q, get_v, get_o = gathers = [
        WeightGather(sems, place, part, whole, sems.take())
        for part, whole in ((ins.wk_cross, wk), (ins.wq_cross, wq), (ins.wv_cross, wv), (ins.wo_cross, wo))
    ]
    get_k.start()
    if summing:
        lanes_half = span(core * (width // 2), width // 2, 2 * DH)
        og_all, self_all, hidden_all, d_qkv_all = scr.gathered

        def rows_of(query):
            return span(query * tokens, tokens)

        load_ffn[0].wait()
        og_all[rows_of(dp), lanes_half] = scr.og[:, lanes_half]
        self_all[rows_of(dp), lanes_half] = self_in[:, lanes_half]
        early = ChunkG(
            sems,
            place,
            [lambda query: og_all.at[rows_of(query), lanes_half], lambda query: self_all.at[rows_of(query), lanes_half]],
            lambda: [],
        )
        shares = [Wire(sems, ref.at[:, lanes_half], ref.at[:, lanes_half], place.mate) for ref in (og_all, self_all)]
        early.s0()
    load_bucket.wait()
    for load in load_small:
        load.wait()
    scr.bucket[...] = scr.bucket[...].T
    bucket = scr.bucket
    keep = jnp.broadcast_to(scr.mask[...].astype(F32), (tokens, tokens)).T
    j_at = lax.broadcasted_iota(jnp.int32, (tokens, tokens), 0)
    i_at = lax.broadcasted_iota(jnp.int32, (tokens, tokens), 1)
    allowed = jnp.logical_or(jnp.logical_and(j_at <= i_at, keep == 1.0), j_at == i_at)
    group = scr.group[0]
    buckets = cfg.buckets
    for h in range(heads):
        scr.p_self[h] = jnp.full((tokens, tokens), NEG, F32)

    def spread(b, _):
        hit = jnp.logical_and(bucket[...] == b, allowed)
        for h in range(heads):
            scr.p_self[h] = jnp.where(hit, scr.table[h, group, b], scr.p_self[h])
        return 0

    lax.fori_loop(0, buckets, spread, 0)
    att_self = scr.att_self

    def attend(h):
        q = qkv[h * DH : (h + 1) * DH]
        k = qkv[own + h * DH : own + (h + 1) * DH]
        v = qkv[2 * own + h * DH : 2 * own + (h + 1) * DH]
        s = tn(k, q) + scr.p_self[h]
        e = jnp.exp(s - jnp.max(s, axis=0, keepdims=True))
        p = e / jnp.sum(e, axis=0, keepdims=True)
        scr.p_self[h] = p
        att_self[h * DH : (h + 1) * DH] = nn(v, p.astype(BF)).astype(BF)

    for h in range(heads):
        attend(h)

    def tensor_sum(bufs):
        return TensorSum(sems, place, *bufs)

    s1 = tensor_sum(scr.s1)
    load_out.wait()
    s1.src[...] = tn(att_self[...], scr.wo_self[...]).astype(BF)
    s1.one()
    s1.two()
    get_v.start()
    bq, bw = scr.bq, scr.bw
    for ref in (bq, bw, scr.stat, scr.top, scr.small[0], scr.bucket_rows):
        ref[...] = jnp.zeros(ref.shape, ref.dtype)
    get_k.one()
    load_enc.wait()
    if summing:
        early.s1()
    kc, vc, e_ref = scr.kc, scr.vc, scr.e

    def project(dst, weight):
        def body(r, _):
            at = span(r * TILE, TILE)
            dst[at] = nt(enc[at], weight[...]).astype(BF)
            return 0

        lax.fori_loop(0, tiles, body, 0)

    s1.three()
    s1.four()
    x2 = scr.x2
    x2[...] = scr.x[...].astype(F32) + s1.out[...].astype(F32)
    cross_in = scr.cross_in
    cross_in[...] = (x2[...] * rms_scale(x2[...]) * gain_cross).astype(BF)
    load_query.wait()
    scr.q_own[...] = nt(scr.wq_own[...], cross_in[...]).astype(BF)
    get_query = QueryGather(sems, place, scr.q_own, scr.q_t)
    get_query.one()
    get_o.start()
    get_q.start()
    get_k.two()
    get_v.one()
    get_k.three()
    project(kc, wk)
    get_query.two()
    get_query.three()
    for h in range(all_heads):
        at = slice(h * DH, (h + 1) * DH)
        bq[at, (h % 2) * tokens : (h % 2 + 1) * tokens] = scr.q_t[at]
    s_ref, mix, stat, top_ref = scr.s, scr.mix, scr.stat, scr.top
    per_half = pairs // 2

    def stat_row(p):
        return (p // per_half) * 8 + 2 * (p - (p // per_half) * per_half)

    def score_pair(p, _):
        head_at = span(p * 2 * DH, 2 * DH)
        score_at = span(p * 2 * tokens, 2 * tokens)
        weights = bq[head_at]
        top = None
        for r in range(tiles):
            at = slice(r * TILE, (r + 1) * TILE)
            s = nn(kc[at, head_at], weights)
            s_ref[at] = s
            part = fold(s, jnp.max)
            top = part if top is None else jnp.maximum(top, part)
        top = jnp.max(top, axis=0, keepdims=True)
        total = None
        for r in range(tiles):
            at = slice(r * TILE, (r + 1) * TILE)
            e = jnp.exp(s_ref[at] - top)
            part = fold(e, jnp.sum)
            total = part if total is None else total + part
            e_ref[at, score_at] = e.astype(BF)
        total = jnp.sum(total, axis=0, keepdims=True)
        scr.inverse[pl.ds(p, 1)] = 1.0 / total
        lse = top + jnp.log(total)
        row = stat_row(p)
        for k in range(2):
            lanes = slice(k * tokens, (k + 1) * tokens)
            stat[pl.ds(row + k, 1)] = lse[:, lanes]
            top_ref[pl.ds(row + k, 1)] = top[:, lanes]
        return 0

    def mix_pair(p, _):
        acc = tn(vc[:, span(p * 2 * DH, 2 * DH)], e_ref[:, span(p * 2 * tokens, 2 * tokens)])
        inverse = scr.inverse[pl.ds(p, 1)]
        for k in range(2):
            lanes = slice(k * tokens, (k + 1) * tokens)
            value = acc[k * DH : (k + 1) * DH, lanes] * inverse[:, lanes]
            mix[span(p * 2 * DH + k * DH, DH)] = value.astype(BF)
        return 0

    lax.fori_loop(0, pairs - 2, score_pair, 0)
    get_v.two()
    get_o.one()
    if summing:
        early.s2()
    lax.fori_loop(pairs - 2, pairs, score_pair, 0)
    get_v.three()
    att, lse = scr.att, scr.lse
    s2 = TensorMix(sems, place, mix, stat, scr.mix_bufs, att, lse)
    project(vc, wv)
    for half in (1 - core, core):
        lax.fori_loop(half * per_half, (half + 1) * per_half, mix_pair, 0)
        if half is not core:
            s2.one()
            get_q.one()
    s2.two()
    for load in load_ffn[1 if summing else 0 :]:
        load.wait()
    og = scr.og
    scr.d_hidden[...] = nt(og[...], down[...]).astype(BF).astype(F32)
    get_o.two()
    s2.three()
    get_o.three()
    s2.four()
    if summing:
        early.s3()
    x3 = scr.x3
    x3[...] = x2[...] + tn(att[...], wo[...])
    ffn_in = scr.ffn_in
    ffn_in[...] = (x3[...] * rms_scale(x3[...]) * gain_ffn).astype(BF)
    gate = nn(ffn_in[...], gate_w[...])
    up = nn(ffn_in[...], up_w[...])
    squared = gate * gate
    curve = jnp.tanh(GELU_SCALE * (gate + GELU_CUBIC * (squared * gate)))
    gelu = 0.5 * gate * (1.0 + curve)
    slope = 0.5 * (1.0 + curve) + 0.5 * gate * (1.0 - curve * curve) * (
        GELU_SCALE * (1.0 + 3.0 * GELU_CUBIC * squared)
    )
    d_hidden = scr.d_hidden[...]
    scr.hidden[...] = (gelu * up).astype(BF)
    scr.d_gate[...] = (d_hidden * up * slope).astype(BF)
    scr.d_up[...] = (d_hidden * gelu).astype(BF)

    g_down, g_gate, g_up, g_small = scr.grads
    chunks = []
    if summing:
        def use_hidden():
            g_down[...] = tn(hidden_all[...], og_all[...]).astype(BF)
            return [fetch(g_down, outs.grads[0])]

        def use_d_qkv():
            whole = jnp.concatenate([d_qkv_all[k] for k in range(cfg.queries)], axis=1)
            g_small[3 * own : 6 * own] = nn(whole, self_all[...]).astype(BF)
            at = pl.ds(3 * own, 3 * own)
            return [fetch(g_small.at[at], outs.grads[3].at[at])]

        for (in_x, source, start, size), bufs in zip(cfg.chunks, scr.chunks):
            rows_at = pl.ds(start, size)
            maker = ChunkX if in_x else ChunkZ
            chunks.append(maker(sems, place, scr.grads[source].at[rows_at], outs.grads[source].at[rows_at], bufs))
        chunks.append(ChunkG(sems, place, [lambda query: hidden_all.at[rows_of(query)]], use_hidden))
        chunks.append(ChunkG(sems, place, [lambda query: d_qkv_all.at[query]], use_d_qkv))
    schedule = iter(cfg.schedule)

    def poll():
        if summing:
            for n, k in next(schedule):
                chunk = chunks[n]
                (chunk.s0, chunk.s1, chunk.s2, chunk.s3, chunk.s4, chunk.s5)[k]()

    if summing:
        hidden_all[rows_of(dp)] = scr.hidden[...]
    else:
        g_down[...] = tn(scr.hidden[...], og[...]).astype(BF)
    poll()
    g_gate[...] = tn(ffn_in[...], scr.d_gate[...]).astype(BF)
    poll()
    g_up[...] = tn(ffn_in[...], scr.d_up[...]).astype(BF)
    poll()
    s3, so = tensor_sum(scr.s3), tensor_sum(scr.so)
    s3.src[...] = (nt(scr.d_gate[...], gate_w[...]) + nt(scr.d_up[...], up_w[...])).astype(BF)
    s3.one()
    so.src[...] = nn(scr.hidden[...], down[...]).astype(BF)
    s3.two()
    poll()
    get_q.two()
    poll()
    s3.three()
    so.one()
    s3.four()
    so.two()
    poll()
    g2, g2_low = scr.g2, scr.g2_low
    dv, gain_grad = norm_back(x3[...], gain_ffn, s3.out[...].astype(F32))
    g2[...] = og[...].astype(F32) + dv
    g2_low[...] = g2[...].astype(BF)
    small = scr.small[0]
    small[2:3, :width] = gain_grad
    g_small[0:own] = nn(att[span(me * own, own)], g2_low[...]).astype(BF)
    poll()
    d_att = nt(wo[...], g2_low[...])
    delta_ref = scr.delta
    for h in range(all_heads):
        at = slice(h * DH, (h + 1) * DH)
        p, k = divmod(h, 2)
        row = (p // per_half) * 8 + 2 * (p % per_half) + k
        share = jnp.exp(top_ref[row : row + 1] - lse[row : row + 1])
        low = (d_att[at] * share).astype(BF)
        bw[at, k * tokens : (k + 1) * tokens] = low
        delta_ref[p : p + 1, k * tokens : (k + 1) * tokens] = jnp.sum(
            low.astype(F32) * att[at].astype(F32), axis=0, keepdims=True
        )
    so.three()
    s4 = tensor_sum(scr.s4)

    def backward_pair(p, _):
        head_at = span(p * 2 * DH, 2 * DH)
        score_at = span(p * 2 * tokens, 2 * tokens)
        wq_block, wa_block = bq[head_at], bw[head_at]
        delta = delta_ref[pl.ds(p, 1)]
        acc = None
        for r in range(tiles):
            at = slice(r * TILE, (r + 1) * TILE)
            e = e_ref[at, score_at]
            grad = nn(vc[at, head_at], wa_block)
            ds = (e.astype(F32) * (grad - delta)).astype(BF)
            part = tn(kc[at, head_at], ds)
            acc = part if acc is None else acc + part
            kc[at, head_at] = nt(ds, wq_block).astype(BF)
            vc[at, head_at] = nt(e, wa_block).astype(BF)
        for k in range(2):
            value = acc[k * DH : (k + 1) * DH, k * tokens : (k + 1) * tokens]
            s4.src[span(p * 2 * DH + k * DH, DH)] = value.astype(BF)
        return 0

    far_at, near_at = (1 - side) * per_half, side * per_half
    far_parts, near_parts = scr.far_parts, scr.near_parts
    kv_near, kv_home, kv_half, kv_far = scr.kv_near, scr.kv_home, scr.kv_half, scr.kv_far
    to_mate, to_across, to_home = [], [], []
    mine, other = span(core * own, own), span((1 - core) * own, own)
    for a in range(2):
        to_mate.append(Wire(sems, far_parts[a].at[other], kv_near.at[a], place.mate))
        to_across.append(Wire(sems, kv_half.at[a], kv_far.at[a], place.across))
        to_home.append(Wire(sems, near_parts[a].at[other], kv_home.at[a], place.mate))

    def weight_part(dst, source, first):
        rows_of = source[:, span(first * 2 * DH, 2 * own, 2 * DH)]

        def body(t, _):
            lanes = span(t * TILE, TILE)
            dst[:, lanes] = tn(rows_of, enc[:, lanes]).astype(BF)
            return 0

        lax.fori_loop(0, width // TILE, body, 0)

    def pass_across(a):
        to_mate[a].wait()
        kv_half[a] = (far_parts[a][mine].astype(F32) + kv_near[a].astype(F32)).astype(BF)
        to_across[a].start()

    if summing:
        early.s4()
        early.s5()
        for wire in shares:
            wire.start()
    for p in range(per_half):
        poll()
        lax.fori_loop(far_at + p, far_at + p + 1, backward_pair, 0)
    poll()
    so.four()
    scr.out_stage[...] = (x3[...] + so.out[...].astype(F32)).astype(BF)
    token_saves = [fetch(scr.out_stage, outs.block_out)]
    if summing:
        for wire in shares:
            wire.came()
    weight_part(far_parts[0], kc, far_at)
    to_mate[0].start()
    weight_part(far_parts[1], vc, far_at)
    to_mate[1].start()
    pass_across(0)
    for p in range(per_half):
        poll()
        lax.fori_loop(near_at + p, near_at + p + 1, backward_pair, 0)
    s4.one()
    poll()
    weight_part(near_parts[0], kc, near_at)
    to_home[0].start()
    s4.two()
    pass_across(1)
    poll()
    weight_part(near_parts[1], vc, near_at)
    to_home[1].start()
    s4.three()
    poll()

    def kv_done(a):
        to_home[a].wait()
        to_across[a].wait()
        total = near_parts[a][mine].astype(F32) + kv_home[a].astype(F32) + kv_far[a].astype(F32)
        g_small[(6 + a) * own : (7 + a) * own] = total.astype(BF)

    kv_done(0)
    s4.four()
    poll()
    get_q.three()
    d_cross = tn(s4.out[...], wq[...])
    dv, gain_grad = norm_back(x2[...], gain_cross, d_cross)
    small[1:2, :width] = gain_grad
    g1, g1_low = scr.g1, scr.g1_low
    g1[...] = g2[...] + dv
    g1_low[...] = g1[...].astype(BF)
    g_small[own : 2 * own] = nn(s4.out[span(me * own, own)], cross_in[...]).astype(BF)
    g_small[2 * own : 3 * own] = nn(att_self[...], g1_low[...]).astype(BF)
    poll()
    d_att_self = nt(scr.wo_self[...], g1_low[...]).astype(BF)
    d_qkv = scr.d_qkv
    for h in range(heads):
        at = slice(h * DH, (h + 1) * DH)
        q = qkv[h * DH : (h + 1) * DH]
        k = qkv[own + h * DH : own + (h + 1) * DH]
        v = qkv[2 * own + h * DH : 2 * own + (h + 1) * DH]
        p = scr.p_self[h]
        grad = tn(v, d_att_self[at])
        ds = (p * (grad - jnp.sum(p * grad, axis=0, keepdims=True))).astype(BF)
        scr.ds_self[h] = ds.astype(F32)
        d_qkv[h * DH : (h + 1) * DH] = nn(k, ds).astype(BF)
        d_qkv[own + h * DH : own + (h + 1) * DH] = nt(q, ds).astype(BF)
        d_qkv[2 * own + h * DH : 2 * own + (h + 1) * DH] = nt(d_att_self[at], p.astype(BF)).astype(BF)
    poll()
    if summing:
        d_qkv_all[dp] = d_qkv[...]
    else:
        g_small[3 * own : 6 * own] = nn(d_qkv[...], self_in[...]).astype(BF)
    poll()
    s5 = tensor_sum(scr.s5)
    total = None
    for k, weight in enumerate(self_weights):
        part = tn(d_qkv[k * own : (k + 1) * own], weight[...])
        total = part if total is None else total + part
    s5.src[...] = total.astype(BF)
    s5.one()
    poll()
    rows_ref = scr.bucket_rows

    def count(b, _):
        hit = bucket[...] == b
        for h in range(heads):
            value = jnp.where(hit, scr.ds_self[h], 0.0)
            rows_ref[pl.ds(h * buckets + b, 1)] = jnp.sum(value, axis=0, keepdims=True)
        return 0

    s5.two()
    lax.fori_loop(0, buckets, count, 0)
    position = jnp.sum(rows_ref[...].T, axis=0, keepdims=True)
    for g in range(cfg.groups):
        hot = jnp.where(group == g, 1.0, 0.0).astype(F32)
        small[8 + g : 9 + g, :tokens] = position * hot
    poll()

    saves = [None, None]

    def encoder_tile(r):
        at = slice(r * TILE, (r + 1) * TILE)
        slot = r % 2
        if saves[slot] is not None:
            saves[slot].wait()
        stage = scr.stage.at[slot]
        stage[...] = (nn(kc[at], wk[...]) + nn(vc[at], wv[...])).astype(BF)
        saves[slot] = fetch(stage, outs.encoder_grad.at[pl.ds(r * TILE, TILE)])

    for r in range(tiles // 2):
        encoder_tile(r)
        poll()
    kv_done(1)
    poll()
    s5.three()
    for r in range(tiles // 2, tiles):
        encoder_tile(r)
        poll()
    s5.four()
    dv, gain_grad = norm_back(scr.x[...].astype(F32), gain_self, s5.out[...].astype(F32))
    scr.og[...] = (g1[...] + dv).astype(BF)
    token_saves.append(fetch(scr.og, outs.decoder_grad))
    small[0:1, :width] = gain_grad
    for copy in saves + token_saves:
        copy.wait()
    if summing:
        little = SmallSum(sems, place, scr.small)
        little.s0()
        poll()
        little.s1()
        poll()
        little.s2()
        poll()
        little.s3()
        poll()
        little.s4()
        last = fetch(little.bufs[6], outs.small_sum)
        poll()
        for chunk in chunks + [early]:
            chunk.finish()
        for wire in shares:
            wire.sent()
    else:
        for copy in [fetch(src, dst) for src, dst in zip(scr.grads, outs.grads)]:
            copy.wait()
        last = fetch(small, outs.small_sum)
    last.wait()
    for gather in gathers + [get_query]:
        gather.end()


def finish_kernel(own, buckets, heads, groups, ins, outs, scr):
    used = [0]

    def copy(src, dst):
        made = pltpu.make_async_copy(src, dst, scr.sems.at[used[0]])
        used[0] += 1
        made.start()
        return made

    loads = [copy(src, dst) for src, dst in zip(ins.grads, scr.low)]
    moves = [copy(src, dst) for src, dst in zip(ins.kept, scr.kept)]
    keeps = []
    for k in range(3):
        outs.gains[k][...] = ins.little[k : k + 1].reshape(outs.gains[k].shape)
    for h in range(heads):
        outs.position[h] = ins.little[8 : 8 + groups, h * buckets : (h + 1) * buckets]
    for k in range(3):
        loads[k].wait()
        scr.wide[k][...] = scr.low[k][...].astype(F32)
        keeps.append(copy(scr.wide[k], outs.wide[k]))
    loads[3].wait()
    for k, out in enumerate(outs.pieces):
        at = slice(k * own, (k + 1) * own)
        scr.wide[3][at] = scr.low[3][at].astype(F32)
        keeps.append(copy(scr.wide[3].at[at], out))
    for k, move in enumerate(moves):
        move.wait()
        keeps.append(copy(scr.kept[k], outs.kept[k]))
    for made in keeps:
        made.wait()


def shards(
    mesh_shape,
    decoder_in,
    encoder_out,
    out_grad,
    group_ids,
    target_mask,
    bucket_ids,
    gain_self,
    gain_cross,
    gain_ffn,
    query_self,
    key_self,
    value_self,
    output_self,
    query_cross,
    key_cross,
    value_cross,
    output_cross,
    gate_weight,
    up_weight,
    down_weight,
    position_bias,
):
    dp_size, tensor_size = mesh_shape
    query_count, tokens, width = decoder_in.shape
    assert query_count == 1 and tensor_size == 4 and dp_size % 2 == 0
    heads = query_self.shape[1] // DH
    own, all_heads = heads * DH, heads * tensor_size
    groups, buckets, _ = position_bias.shape
    rows, units = encoder_out.shape[1], gate_weight.shape[1]
    summing = dp_size == 8

    def vmem(*shape, kind=BF):
        return pltpu.VMEM(shape, kind)

    def shape_of(*shape, kind=BF):
        return jax.ShapeDtypeStruct(shape, kind)

    inputs = dict(
        x=(decoder_in[0], ANY),
        out_grad=(out_grad[0], ANY),
        encoder=(encoder_out[0], ANY),
        group=(group_ids, ANY),
        mask=(target_mask, ANY),
        bucket=(bucket_ids, ANY),
        gains=[(gain_self, ANY), (gain_cross, ANY), (gain_ffn, ANY)],
        wq_self=(query_self.T, ANY),
        wk_self=(key_self.T, ANY),
        wv_self=(value_self.T, ANY),
        wo_self=(output_self, ANY),
        wq_cross=(query_cross.T, ANY),
        wk_cross=(key_cross.T, ANY),
        wv_cross=(value_cross.T, ANY),
        wo_cross=(output_cross, ANY),
        gate_w=(gate_weight, ANY),
        up_w=(up_weight, ANY),
        down_w=(down_weight, ANY),
        table=(jnp.transpose(position_bias, (2, 0, 1)), ANY),
    )
    grad_shapes = [(units, width), (width, units), (width, units), (8 * own, width)]
    outputs = dict(
        block_out=(shape_of(tokens, width), ANY),
        decoder_grad=(shape_of(tokens, width), ANY),
        encoder_grad=(shape_of(rows, width), ANY),
        grads=[(shape_of(*shape), ANY) for shape in grad_shapes],
        small_sum=(shape_of(16, width, kind=F32), ANY),
    )
    plan = chunk_plan(own, width, units)
    all_own = all_heads * DH

    def sum_bufs(count, lanes):
        return [vmem(size, lanes) for size in (count, count // 2, count // 2, count // 2, count)]

    def chunk_bufs(in_x, source, size):
        lanes = grad_shapes[source][1]
        full = () if in_x else (0, 4)
        return [vmem(size if k in full else size // 2, lanes) for k in range(5)]

    token_low, token_wide = vmem(tokens, width), vmem(tokens, width, kind=F32)
    stats, kv_block = vmem(16, tokens, kind=F32), vmem(2, own, width)
    halves = vmem(all_own // 2, tokens)
    scratch = dict(
        gains=[vmem(width, kind=F32)] * 3, mask=vmem(1, tokens, kind=jnp.int32),
        group=pltpu.SMEM((1,), jnp.int32), table=pltpu.SMEM((heads, groups, buckets), F32),
        x=token_low, og=token_low, out_stage=token_low, wqkv=[vmem(own, width)] * 3, wo_self=vmem(own, width), wq_own=vmem(own, width),
        q_own=vmem(own, tokens), q_t=vmem(all_own, tokens),
        enc=vmem(rows, width), down=vmem(units, width), gate_w=vmem(width, units), up_w=vmem(width, units),
        self_in=token_low, cross_in=token_low, ffn_in=token_low, g1_low=token_low, g2_low=token_low,
        x2=token_wide, x3=token_wide, g1=token_wide, g2=token_wide,
        qkv=vmem(3 * own, tokens), d_qkv=vmem(3 * own, tokens), att_self=vmem(own, tokens),
        bucket=vmem(tokens, tokens, kind=jnp.int32), bucket_rows=vmem(128, tokens, kind=F32),
        p_self=vmem(heads, tokens, tokens, kind=F32), ds_self=vmem(heads, tokens, tokens, kind=F32),
        wk=vmem(all_own, width), wq=vmem(all_own, width), wv=vmem(all_own, width), wo=vmem(all_own, width),
        bq=vmem(all_own, 2 * tokens), bw=vmem(all_own, 2 * tokens),
        kc=vmem(rows, all_own), vc=vmem(rows, all_own),
        e=vmem(rows, all_heads * tokens), s=vmem(rows, 2 * tokens, kind=F32),
        mix=vmem(all_own, tokens), att=vmem(all_own, tokens), stat=stats, top=stats, lse=stats,
        mix_bufs=[halves] * 3 + [vmem(8, tokens, kind=F32)] * 3,
        delta=vmem(8, 2 * tokens, kind=F32), inverse=vmem(8, 2 * tokens, kind=F32),
        d_hidden=vmem(tokens, units, kind=F32), hidden=vmem(tokens, units),
        d_gate=vmem(tokens, units), d_up=vmem(tokens, units),
        s1=sum_bufs(tokens, width), s3=sum_bufs(tokens, width), so=sum_bufs(tokens, width),
        s4=sum_bufs(all_own, tokens), s5=sum_bufs(tokens, width),
        far_parts=[vmem(2 * own, width)] * 2, near_parts=[vmem(2 * own, width)] * 2,
        kv_near=kv_block, kv_home=kv_block, kv_half=kv_block, kv_far=kv_block,
        stage=vmem(2, TILE, width),
        grads=[vmem(*shape) for shape in grad_shapes],
        small=[vmem(16, width, kind=F32)] * (7 if summing else 1),
        gathered=[vmem(dp_size * tokens, width)] * 2
        + [vmem(dp_size * tokens, units), vmem(dp_size, 3 * own, tokens)] if summing else [],
        chunks=[chunk_bufs(in_x, source, size) for in_x, source, _, size in plan] if summing else [],
        sems=pltpu.SemaphoreType.DMA((400,)),
    )
    pair = lambda entry: isinstance(entry, tuple)
    first = lambda tree: jax.tree.map(lambda entry: entry[0], tree, is_leaf=pair)
    second = lambda tree: jax.tree.map(lambda entry: entry[1], tree, is_leaf=pair)
    flat = jax.tree.leaves
    trees = [jax.tree.structure(first(inputs)), jax.tree.structure(first(outputs)), jax.tree.structure(scratch)]
    cfg = SimpleNamespace(
        trees=trees, heads=heads, all_heads=all_heads, width=width, tokens=tokens, rows=rows,
        buckets=buckets, groups=groups, queries=dp_size, summing=summing, chunks=plan, schedule=SCHEDULE,
    )
    result = pl.pallas_call(
        functools.partial(block_kernel, cfg),
        out_shape=flat(first(outputs)),
        in_specs=flat(second(inputs)),
        out_specs=flat(second(outputs)),
        scratch_shapes=flat(scratch),
        compiler_params=pltpu.CompilerParams(collective_id=0, has_side_effects=True, vmem_limit_bytes=63 << 20),
        name="block",
    )(*flat(first(inputs)))
    got = SimpleNamespace(**jax.tree.unflatten(trees[1], result))
    kept = [got.block_out, got.decoder_grad, got.encoder_grad]
    if summing:
        inputs = dict(grads=got.grads, kept=kept, little=got.small_sum)
        outputs = dict(
            kept=[shape_of(*value.shape) for value in kept],
            gains=[shape_of(width, kind=F32)] * 3,
            position=shape_of(heads, groups, buckets, kind=F32),
            wide=[shape_of(*shape, kind=F32) for shape in grad_shapes[:3]],
            pieces=[shape_of(own, width, kind=F32)] * 8,
        )
        scratch = dict(
            low=[vmem(*shape) for shape in grad_shapes],
            kept=[vmem(*value.shape) for value in kept],
            wide=[vmem(*shape, kind=F32) for shape in grad_shapes],
            sems=pltpu.SemaphoreType.DMA((32,)),
        )
        trees = [jax.tree.structure(inputs), jax.tree.structure(outputs), jax.tree.structure(scratch)]

        def finish(*refs):
            groups_of, at = [], 0
            for tree in trees:
                groups_of.append(SimpleNamespace(**jax.tree.unflatten(tree, refs[at : at + tree.num_leaves])))
                at += tree.num_leaves
            finish_kernel(own, buckets, heads, groups, *groups_of)

        specs_in = dict(grads=[ANY] * 4, kept=[ANY] * 3, little=VMEM)
        specs_out = dict(kept=[ANY] * 3, gains=[VMEM] * 3, position=VMEM, wide=[ANY] * 3, pieces=[ANY] * 8)
        result = pl.pallas_call(
            finish,
            out_shape=flat(outputs),
            in_specs=flat(specs_in),
            out_specs=flat(specs_out),
            scratch_shapes=flat(scratch),
            compiler_params=pltpu.CompilerParams(vmem_limit_bytes=63 << 20),
            name="finish",
        )(*flat(inputs))
        done = SimpleNamespace(**jax.tree.unflatten(trees[1], result))
        kept, gain_grads, position = done.kept, done.gains, jnp.transpose(done.position, (1, 2, 0))
        wide, pieces = done.wide, done.pieces
    else:
        sums, little = lax.psum(([value.astype(F32) for value in got.grads], got.small_sum), "dp")
        wide = sums[:3]
        pieces = [sums[3][k * own : (k + 1) * own] for k in range(8)]
        gain_grads = [little[k] for k in range(3)]
        position = little[8 : 8 + groups, : heads * buckets].reshape(groups, heads, buckets)
        position = jnp.transpose(position, (0, 2, 1))
    down, gate, up = wide
    oc, qc, os, qs, ks, vs, kc, vc = pieces
    return (
        *[value[None] for value in kept], *gain_grads,
        qs.T, ks.T, vs.T, os, qc.T, kc.T, vc.T, oc, gate, up, down, position,
    )


def solution(mesh):
    rows = P("dp", None, None)
    encoder = P("dp", "tensor", None)
    columns, lines, whole = P(None, "tensor"), P("tensor", None), P()
    head_table = P(None, None, "tensor")
    weights = (columns, columns, columns, lines, columns, columns, columns, lines, columns, columns, lines, head_table)
    return jax.shard_map(
        functools.partial(shards, (mesh.shape["dp"], mesh.shape["tensor"])),
        mesh=mesh,
        in_specs=(rows, encoder, rows, P("dp"), P("dp", None), whole, whole, whole, whole) + weights,
        out_specs=(rows, rows, encoder, whole, whole, whole) + weights,
        check_vma=False,
    )
```

```python
import functools
from types import SimpleNamespace

import jax
import jax.numpy as jnp
from jax import lax
from jax.experimental import pallas as pl
from jax.experimental.pallas import tpu as pltpu
from jax.sharding import PartitionSpec as P

DH = 64
EPS = 1e-06
NEG = -1000000000.0
TILE = 256
MESH = pl.DeviceIdType.MESH
BF = jnp.bfloat16
F32 = jnp.float32
VMEM = pl.BlockSpec(memory_space=pltpu.VMEM)
SMEM = pl.BlockSpec(memory_space=pltpu.SMEM)
ANY = pl.BlockSpec(memory_space=pl.ANY)
GELU_SCALE = 0.7978845608028654
GELU_CUBIC = 0.044715


IN_X = (True, True, True, True, False, False, True, True, True)
SCHEDULE = (
    (),
    (),
    ((2, 0), (9, 0),),
    (),
    ((1, 0), (3, 0), (0, 0),),
    (),
    ((4, 0),),
    (),
    (),
    ((9, 1),),
    (),
    (),
    ((4, 1), (9, 2), (1, 1),),
    ((3, 1),),
    (),
    ((9, 3), (1, 2), (4, 2),),
    (),
    ((7, 0), (0, 1), (3, 2), (1, 3),),
    (),
    (),
    ((10, 0), (4, 3),),
    ((5, 0), (0, 2), (7, 1), (6, 0), (3, 3),),
    (),
    ((1, 4), (10, 1),),
    (),
    ((0, 3),),
    ((8, 0), (3, 4), (6, 1), (2, 1),),
    ((5, 1), (0, 4), (10, 2),),
    ((4, 4), (6, 2),),
    ((7, 2),),
    ((2, 2), (5, 2), (6, 3), (3, 5), (8, 1), (7, 3), (10, 3), (8, 2), (2, 3),),
    ((6, 4), (8, 3), (7, 4), (10, 4), (2, 4), (5, 3), (1, 5), (9, 4), (6, 5), (8, 4), (10, 5),),
    ((4, 5), (5, 4), (9, 5), (7, 5),),
    (),
    ((0, 5), (2, 5), (5, 5), (8, 5),),
)


def nn(left, right):
    return lax.dot_general(left, right, (((1,), (0,)), ((), ())), preferred_element_type=F32)


def nt(left, right):
    return lax.dot_general(left, right, (((1,), (1,)), ((), ())), preferred_element_type=F32)


def tn(left, right):
    return lax.dot_general(left, right, (((0,), (0,)), ((), ())), preferred_element_type=F32)


def span(start, size, step=None):
    return pl.ds(pl.multiple_of(start, step or size), size)


class Sems:
    def __init__(self, ref):
        self.ref, self.used = ref, 0

    def take(self):
        self.used += 1
        assert self.used <= self.ref.shape[0]
        return self.ref.at[self.used - 1]


class Wire:
    def __init__(self, sems, src, dst, device):
        self.copy = pltpu.make_async_remote_copy(
            src_ref=src, dst_ref=dst, send_sem=sems.take(), recv_sem=sems.take(), device_id=device, device_id_type=MESH
        )

    def start(self):
        self.copy.start()

    def sent(self):
        self.copy.wait_send()

    def came(self):
        self.copy.wait_recv()

    def wait(self):
        self.copy.wait()


class TensorSum:
    def __init__(self, sems, place, src, near, half, far, out):
        self.src, self.near, self.half, self.far, self.out = src, near, half, far, out
        size = src.shape[0] // 2
        self.mine = span(place.core * size, size)
        other = span((1 - place.core) * size, size)
        self.first = Wire(sems, src.at[other], near, place.mate)
        self.second = Wire(sems, half, far, place.across)
        self.third = Wire(sems, out.at[self.mine], out.at[self.mine], place.mate)

    def one(self):
        self.first.start()

    def two(self):
        self.first.wait()
        self.half[...] = (self.src[self.mine].astype(F32) + self.near[...].astype(F32)).astype(BF)
        self.second.start()

    def three(self):
        self.second.wait()
        self.out[self.mine] = (self.half[...].astype(F32) + self.far[...].astype(F32)).astype(BF)
        self.third.start()

    def four(self):
        self.third.wait()


class TensorMix:
    def __init__(self, sems, place, mix, stat, bufs, out, total):
        self.place, self.mix, self.stat, self.out, self.total = place, mix, stat, out, total
        near, half, far, near_stat, half_stat, far_stat = bufs
        self.bufs = bufs
        size, core = mix.shape[0] // 2, place.core
        self.size = size
        self.mine, other = span(core * size, size), span((1 - core) * size, size)
        self.mine_stat, other_stat = span(core * 8, 8), span((1 - core) * 8, 8)
        self.first = [
            Wire(sems, mix.at[other], near, place.mate),
            Wire(sems, stat.at[other_stat], near_stat, place.mate),
        ]
        self.second = [Wire(sems, half, far, place.across), Wire(sems, half_stat, far_stat, place.across)]
        self.third = [
            Wire(sems, out.at[self.mine], out.at[self.mine], place.mate),
            Wire(sems, total.at[self.mine_stat], total.at[self.mine_stat], place.mate),
        ]

    def join(self, ours, theirs, ours_stat, theirs_stat, flip, store):
        low_stat = jnp.where(flip, theirs_stat, ours_stat)
        high_stat = jnp.where(flip, ours_stat, theirs_stat)
        top = jnp.maximum(low_stat, high_stat)
        total = top + jnp.log(jnp.exp(low_stat - top) + jnp.exp(high_stat - top))
        low_share, high_share = jnp.exp(low_stat - total), jnp.exp(high_stat - total)
        for h in range(self.size // DH):
            rows = slice(h * DH, (h + 1) * DH)
            a, b = ours(rows), theirs(rows)
            low, high = jnp.where(flip, b, a), jnp.where(flip, a, b)
            store(rows, (low * low_share[h : h + 1] + high * high_share[h : h + 1]).astype(BF))
        return total

    def one(self):
        for wire in self.first:
            wire.start()

    def two(self):
        near, half, far, near_stat, half_stat, far_stat = self.bufs
        core, size = self.place.core, self.size
        for wire in self.first:
            wire.wait()

        def ours(rows):
            return self.mix[span(core * size + rows.start, DH)].astype(F32)

        def store(rows, value):
            half[rows] = value

        half_stat[...] = self.join(
            ours, lambda rows: near[rows].astype(F32), self.stat[self.mine_stat], near_stat[...], core == 1, store
        )
        for wire in self.second:
            wire.start()

    def three(self):
        near, half, far, near_stat, half_stat, far_stat = self.bufs
        core, size = self.place.core, self.size
        for wire in self.second:
            wire.wait()

        def store(rows, value):
            self.out[span(core * size + rows.start, DH)] = value

        self.total[self.mine_stat] = self.join(
            lambda rows: half[rows].astype(F32),
            lambda rows: far[rows].astype(F32),
            half_stat[...],
            far_stat[...],
            self.place.side == 1,
            store,
        )
        for wire in self.third:
            wire.start()

    def four(self):
        for wire in self.third:
            wire.wait()


class WeightGather:
    def __init__(self, sems, place, own, whole, local):
        rows = own.shape[0]
        half = rows // 2
        me, core, side, x = place.me, place.core, place.side, place.x
        there = (1 - side) * 2 + core
        self.own, self.whole = own, whole
        mine = span(me * rows, rows)
        direct = span(there * rows + x * half, half)
        relayed = span(there * rows + (1 - x) * half, half)
        self.across = Wire(sems, own.at[span(x * half, half)], whole.at[span(me * rows + x * half, half)], place.across)
        self.mate = Wire(sems, own, whole.at[mine], place.mate)
        self.side = Wire(sems, whole.at[direct], whole.at[direct], place.beside)
        self.direct = Wire(sems, whole.at[direct], whole.at[direct], place.mate)
        self.relayed = Wire(sems, whole.at[relayed], whole.at[relayed], place.mate)
        self.keep = pltpu.make_async_copy(own, whole.at[mine], local)

    def start(self):
        self.across.start()
        self.mate.start()
        self.keep.start()

    def one(self):
        self.across.came()
        self.side.start()
        self.direct.start()

    def two(self):
        self.side.came()
        self.relayed.start()

    def three(self):
        self.mate.came()
        self.keep.wait()
        self.direct.came()
        self.relayed.came()

    def end(self):
        for wire in (self.across, self.mate, self.side, self.direct, self.relayed):
            wire.sent()


class QueryGather:
    def __init__(self, sems, place, own, whole):
        rows = own.shape[0]
        there = (1 - place.side) * 2 + place.core
        self.own, self.whole, self.mine = own, whole, span(place.me * rows, rows)
        self.across = Wire(sems, own, whole.at[self.mine], place.across)
        self.mate = Wire(sems, own, whole.at[self.mine], place.mate)
        theirs = whole.at[span(there * rows, rows)]
        self.onward = Wire(sems, theirs, theirs, place.mate)

    def one(self):
        self.across.start()
        self.mate.start()
        self.whole[self.mine] = self.own[...]

    def two(self):
        self.across.came()
        self.onward.start()

    def three(self):
        self.mate.came()
        self.onward.came()

    def end(self):
        for wire in (self.across, self.mate, self.onward):
            wire.sent()


class ChunkX:
    def __init__(self, sems, place, g, out, bufs):
        self.place = place
        near, inn, mid, tot, fin = self.bufs = bufs
        half = g.shape[0] // 2
        x = place.x
        self.g, self.mine = g, span(x * half, half)
        other = span((1 - x) * half, half)
        self.rs = Wire(sems, g.at[other], near, place.beside)
        self.out = Wire(sems, g.at[self.mine], inn, place.pair)
        self.middle = Wire(sems, g.at[self.mine], mid, place.middle)
        self.back = Wire(sems, tot, tot, place.pair)
        self.ag = Wire(sems, tot, fin, place.beside)
        self.save = [
            pltpu.make_async_copy(tot, out.at[self.mine], sems.take()),
            pltpu.make_async_copy(fin, out.at[other], sems.take()),
        ]

    def s0(self):
        self.rs.start()

    def s1(self):
        self.rs.wait()
        self.g[self.mine] = self.g[self.mine] + self.bufs[0][...]

        @pl.when(self.place.end)
        def _():
            self.out.start()

    def s2(self):
        @pl.when(self.place.inner)
        def _():
            self.out.came()
            self.g[self.mine] = self.g[self.mine] + self.bufs[1][...]
            self.middle.start()

    def s3(self):
        @pl.when(self.place.inner)
        def _():
            self.middle.wait()
            self.bufs[3][...] = self.g[self.mine] + self.bufs[2][...]
            self.back.start()
            self.ag.start()
            self.save[0].start()

    def s4(self):
        @pl.when(self.place.end)
        def _():
            self.back.came()
            self.ag.start()
            self.save[0].start()

    def s5(self):
        self.ag.came()
        self.save[1].start()

    def finish(self):
        @pl.when(self.place.end)
        def _():
            self.out.sent()

        @pl.when(self.place.inner)
        def _():
            self.back.sent()

        self.ag.sent()
        for copy in self.save:
            copy.wait()


class ChunkZ:
    def __init__(self, sems, place, g, out, bufs):
        self.place = place
        inn, mid, r, xr, tot = self.bufs = bufs
        half = g.shape[0] // 2
        at = place.high
        self.g, self.mine = g, span(at * half, half)
        self.other = span((1 - at) * half, half)
        self.out = Wire(sems, g, inn, place.pair)
        self.rs = Wire(sems, g.at[self.other], mid, place.middle)
        self.x = Wire(sems, r, xr, place.beside)
        self.ag = Wire(sems, tot.at[self.mine], tot.at[self.mine], place.middle)
        self.back = [
            Wire(sems, tot.at[self.mine], tot.at[self.mine], place.pair),
            Wire(sems, tot.at[self.other], tot.at[self.other], place.pair),
        ]
        self.save = pltpu.make_async_copy(tot, out, sems.take())

    def s0(self):
        @pl.when(self.place.end)
        def _():
            self.out.start()

    def s1(self):
        @pl.when(self.place.inner)
        def _():
            self.out.came()
            self.g[...] = self.g[...] + self.bufs[0][...]
            self.rs.start()

    def s2(self):
        @pl.when(self.place.inner)
        def _():
            self.rs.wait()
            self.bufs[2][...] = self.g[self.mine] + self.bufs[1][...]
            self.x.start()

    def s3(self):
        @pl.when(self.place.inner)
        def _():
            self.x.wait()
            self.bufs[4][self.mine] = self.bufs[2][...] + self.bufs[3][...]
            self.ag.start()
            self.back[0].start()

    def s4(self):
        @pl.when(self.place.inner)
        def _():
            self.ag.came()
            self.back[1].start()
            self.save.start()

    def s5(self):
        @pl.when(self.place.end)
        def _():
            for wire in self.back:
                wire.came()
            self.save.start()

    def finish(self):
        @pl.when(self.place.end)
        def _():
            self.out.sent()

        @pl.when(self.place.inner)
        def _():
            self.ag.sent()
            for wire in self.back:
                wire.sent()

        self.save.wait()


class ChunkG:
    def __init__(self, sems, place, blocks, use=None):
        def wires(query, device):
            return [Wire(sems, block(query), block(query), device) for block in blocks]

        self.place, self.use = place, use
        first, second = place.far
        self.pair = wires(place.query, place.pair)
        self.x0 = wires(place.query, place.beside)
        self.x1 = wires(place.pair[0], place.beside)
        self.middle = wires(place.query, place.middle) + wires(place.pair[0], place.middle)
        self.back = wires(first, place.pair) + wires(second, place.pair)
        self.x2 = wires(first, place.beside) + wires(second, place.beside)

    def s0(self):
        for wire in self.pair + self.x0:
            wire.start()

    def s1(self):
        for wire in self.pair:
            wire.came()

        @pl.when(self.place.inner)
        def _():
            for wire in self.middle:
                wire.start()

        for wire in self.x1:
            wire.start()

    def s2(self):
        @pl.when(self.place.inner)
        def _():
            for wire in self.middle:
                wire.came()
            for wire in self.back + self.x2:
                wire.start()

    def s3(self):
        @pl.when(self.place.end)
        def _():
            for wire in self.back:
                wire.came()
            for wire in self.x2:
                wire.start()

    def s4(self):
        for wire in self.x0 + self.x1 + self.x2:
            wire.came()

    def s5(self):
        self.saves = self.use()

    def finish(self):
        for wire in self.pair + self.x0 + self.x1 + self.x2:
            wire.sent()

        @pl.when(self.place.inner)
        def _():
            for wire in self.middle + self.back:
                wire.sent()

        for copy in self.saves:
            copy.wait()


class SmallSum:
    def __init__(self, sems, place, bufs):
        self.place = place
        own, near, sum1, inn, sum2, mid, tot = self.bufs = bufs
        self.x = Wire(sems, own, near, place.beside)
        self.out = Wire(sems, sum1, inn, place.pair)
        self.middle = Wire(sems, sum2, mid, place.middle)
        self.back = Wire(sems, tot, tot, place.pair)

    def s0(self):
        self.x.start()

    def s1(self):
        own, near, sum1, inn, sum2, mid, tot = self.bufs
        self.x.wait()
        sum1[...] = own[...] + near[...]

        @pl.when(self.place.end)
        def _():
            self.out.start()

    def s2(self):
        own, near, sum1, inn, sum2, mid, tot = self.bufs

        @pl.when(self.place.inner)
        def _():
            self.out.came()
            sum2[...] = sum1[...] + inn[...]
            self.middle.start()

    def s3(self):
        own, near, sum1, inn, sum2, mid, tot = self.bufs

        @pl.when(self.place.inner)
        def _():
            self.middle.wait()
            tot[...] = sum2[...] + mid[...]
            self.back.start()
            self.back.sent()

    def s4(self):
        @pl.when(self.place.end)
        def _():
            self.out.sent()
            self.back.came()


def rms_scale(values):
    return lax.rsqrt(jnp.mean(values * values, axis=-1, keepdims=True) + EPS)


def norm_back(values, gain, dy):
    scale = rms_scale(values)
    normal = values * scale
    gain_grad = jnp.sum(dy * normal, axis=0, keepdims=True)
    pulled = dy * gain
    mean = jnp.mean(pulled * normal, axis=-1, keepdims=True)
    return scale * (pulled - normal * mean), gain_grad


def fold(values, op):
    rows, width = values.shape
    return op(values.reshape(rows // 8, 8, width), axis=0)


def chunk_plan(own, width, units):
    plan = [(a, k * (width // 2), width // 2) for a in (1, 2) for k in range(2)]
    plan += [(3, k * own, own) for k in (0, 1, 2, 6, 7)]
    return [(in_x, *block) for in_x, block in zip(IN_X, plan)]


def block_kernel(cfg, *refs):
    groups, at = [], 0
    for tree in cfg.trees:
        groups.append(SimpleNamespace(**jax.tree.unflatten(tree, refs[at : at + tree.num_leaves])))
        at += tree.num_leaves
    ins, outs, scr = groups
    heads, all_heads, width, tokens, rows = cfg.heads, cfg.all_heads, cfg.width, cfg.tokens, cfg.rows
    own, pairs, tiles = heads * DH, all_heads // 2, rows // TILE
    summing = cfg.summing
    sems = Sems(scr.sems)
    dp, me = lax.axis_index("dp"), lax.axis_index("tensor")
    core, side = lax.rem(me, 2), me // 2
    x, z = lax.rem(dp, 2), dp // 2
    place = SimpleNamespace(
        me=me,
        core=core,
        side=side,
        x=x,
        mate=(dp, side * 2 + 1 - core),
        across=(dp, (1 - side) * 2 + core),
        beside=(dp + 1 - 2 * x, me),
    )
    barrier = pltpu.get_barrier_semaphore()
    for friend in (place.mate, place.across, place.beside):
        pl.semaphore_signal(barrier, inc=1, device_id=friend, device_id_type=MESH)
    if summing:
        inner = jnp.logical_or(z == 1, z == 2)
        place.inner, place.end = inner, jnp.logical_not(inner)
        place.high = z // 2
        place.pair = ((z + 1 - 2 * lax.rem(z, 2)) * 2 + x, me)
        place.middle = ((3 - z) * 2 + x, me)
        place.query = dp
        place.far = ((2 - z // 2) * 2 + x, 3 * (1 - z // 2) * 2 + x)
        pl.semaphore_signal(barrier, inc=1, device_id=place.pair, device_id_type=MESH)

        @pl.when(inner)
        def _():
            pl.semaphore_signal(barrier, inc=1, device_id=place.middle, device_id_type=MESH)

    def fetch(src, dst):
        copy = pltpu.make_async_copy(src, dst, sems.take())
        copy.start()
        return copy

    enc, down, gate_w, up_w = scr.enc, scr.down, scr.gate_w, scr.up_w
    first_loads = [fetch(ins.x, scr.x)] + [fetch(src, dst) for src, dst in zip(ins.gains, scr.gains)]
    self_weights = scr.wqkv
    for src, dst in zip((ins.wq_self, ins.wk_self, ins.wv_self), self_weights):
        first_loads.append(fetch(src, dst))
    load_bucket, load_out = fetch(ins.bucket, scr.bucket), fetch(ins.wo_self, scr.wo_self)
    load_small = [fetch(ins.mask, scr.mask), fetch(ins.group, scr.group), fetch(ins.table, scr.table)]
    load_query = fetch(ins.wq_cross, scr.wq_own)
    load_enc = fetch(ins.encoder, enc)
    load_ffn = [fetch(ins.out_grad, scr.og), fetch(ins.down_w, down), fetch(ins.gate_w, gate_w), fetch(ins.up_w, up_w)]

    for load in first_loads:
        load.wait()
    gain_self, gain_cross, gain_ffn = (gain[...].reshape(1, width) for gain in scr.gains)
    xv = scr.x[...].astype(F32)
    self_in = scr.self_in
    self_in[...] = (xv * rms_scale(xv) * gain_self).astype(BF)
    qkv = scr.qkv
    for k, weight in enumerate(self_weights):
        qkv[k * own : (k + 1) * own] = nt(weight[...], self_in[...]).astype(BF)
    if summing:
        pl.semaphore_wait(barrier, 4 + inner.astype(jnp.int32))
    else:
        pl.semaphore_wait(barrier, 3)
    wk, wq, wv, wo = scr.wk, scr.wq, scr.wv, scr.wo
    get_k, get_q, get_v, get_o = gathers = [
        WeightGather(sems, place, part, whole, sems.take())
        for part, whole in ((ins.wk_cross, wk), (ins.wq_cross, wq), (ins.wv_cross, wv), (ins.wo_cross, wo))
    ]
    get_k.start()
    if summing:
        lanes_half = span(core * (width // 2), width // 2, 2 * DH)
        og_all, self_all, hidden_all, d_qkv_all = scr.gathered

        def rows_of(query):
            return span(query * tokens, tokens)

        load_ffn[0].wait()
        og_all[rows_of(dp), lanes_half] = scr.og[:, lanes_half]
        self_all[rows_of(dp), lanes_half] = self_in[:, lanes_half]
        early = ChunkG(
            sems,
            place,
            [lambda query: og_all.at[rows_of(query), lanes_half], lambda query: self_all.at[rows_of(query), lanes_half]],
            lambda: [],
        )
        shares = [Wire(sems, ref.at[:, lanes_half], ref.at[:, lanes_half], place.mate) for ref in (og_all, self_all)]
        early.s0()
    load_bucket.wait()
    for load in load_small:
        load.wait()
    scr.bucket[...] = scr.bucket[...].T
    bucket = scr.bucket
    keep = jnp.broadcast_to(scr.mask[...].astype(F32), (tokens, tokens)).T
    j_at = lax.broadcasted_iota(jnp.int32, (tokens, tokens), 0)
    i_at = lax.broadcasted_iota(jnp.int32, (tokens, tokens), 1)
    allowed = jnp.logical_or(jnp.logical_and(j_at <= i_at, keep == 1.0), j_at == i_at)
    group = scr.group[0]
    buckets = cfg.buckets
    for h in range(heads):
        scr.p_self[h] = jnp.full((tokens, tokens), NEG, F32)

    def spread(b, _):
        hit = jnp.logical_and(bucket[...] == b, allowed)
        for h in range(heads):
            scr.p_self[h] = jnp.where(hit, scr.table[h, group, b], scr.p_self[h])
        return 0

    lax.fori_loop(0, buckets, spread, 0)
    att_self = scr.att_self

    def attend(h):
        q = qkv[h * DH : (h + 1) * DH]
        k = qkv[own + h * DH : own + (h + 1) * DH]
        v = qkv[2 * own + h * DH : 2 * own + (h + 1) * DH]
        s = tn(k, q) + scr.p_self[h]
        e = jnp.exp(s - jnp.max(s, axis=0, keepdims=True))
        p = e / jnp.sum(e, axis=0, keepdims=True)
        scr.p_self[h] = p
        att_self[h * DH : (h + 1) * DH] = nn(v, p.astype(BF)).astype(BF)

    for h in range(heads):
        attend(h)

    def tensor_sum(bufs):
        return TensorSum(sems, place, *bufs)

    s1 = tensor_sum(scr.s1)
    load_out.wait()
    s1.src[...] = tn(att_self[...], scr.wo_self[...]).astype(BF)
    s1.one()
    s1.two()
    get_v.start()
    bq, bw = scr.bq, scr.bw
    for ref in (bq, bw, scr.stat, scr.top, scr.small[0], scr.bucket_rows):
        ref[...] = jnp.zeros(ref.shape, ref.dtype)
    get_k.one()
    load_enc.wait()
    if summing:
        early.s1()
    kc, vc, e_ref = scr.kc, scr.vc, scr.e

    def project(dst, weight):
        def body(r, _):
            at = span(r * TILE, TILE)
            dst[at] = nt(enc[at], weight[...]).astype(BF)
            return 0

        lax.fori_loop(0, tiles, body, 0)

    s1.three()
    s1.four()
    x2 = scr.x2
    x2[...] = scr.x[...].astype(F32) + s1.out[...].astype(F32)
    cross_in = scr.cross_in
    cross_in[...] = (x2[...] * rms_scale(x2[...]) * gain_cross).astype(BF)
    load_query.wait()
    scr.q_own[...] = nt(scr.wq_own[...], cross_in[...]).astype(BF)
    get_query = QueryGather(sems, place, scr.q_own, scr.q_t)
    get_query.one()
    get_o.start()
    get_q.start()
    get_k.two()
    get_v.one()
    get_k.three()
    project(kc, wk)
    get_query.two()
    get_query.three()
    for h in range(all_heads):
        at = slice(h * DH, (h + 1) * DH)
        bq[at, (h % 2) * tokens : (h % 2 + 1) * tokens] = scr.q_t[at]
    s_ref, mix, stat, top_ref = scr.s, scr.mix, scr.stat, scr.top
    per_half = pairs // 2

    def stat_row(p):
        return (p // per_half) * 8 + 2 * (p - (p // per_half) * per_half)

    def score_pair(p, _):
        head_at = span(p * 2 * DH, 2 * DH)
        score_at = span(p * 2 * tokens, 2 * tokens)
        weights = bq[head_at]
        top = None
        for r in range(tiles):
            at = slice(r * TILE, (r + 1) * TILE)
            s = nn(kc[at, head_at], weights)
            s_ref[at] = s
            part = fold(s, jnp.max)
            top = part if top is None else jnp.maximum(top, part)
        top = jnp.max(top, axis=0, keepdims=True)
        total = None
        for r in range(tiles):
            at = slice(r * TILE, (r + 1) * TILE)
            e = jnp.exp(s_ref[at] - top)
            part = fold(e, jnp.sum)
            total = part if total is None else total + part
            e_ref[at, score_at] = e.astype(BF)
        total = jnp.sum(total, axis=0, keepdims=True)
        scr.inverse[pl.ds(p, 1)] = 1.0 / total
        lse = top + jnp.log(total)
        row = stat_row(p)
        for k in range(2):
            lanes = slice(k * tokens, (k + 1) * tokens)
            stat[pl.ds(row + k, 1)] = lse[:, lanes]
            top_ref[pl.ds(row + k, 1)] = top[:, lanes]
        return 0

    def mix_pair(p, _):
        acc = tn(vc[:, span(p * 2 * DH, 2 * DH)], e_ref[:, span(p * 2 * tokens, 2 * tokens)])
        inverse = scr.inverse[pl.ds(p, 1)]
        for k in range(2):
            lanes = slice(k * tokens, (k + 1) * tokens)
            value = acc[k * DH : (k + 1) * DH, lanes] * inverse[:, lanes]
            mix[span(p * 2 * DH + k * DH, DH)] = value.astype(BF)
        return 0

    lax.fori_loop(0, pairs - 2, score_pair, 0)
    get_v.two()
    get_o.one()
    if summing:
        early.s2()
    lax.fori_loop(pairs - 2, pairs, score_pair, 0)
    get_v.three()
    att, lse = scr.att, scr.lse
    s2 = TensorMix(sems, place, mix, stat, scr.mix_bufs, att, lse)
    project(vc, wv)
    for half in (1 - core, core):
        lax.fori_loop(half * per_half, (half + 1) * per_half, mix_pair, 0)
        if half is not core:
            s2.one()
            get_q.one()
    s2.two()
    for load in load_ffn[1 if summing else 0 :]:
        load.wait()
    og = scr.og
    scr.d_hidden[...] = nt(og[...], down[...]).astype(BF).astype(F32)
    get_o.two()
    s2.three()
    get_o.three()
    s2.four()
    if summing:
        early.s3()
    x3 = scr.x3
    x3[...] = x2[...] + tn(att[...], wo[...])
    ffn_in = scr.ffn_in
    ffn_in[...] = (x3[...] * rms_scale(x3[...]) * gain_ffn).astype(BF)
    gate = nn(ffn_in[...], gate_w[...])
    up = nn(ffn_in[...], up_w[...])
    squared = gate * gate
    curve = jnp.tanh(GELU_SCALE * (gate + GELU_CUBIC * (squared * gate)))
    gelu = 0.5 * gate * (1.0 + curve)
    slope = 0.5 * (1.0 + curve) + 0.5 * gate * (1.0 - curve * curve) * (
        GELU_SCALE * (1.0 + 3.0 * GELU_CUBIC * squared)
    )
    d_hidden = scr.d_hidden[...]
    scr.hidden[...] = (gelu * up).astype(BF)
    scr.d_gate[...] = (d_hidden * up * slope).astype(BF)
    scr.d_up[...] = (d_hidden * gelu).astype(BF)

    g_down, g_gate, g_up, g_small = scr.grads
    chunks = []
    if summing:
        def use_hidden():
            g_down[...] = tn(hidden_all[...], og_all[...]).astype(BF)
            return [fetch(g_down, outs.grads[0])]

        def use_d_qkv():
            whole = jnp.concatenate([d_qkv_all[k] for k in range(cfg.queries)], axis=1)
            g_small[3 * own : 6 * own] = nn(whole, self_all[...]).astype(BF)
            at = pl.ds(3 * own, 3 * own)
            return [fetch(g_small.at[at], outs.grads[3].at[at])]

        for (in_x, source, start, size), bufs in zip(cfg.chunks, scr.chunks):
            rows_at = pl.ds(start, size)
            maker = ChunkX if in_x else ChunkZ
            chunks.append(maker(sems, place, scr.grads[source].at[rows_at], outs.grads[source].at[rows_at], bufs))
        chunks.append(ChunkG(sems, place, [lambda query: hidden_all.at[rows_of(query)]], use_hidden))
        chunks.append(ChunkG(sems, place, [lambda query: d_qkv_all.at[query]], use_d_qkv))
    schedule = iter(cfg.schedule)

    def poll():
        if summing:
            for n, k in next(schedule):
                chunk = chunks[n]
                (chunk.s0, chunk.s1, chunk.s2, chunk.s3, chunk.s4, chunk.s5)[k]()

    if summing:
        hidden_all[rows_of(dp)] = scr.hidden[...]
    else:
        g_down[...] = tn(scr.hidden[...], og[...]).astype(BF)
    poll()
    g_gate[...] = tn(ffn_in[...], scr.d_gate[...]).astype(BF)
    poll()
    g_up[...] = tn(ffn_in[...], scr.d_up[...]).astype(BF)
    poll()
    s3, so = tensor_sum(scr.s3), tensor_sum(scr.so)
    s3.src[...] = (nt(scr.d_gate[...], gate_w[...]) + nt(scr.d_up[...], up_w[...])).astype(BF)
    s3.one()
    so.src[...] = nn(scr.hidden[...], down[...]).astype(BF)
    s3.two()
    poll()
    get_q.two()
    poll()
    s3.three()
    so.one()
    s3.four()
    so.two()
    poll()
    g2, g2_low = scr.g2, scr.g2_low
    dv, gain_grad = norm_back(x3[...], gain_ffn, s3.out[...].astype(F32))
    g2[...] = og[...].astype(F32) + dv
    g2_low[...] = g2[...].astype(BF)
    small = scr.small[0]
    small[2:3, :width] = gain_grad
    g_small[0:own] = nn(att[span(me * own, own)], g2_low[...]).astype(BF)
    poll()
    d_att = nt(wo[...], g2_low[...])
    delta_ref = scr.delta
    for h in range(all_heads):
        at = slice(h * DH, (h + 1) * DH)
        p, k = divmod(h, 2)
        row = (p // per_half) * 8 + 2 * (p % per_half) + k
        share = jnp.exp(top_ref[row : row + 1] - lse[row : row + 1])
        low = (d_att[at] * share).astype(BF)
        bw[at, k * tokens : (k + 1) * tokens] = low
        delta_ref[p : p + 1, k * tokens : (k + 1) * tokens] = jnp.sum(
            low.astype(F32) * att[at].astype(F32), axis=0, keepdims=True
        )
    so.three()
    s4 = tensor_sum(scr.s4)

    def backward_pair(p, _):
        head_at = span(p * 2 * DH, 2 * DH)
        score_at = span(p * 2 * tokens, 2 * tokens)
        wq_block, wa_block = bq[head_at], bw[head_at]
        delta = delta_ref[pl.ds(p, 1)]
        acc = None
        for r in range(tiles):
            at = slice(r * TILE, (r + 1) * TILE)
            e = e_ref[at, score_at]
            grad = nn(vc[at, head_at], wa_block)
            ds = (e.astype(F32) * (grad - delta)).astype(BF)
            part = tn(kc[at, head_at], ds)
            acc = part if acc is None else acc + part
            kc[at, head_at] = nt(ds, wq_block).astype(BF)
            vc[at, head_at] = nt(e, wa_block).astype(BF)
        for k in range(2):
            value = acc[k * DH : (k + 1) * DH, k * tokens : (k + 1) * tokens]
            s4.src[span(p * 2 * DH + k * DH, DH)] = value.astype(BF)
        return 0

    far_at, near_at = (1 - side) * per_half, side * per_half
    far_parts, near_parts = scr.far_parts, scr.near_parts
    kv_near, kv_home, kv_half, kv_far = scr.kv_near, scr.kv_home, scr.kv_half, scr.kv_far
    to_mate, to_across, to_home = [], [], []
    mine, other = span(core * own, own), span((1 - core) * own, own)
    for a in range(2):
        to_mate.append(Wire(sems, far_parts[a].at[other], kv_near.at[a], place.mate))
        to_across.append(Wire(sems, kv_half.at[a], kv_far.at[a], place.across))
        to_home.append(Wire(sems, near_parts[a].at[other], kv_home.at[a], place.mate))

    def weight_part(dst, source, first):
        rows_of = source[:, span(first * 2 * DH, 2 * own, 2 * DH)]

        def body(t, _):
            lanes = span(t * TILE, TILE)
            dst[:, lanes] = tn(rows_of, enc[:, lanes]).astype(BF)
            return 0

        lax.fori_loop(0, width // TILE, body, 0)

    def pass_across(a):
        to_mate[a].wait()
        kv_half[a] = (far_parts[a][mine].astype(F32) + kv_near[a].astype(F32)).astype(BF)
        to_across[a].start()

    if summing:
        early.s4()
        early.s5()
        for wire in shares:
            wire.start()
    for p in range(per_half):
        poll()
        lax.fori_loop(far_at + p, far_at + p + 1, backward_pair, 0)
    poll()
    so.four()
    scr.out_stage[...] = (x3[...] + so.out[...].astype(F32)).astype(BF)
    token_saves = [fetch(scr.out_stage, outs.block_out)]
    if summing:
        for wire in shares:
            wire.came()
    weight_part(far_parts[0], kc, far_at)
    to_mate[0].start()
    weight_part(far_parts[1], vc, far_at)
    to_mate[1].start()
    pass_across(0)
    for p in range(per_half):
        poll()
        lax.fori_loop(near_at + p, near_at + p + 1, backward_pair, 0)
    s4.one()
    poll()
    weight_part(near_parts[0], kc, near_at)
    to_home[0].start()
    s4.two()
    pass_across(1)
    poll()
    weight_part(near_parts[1], vc, near_at)
    to_home[1].start()
    s4.three()
    poll()

    def kv_done(a):
        to_home[a].wait()
        to_across[a].wait()
        total = near_parts[a][mine].astype(F32) + kv_home[a].astype(F32) + kv_far[a].astype(F32)
        g_small[(6 + a) * own : (7 + a) * own] = total.astype(BF)

    kv_done(0)
    s4.four()
    poll()
    get_q.three()
    d_cross = tn(s4.out[...], wq[...])
    dv, gain_grad = norm_back(x2[...], gain_cross, d_cross)
    small[1:2, :width] = gain_grad
    g1, g1_low = scr.g1, scr.g1_low
    g1[...] = g2[...] + dv
    g1_low[...] = g1[...].astype(BF)
    g_small[own : 2 * own] = nn(s4.out[span(me * own, own)], cross_in[...]).astype(BF)
    g_small[2 * own : 3 * own] = nn(att_self[...], g1_low[...]).astype(BF)
    poll()
    d_att_self = nt(scr.wo_self[...], g1_low[...]).astype(BF)
    d_qkv = scr.d_qkv
    for h in range(heads):
        at = slice(h * DH, (h + 1) * DH)
        q = qkv[h * DH : (h + 1) * DH]
        k = qkv[own + h * DH : own + (h + 1) * DH]
        v = qkv[2 * own + h * DH : 2 * own + (h + 1) * DH]
        p = scr.p_self[h]
        grad = tn(v, d_att_self[at])
        ds = (p * (grad - jnp.sum(p * grad, axis=0, keepdims=True))).astype(BF)
        scr.ds_self[h] = ds.astype(F32)
        d_qkv[h * DH : (h + 1) * DH] = nn(k, ds).astype(BF)
        d_qkv[own + h * DH : own + (h + 1) * DH] = nt(q, ds).astype(BF)
        d_qkv[2 * own + h * DH : 2 * own + (h + 1) * DH] = nt(d_att_self[at], p.astype(BF)).astype(BF)
    poll()
    if summing:
        d_qkv_all[dp] = d_qkv[...]
    else:
        g_small[3 * own : 6 * own] = nn(d_qkv[...], self_in[...]).astype(BF)
    poll()
    s5 = tensor_sum(scr.s5)
    total = None
    for k, weight in enumerate(self_weights):
        part = tn(d_qkv[k * own : (k + 1) * own], weight[...])
        total = part if total is None else total + part
    s5.src[...] = total.astype(BF)
    s5.one()
    poll()
    rows_ref = scr.bucket_rows

    def count(b, _):
        hit = bucket[...] == b
        for h in range(heads):
            value = jnp.where(hit, scr.ds_self[h], 0.0)
            rows_ref[pl.ds(h * buckets + b, 1)] = jnp.sum(value, axis=0, keepdims=True)
        return 0

    s5.two()
    lax.fori_loop(0, buckets, count, 0)
    position = jnp.sum(rows_ref[...].T, axis=0, keepdims=True)
    for g in range(cfg.groups):
        hot = jnp.where(group == g, 1.0, 0.0).astype(F32)
        small[8 + g : 9 + g, :tokens] = position * hot
    poll()

    saves = [None, None]

    def encoder_tile(r):
        at = slice(r * TILE, (r + 1) * TILE)
        slot = r % 2
        if saves[slot] is not None:
            saves[slot].wait()
        stage = scr.stage.at[slot]
        stage[...] = (nn(kc[at], wk[...]) + nn(vc[at], wv[...])).astype(BF)
        saves[slot] = fetch(stage, outs.encoder_grad.at[pl.ds(r * TILE, TILE)])

    for r in range(tiles // 2):
        encoder_tile(r)
        poll()
    kv_done(1)
    poll()
    s5.three()
    for r in range(tiles // 2, tiles):
        encoder_tile(r)
        poll()
    s5.four()
    dv, gain_grad = norm_back(scr.x[...].astype(F32), gain_self, s5.out[...].astype(F32))
    scr.og[...] = (g1[...] + dv).astype(BF)
    token_saves.append(fetch(scr.og, outs.decoder_grad))
    small[0:1, :width] = gain_grad
    for copy in saves + token_saves:
        copy.wait()
    if summing:
        little = SmallSum(sems, place, scr.small)
        little.s0()
        poll()
        little.s1()
        poll()
        little.s2()
        poll()
        little.s3()
        poll()
        little.s4()
        last = fetch(little.bufs[6], outs.small_sum)
        poll()
        for chunk in chunks + [early]:
            chunk.finish()
        for wire in shares:
            wire.sent()
    else:
        for copy in [fetch(src, dst) for src, dst in zip(scr.grads, outs.grads)]:
            copy.wait()
        last = fetch(small, outs.small_sum)
    last.wait()
    for gather in gathers + [get_query]:
        gather.end()


def finish_kernel(own, buckets, heads, groups, ins, outs, scr):
    used = [0]

    def copy(src, dst):
        made = pltpu.make_async_copy(src, dst, scr.sems.at[used[0]])
        used[0] += 1
        made.start()
        return made

    loads = [copy(src, dst) for src, dst in zip(ins.grads, scr.low)]
    moves = [copy(src, dst) for src, dst in zip(ins.kept, scr.kept)]
    keeps = []
    for k in range(3):
        outs.gains[k][...] = ins.little[k : k + 1].reshape(outs.gains[k].shape)
    for h in range(heads):
        outs.position[h] = ins.little[8 : 8 + groups, h * buckets : (h + 1) * buckets]
    for k in range(3):
        loads[k].wait()
        scr.wide[k][...] = scr.low[k][...].astype(F32)
        keeps.append(copy(scr.wide[k], outs.wide[k]))
    loads[3].wait()
    for k, out in enumerate(outs.pieces):
        at = slice(k * own, (k + 1) * own)
        scr.wide[3][at] = scr.low[3][at].astype(F32)
        keeps.append(copy(scr.wide[3].at[at], out))
    for k, move in enumerate(moves):
        move.wait()
        keeps.append(copy(scr.kept[k], outs.kept[k]))
    for made in keeps:
        made.wait()


def shards(
    mesh_shape,
    decoder_in,
    encoder_out,
    out_grad,
    group_ids,
    target_mask,
    bucket_ids,
    gain_self,
    gain_cross,
    gain_ffn,
    query_self,
    key_self,
    value_self,
    output_self,
    query_cross,
    key_cross,
    value_cross,
    output_cross,
    gate_weight,
    up_weight,
    down_weight,
    position_bias,
):
    dp_size, tensor_size = mesh_shape
    query_count, tokens, width = decoder_in.shape
    assert query_count == 1 and tensor_size == 4 and dp_size % 2 == 0
    heads = query_self.shape[1] // DH
    own, all_heads = heads * DH, heads * tensor_size
    groups, buckets, _ = position_bias.shape
    rows, units = encoder_out.shape[1], gate_weight.shape[1]
    summing = dp_size == 8

    def vmem(*shape, kind=BF):
        return pltpu.VMEM(shape, kind)

    def shape_of(*shape, kind=BF):
        return jax.ShapeDtypeStruct(shape, kind)

    inputs = dict(
        x=(decoder_in[0], ANY),
        out_grad=(out_grad[0], ANY),
        encoder=(encoder_out[0], ANY),
        group=(group_ids, ANY),
        mask=(target_mask, ANY),
        bucket=(bucket_ids, ANY),
        gains=[(gain_self, ANY), (gain_cross, ANY), (gain_ffn, ANY)],
        wq_self=(query_self.T, ANY),
        wk_self=(key_self.T, ANY),
        wv_self=(value_self.T, ANY),
        wo_self=(output_self, ANY),
        wq_cross=(query_cross.T, ANY),
        wk_cross=(key_cross.T, ANY),
        wv_cross=(value_cross.T, ANY),
        wo_cross=(output_cross, ANY),
        gate_w=(gate_weight, ANY),
        up_w=(up_weight, ANY),
        down_w=(down_weight, ANY),
        table=(jnp.transpose(position_bias, (2, 0, 1)), ANY),
    )
    grad_shapes = [(units, width), (width, units), (width, units), (8 * own, width)]
    outputs = dict(
        block_out=(shape_of(tokens, width), ANY),
        decoder_grad=(shape_of(tokens, width), ANY),
        encoder_grad=(shape_of(rows, width), ANY),
        grads=[(shape_of(*shape), ANY) for shape in grad_shapes],
        small_sum=(shape_of(16, width, kind=F32), ANY),
    )
    plan = chunk_plan(own, width, units)
    all_own = all_heads * DH

    def sum_bufs(count, lanes):
        return [vmem(size, lanes) for size in (count, count // 2, count // 2, count // 2, count)]

    def chunk_bufs(in_x, source, size):
        lanes = grad_shapes[source][1]
        full = () if in_x else (0, 4)
        return [vmem(size if k in full else size // 2, lanes) for k in range(5)]

    token_low, token_wide = vmem(tokens, width), vmem(tokens, width, kind=F32)
    stats, kv_block = vmem(16, tokens, kind=F32), vmem(2, own, width)
    halves = vmem(all_own // 2, tokens)
    scratch = dict(
        gains=[vmem(width, kind=F32)] * 3, mask=vmem(1, tokens, kind=jnp.int32),
        group=pltpu.SMEM((1,), jnp.int32), table=pltpu.SMEM((heads, groups, buckets), F32),
        x=token_low, og=token_low, out_stage=token_low, wqkv=[vmem(own, width)] * 3, wo_self=vmem(own, width), wq_own=vmem(own, width),
        q_own=vmem(own, tokens), q_t=vmem(all_own, tokens),
        enc=vmem(rows, width), down=vmem(units, width), gate_w=vmem(width, units), up_w=vmem(width, units),
        self_in=token_low, cross_in=token_low, ffn_in=token_low, g1_low=token_low, g2_low=token_low,
        x2=token_wide, x3=token_wide, g1=token_wide, g2=token_wide,
        qkv=vmem(3 * own, tokens), d_qkv=vmem(3 * own, tokens), att_self=vmem(own, tokens),
        bucket=vmem(tokens, tokens, kind=jnp.int32), bucket_rows=vmem(128, tokens, kind=F32),
        p_self=vmem(heads, tokens, tokens, kind=F32), ds_self=vmem(heads, tokens, tokens, kind=F32),
        wk=vmem(all_own, width), wq=vmem(all_own, width), wv=vmem(all_own, width), wo=vmem(all_own, width),
        bq=vmem(all_own, 2 * tokens), bw=vmem(all_own, 2 * tokens),
        kc=vmem(rows, all_own), vc=vmem(rows, all_own),
        e=vmem(rows, all_heads * tokens), s=vmem(rows, 2 * tokens, kind=F32),
        mix=vmem(all_own, tokens), att=vmem(all_own, tokens), stat=stats, top=stats, lse=stats,
        mix_bufs=[halves] * 3 + [vmem(8, tokens, kind=F32)] * 3,
        delta=vmem(8, 2 * tokens, kind=F32), inverse=vmem(8, 2 * tokens, kind=F32),
        d_hidden=vmem(tokens, units, kind=F32), hidden=vmem(tokens, units),
        d_gate=vmem(tokens, units), d_up=vmem(tokens, units),
        s1=sum_bufs(tokens, width), s3=sum_bufs(tokens, width), so=sum_bufs(tokens, width),
        s4=sum_bufs(all_own, tokens), s5=sum_bufs(tokens, width),
        far_parts=[vmem(2 * own, width)] * 2, near_parts=[vmem(2 * own, width)] * 2,
        kv_near=kv_block, kv_home=kv_block, kv_half=kv_block, kv_far=kv_block,
        stage=vmem(2, TILE, width),
        grads=[vmem(*shape) for shape in grad_shapes],
        small=[vmem(16, width, kind=F32)] * (7 if summing else 1),
        gathered=[vmem(dp_size * tokens, width)] * 2
        + [vmem(dp_size * tokens, units), vmem(dp_size, 3 * own, tokens)] if summing else [],
        chunks=[chunk_bufs(in_x, source, size) for in_x, source, _, size in plan] if summing else [],
        sems=pltpu.SemaphoreType.DMA((400,)),
    )
    pair = lambda entry: isinstance(entry, tuple)
    first = lambda tree: jax.tree.map(lambda entry: entry[0], tree, is_leaf=pair)
    second = lambda tree: jax.tree.map(lambda entry: entry[1], tree, is_leaf=pair)
    flat = jax.tree.leaves
    trees = [jax.tree.structure(first(inputs)), jax.tree.structure(first(outputs)), jax.tree.structure(scratch)]
    cfg = SimpleNamespace(
        trees=trees, heads=heads, all_heads=all_heads, width=width, tokens=tokens, rows=rows,
        buckets=buckets, groups=groups, queries=dp_size, summing=summing, chunks=plan, schedule=SCHEDULE,
    )
    result = pl.pallas_call(
        functools.partial(block_kernel, cfg),
        out_shape=flat(first(outputs)),
        in_specs=flat(second(inputs)),
        out_specs=flat(second(outputs)),
        scratch_shapes=flat(scratch),
        compiler_params=pltpu.CompilerParams(collective_id=0, has_side_effects=True, vmem_limit_bytes=63 << 20),
        name="block",
    )(*flat(first(inputs)))
    got = SimpleNamespace(**jax.tree.unflatten(trees[1], result))
    kept = [got.block_out, got.decoder_grad, got.encoder_grad]
    if summing:
        inputs = dict(grads=got.grads, kept=kept, little=got.small_sum)
        outputs = dict(
            kept=[shape_of(*value.shape) for value in kept],
            gains=[shape_of(width, kind=F32)] * 3,
            position=shape_of(heads, groups, buckets, kind=F32),
            wide=[shape_of(*shape, kind=F32) for shape in grad_shapes[:3]],
            pieces=[shape_of(own, width, kind=F32)] * 8,
        )
        scratch = dict(
            low=[vmem(*shape) for shape in grad_shapes],
            kept=[vmem(*value.shape) for value in kept],
            wide=[vmem(*shape, kind=F32) for shape in grad_shapes],
            sems=pltpu.SemaphoreType.DMA((32,)),
        )
        trees = [jax.tree.structure(inputs), jax.tree.structure(outputs), jax.tree.structure(scratch)]

        def finish(*refs):
            groups_of, at = [], 0
            for tree in trees:
                groups_of.append(SimpleNamespace(**jax.tree.unflatten(tree, refs[at : at + tree.num_leaves])))
                at += tree.num_leaves
            finish_kernel(own, buckets, heads, groups, *groups_of)

        specs_in = dict(grads=[ANY] * 4, kept=[ANY] * 3, little=VMEM)
        specs_out = dict(kept=[ANY] * 3, gains=[VMEM] * 3, position=VMEM, wide=[ANY] * 3, pieces=[ANY] * 8)
        result = pl.pallas_call(
            finish,
            out_shape=flat(outputs),
            in_specs=flat(specs_in),
            out_specs=flat(specs_out),
            scratch_shapes=flat(scratch),
            compiler_params=pltpu.CompilerParams(vmem_limit_bytes=63 << 20),
            name="finish",
        )(*flat(inputs))
        done = SimpleNamespace(**jax.tree.unflatten(trees[1], result))
        kept, gain_grads, position = done.kept, done.gains, jnp.transpose(done.position, (1, 2, 0))
        wide, pieces = done.wide, done.pieces
    else:
        sums, little = lax.psum(([value.astype(F32) for value in got.grads], got.small_sum), "dp")
        wide = sums[:3]
        pieces = [sums[3][k * own : (k + 1) * own] for k in range(8)]
        gain_grads = [little[k] for k in range(3)]
        position = little[8 : 8 + groups, : heads * buckets].reshape(groups, heads, buckets)
        position = jnp.transpose(position, (0, 2, 1))
    down, gate, up = wide
    oc, qc, os, qs, ks, vs, kc, vc = pieces
    return (
        *[value[None] for value in kept], *gain_grads,
        qs.T, ks.T, vs.T, os, qc.T, kc.T, vc.T, oc, gate, up, down, position,
    )


def solution(mesh):
    rows = P("dp", None, None)
    encoder = P("dp", "tensor", None)
    columns, lines, whole = P(None, "tensor"), P("tensor", None), P()
    head_table = P(None, None, "tensor")
    weights = (columns, columns, columns, lines, columns, columns, columns, lines, columns, columns, lines, head_table)
    return jax.shard_map(
        functools.partial(shards, (mesh.shape["dp"], mesh.shape["tensor"])),
        mesh=mesh,
        in_specs=(rows, encoder, rows, P("dp"), P("dp", None), whole, whole, whole, whole) + weights,
        out_specs=(rows, rows, encoder, whole, whole, whole) + weights,
        check_vma=False,
    )
```
